256 devices in a mesh: cells: 64 (over y, z, core), bands: 4 (over x).
Axes of the slice: x: 4, y: 4, z: 8, core: 2. Of those that a mesh axis runs over, the one named last changes fastest.
Arguments:
- psi: bfloat16 [1024, 16, 16, 512], P('cells', None, None, 'bands'), may hold values from -64 to 64
- cell_ham: bfloat16 [512, 729, 729], P('cells'), may hold values from -2 to 2
- proj_table: bfloat16 [4, 8, 16, 729], replicated, may hold values from -0.21875 to 0.21875
- coupling: float32 [4, 16, 16], replicated, may hold values from -0.5 to 0.5
- atom_kind: int32 [128, 2, 2], P('cells'), may hold values from -1 to 3, as said below
Outputs:
- filtered: bfloat16 [1024, 16, 16, 512], P('cells', None, None, 'bands')
- correlation: float32 [512, 512], P('cells', 'bands')
The draws below stay inside these ranges and needn't reach their ends.
Inputs may be any that keep to these rules, and one draw needn't show every extreme that they name: `atom_kind`: -1 marks a vertex without an atom; other values name the species.
All inputs are finite; a program needn't handle non-finite values.
Results may differ from the reference program's by a relative error of at most 0.0066.
Values may be sent and summed in bfloat16 or wider, within the bound.
No kernel may reach another device: no remote copies, remote signals or barrier semaphores. Data moves between devices by JAX's collectives and lax.ppermute only.
A program may use at most 128 MiB of HBM per device.

```python
import math
import jax
import jax.numpy as jnp
from jax import lax

ORDER = 8
NODES_CELL = 729
CPD = 2
BLOCK = 16
NODES_DEV = 4096
BAND_DEV = 128
NPROJ = 16
KINDS = 4
DEGREE = 3
BLOCKS = 64
CELLS = 512
BANDS = 512


def draw_psi(key, part):
    main_key, node_key, band_key, common_key, loading_key = jax.random.split(key, 5)
    rows_total = BLOCKS * BLOCK
    full_shape = (rows_total, BLOCK, BLOCK, BANDS)
    row_shape = (rows_total, BLOCK, BLOCK, 1)
    owner_index = (jnp.arange(rows_total) // BLOCK).astype(jnp.float32)
    position = (owner_index / max(BLOCKS - 1, 1)).reshape(rows_total, 1, 1, 1)
    randomness = jnp.clip(jax.random.normal(main_key, full_shape, jnp.float32), -6.0, 6.0)
    node_scale = jnp.exp(jax.random.uniform(node_key, row_shape, jnp.float32, math.log(0.2), math.log(2.0)))
    rise_factor = 1.0 + 2.0 * position
    strength = 0.8
    band_scale = jnp.exp(jax.random.uniform(band_key, (BANDS,), jnp.float32, math.log(0.3), math.log(3.0)))
    common_rows = jnp.clip(jax.random.normal(common_key, row_shape, jnp.float32), -4.0, 4.0)
    common_bands = jnp.clip(jax.random.normal(loading_key, (BANDS,), jnp.float32), -3.0, 3.0)
    values = node_scale * jnp.sqrt(rise_factor) * band_scale * (randomness + strength * common_rows * common_bands)
    return jnp.clip(values, -64.0, 64.0).astype(jnp.bfloat16)


def draw_cell_ham(key, part):
    node_index = jnp.arange(ORDER + 1)
    edge_factor = ((node_index == 0) | (node_index == ORDER)).astype(jnp.float32) + 1.0
    multiplicity = (edge_factor[:, None, None] * edge_factor[None, :, None] * edge_factor[None, None, :]).reshape(-1)
    inverse_root = 1.0 / jnp.sqrt(multiplicity)
    spread = 0.45 / math.sqrt(NODES_CELL)

    def one_cell(cell_index):
        cell_key = jax.random.fold_in(key, cell_index)
        diagonal_key, coupling_key = jax.random.split(cell_key)
        diagonal = jax.random.uniform(diagonal_key, (NODES_CELL,), jnp.float32, 0.5, 1.5)
        random_part = jnp.clip(jax.random.normal(coupling_key, (NODES_CELL, NODES_CELL), jnp.float32), -5.0, 5.0)
        symmetric = (random_part + random_part.T) * (spread / math.sqrt(2.0))
        matrix = symmetric * inverse_root[:, None] * inverse_root[None, :] + jnp.diag(diagonal / multiplicity)
        return jnp.clip(matrix, -2.0, 2.0).astype(jnp.bfloat16)
    return lax.map(one_cell, jnp.arange(CELLS))


def draw_atom_kind(key, part):
    presence_key, species_key = jax.random.split(key)
    full_shape = (BLOCKS * CPD, CPD, CPD)
    owner_index = jnp.arange(BLOCKS * CPD, dtype=jnp.int32) // CPD
    threshold = 25 + 70 * owner_index // max(BLOCKS - 1, 1)
    dice_rolls = jax.random.randint(presence_key, full_shape, 0, 100)
    species = jax.random.randint(species_key, full_shape, 0, KINDS)
    chosen = jnp.where(dice_rolls < threshold[:, None, None], species, -1)
    chosen = chosen.at[0, 0, 0].set(-1)
    chosen = chosen.at[BLOCKS * CPD - 1, CPD - 1, CPD - 1].set(KINDS - 1)
    return chosen.astype(jnp.int32)


def centred(rng, dims, width, bound, held_as=jnp.bfloat16):
    return jnp.clip(width * jax.random.normal(rng, dims, jnp.float32), -bound, bound).astype(held_as)


def setup_inputs(seed: int = 0) -> dict:
    splits = jax.random.split(jax.random.key(seed), 6)
    return {
        "psi": draw_psi(jax.random.fold_in(splits[5], 71), 0),
        "cell_ham": draw_cell_ham(jax.random.fold_in(splits[5], 71), 0),
        "proj_table": centred(splits[2], (KINDS, 8, NPROJ, NODES_CELL), NODES_CELL ** -0.5, 0.21875),
        "coupling": centred(splits[3], (KINDS, NPROJ, NPROJ), 0.08, 0.5, jnp.float32),
        "atom_kind": draw_atom_kind(jax.random.fold_in(splits[5], 71), 0),
    }


filter_center = 1.0
highest = lax.Precision.HIGHEST


def cube_root(amount):
    result = 1
    while (result + 1) ** 3 <= amount:
        result = result + 1
    return result


def index_triples(extent):
    return [(along_one, along_two, along_three) for along_one in range(extent) for along_two in range(extent) for along_three in range(extent)]


def fetch_upper(blocks, offsets):
    extended = blocks
    for axis_position, offset in zip((1, 2, 3), offsets):
        neighbour = jnp.roll(extended, -offset, axis=0)
        upper_face = lax.slice_in_dim(neighbour, 0, 1, axis=axis_position)
        extended = jnp.concatenate([extended, upper_face], axis=axis_position)
    return extended


def fold_upper(extended, offsets):
    folded = extended
    for axis_position, offset in zip((1, 2, 3), offsets):
        length = folded.shape[axis_position] - 1
        upper_rim = lax.slice_in_dim(folded, length, length + 1, axis=axis_position)
        arrived = jnp.roll(upper_rim, offset, axis=0)
        lower_face = lax.slice_in_dim(folded, 0, 1, axis=axis_position) + arrived
        remainder = lax.slice_in_dim(folded, 1, length, axis=axis_position)
        folded = jnp.concatenate([lower_face, remainder], axis=axis_position)
    return folded


def corner_values(vertices):
    collected = []
    for cell_one, cell_two, cell_three in index_triples(CPD):
        corners = [vertices[:, cell_one + corner_one, cell_two + corner_two, cell_three + corner_three] for corner_one, corner_two, corner_three in index_triples(2)]
        collected.append(jnp.stack(corners, axis=1))
    return jnp.stack(collected, axis=1)


def corner_fold(corner_parts):
    summed = jnp.zeros((corner_parts.shape[0], CPD + 1, CPD + 1, CPD + 1) + corner_parts.shape[3:], jnp.float32)
    for position, (cell_one, cell_two, cell_three) in enumerate(index_triples(CPD)):
        for corner_position, (corner_one, corner_two, corner_three) in enumerate(index_triples(2)):
            summed = summed.at[:, cell_one + corner_one, cell_two + corner_two, cell_three + corner_three].add(corner_parts[:, position, corner_position])
    return summed


def cell_vectors(extended):
    collected = []
    for cell_one, cell_two, cell_three in index_triples(CPD):
        window = extended[:, cell_one * ORDER:cell_one * ORDER + ORDER + 1, cell_two * ORDER:cell_two * ORDER + ORDER + 1, cell_three * ORDER:cell_three * ORDER + ORDER + 1]
        collected.append(window.reshape(window.shape[0], NODES_CELL, window.shape[-1]))
    return jnp.stack(collected, axis=1)


def assemble(cell_terms):
    edge_nodes = CPD * ORDER + 1
    summed = jnp.zeros((cell_terms.shape[0], edge_nodes, edge_nodes, edge_nodes, cell_terms.shape[-1]), jnp.float32)
    for position, (cell_one, cell_two, cell_three) in enumerate(index_triples(CPD)):
        cube_term = cell_terms[:, position].reshape(cell_terms.shape[0], ORDER + 1, ORDER + 1, ORDER + 1, cell_terms.shape[-1])
        summed = summed.at[:, cell_one * ORDER:cell_one * ORDER + ORDER + 1, cell_two * ORDER:cell_two * ORDER + ORDER + 1, cell_three * ORDER:cell_three * ORDER + ORDER + 1].add(cube_term)
    return summed


def reference(psi, cell_ham, proj_table, coupling, atom_kind):
    grid_side = cube_root(BLOCKS)
    offsets = (1, grid_side, grid_side * grid_side)
    band_groups = BANDS // BAND_DEV
    kinds = atom_kind.reshape(BLOCKS, CPD, CPD, CPD)
    kinds_extended = fetch_upper(kinds, offsets)
    species = jnp.arange(KINDS, dtype=jnp.int32)
    corner_hot = (corner_values(kinds_extended)[..., None] == species).astype(jnp.float32)
    projectors = jnp.einsum('dcok,kopn->dcopn', corner_hot, proj_table.astype(jnp.float32), precision=highest)
    owned_hot = (kinds[..., None] == species).astype(jnp.float32)
    couplings = jnp.einsum('dxyzk,kpq->dxyzpq', owned_hot, coupling, precision=highest)
    hams = cell_ham.reshape(BLOCKS, CPD ** 3, NODES_CELL, NODES_CELL)

    def apply_operator(vectors):
        extended = fetch_upper(vectors, offsets)
        cell_values = cell_vectors(extended).astype(jnp.float32)
        local_part = jnp.einsum('dcij,dcjb->dcib', hams.astype(jnp.float32), cell_values, precision=highest)
        coefficient_parts = jnp.einsum('dcopn,dcnb->dcopb', projectors, cell_values, precision=highest)
        coeffs = fold_upper(corner_fold(coefficient_parts), offsets)
        weights = jnp.einsum('dxyzpq,dxyzqb->dxyzpb', couplings, coeffs, precision=highest).astype(jnp.bfloat16)
        corner_weights = corner_values(fetch_upper(weights, offsets)).astype(jnp.float32)
        projector_part = jnp.einsum('dcopn,dcopb->dcnb', projectors, corner_weights, precision=highest)
        return fold_upper(assemble(local_part + projector_part), offsets)

    def filter_block(start_block):
        previous = start_block
        current = (apply_operator(previous) - filter_center * previous.astype(jnp.float32)).astype(jnp.bfloat16)
        for degree in range(1, DEGREE):
            applied = apply_operator(current)
            upcoming = 2.0 * (applied - filter_center * current.astype(jnp.float32)) - previous.astype(jnp.float32)
            previous, current = current, upcoming.astype(jnp.bfloat16)
        return current

    grouped = psi.reshape(BLOCKS, BLOCK, BLOCK, BLOCK, band_groups, BAND_DEV)
    grouped = jnp.moveaxis(grouped, 4, 0)
    results = lax.map(filter_block, grouped)
    filtered = jnp.moveaxis(results, 0, 4).reshape(BLOCKS * BLOCK, BLOCK, BLOCK, BANDS)
    flat_nodes = filtered.reshape(-1, BANDS)
    inverse_count = 1.0 / (BLOCKS * NODES_DEV)
    correlation = jnp.dot(flat_nodes.T, flat_nodes, preferred_element_type=jnp.float32) * inverse_count
    return filtered, correlation
```

```python
import functools

import jax
import jax.numpy as jnp
from jax import lax
from jax.experimental import pallas as pl
from jax.experimental.pallas import tpu as pltpu
from jax.sharding import PartitionSpec as P


F32 = jnp.float32
BF16 = jnp.bfloat16
HIGHEST = lax.Precision.HIGHEST

SIDE = 17
ZPAD = 24
SLAB = SIDE * ZPAD
ROWS = 6944
CHUNK = 496
FACE = 304
PLANE = SIDE * SIDE
CELL = 729
LANES = 128


def shifted(x, axis, by):
    devices = lax.axis_size(axis)
    return lax.ppermute(x, axis, [(i, (i + by) % devices) for i in range(devices)])


def cube_root(amount):
    result = 1
    while (result + 1) ** 3 <= amount:
        result = result + 1
    return result


def cost(flops, nbytes):
    return pl.CostEstimate(flops=int(flops), bytes_accessed=int(nbytes), transcendentals=0)


def shape(dims, dtype):
    return jax.ShapeDtypeStruct(dims, dtype)


VMEM = pl.BlockSpec(memory_space=pltpu.VMEM)
SMEM = pl.BlockSpec(memory_space=pltpu.SMEM)


def cell_base(a, b, c):
    return a * (8 * SLAB) + b * (8 * ZPAD) + c * 8


def line_start(base, x, y):
    return pl.multiple_of(base + (x * SLAB + y * ZPAD), 8)


def tables_kernel(kinds, table, table_t, coupling, rows_out, columns_out, mix_out):
    lane = lax.broadcasted_iota(jnp.int32, (1, LANES), 1) // 16
    lane_wide = lax.broadcasted_iota(jnp.int32, (16, LANES), 1) // 16

    def cell(position, carry):
        a, b, c = position // 4, (position // 2) % 2, position % 2
        lane_kind = jnp.full((1, LANES), -1, jnp.int32)
        for o in range(8):
            i, j, k = o // 4, (o // 2) % 2, o % 2
            kind = kinds[(a + i) * 9 + (b + j) * 3 + c + k]
            found = table[jnp.maximum(kind, 0), o * 16 : (o + 1) * 16, :]
            keep = jnp.where(kind >= 0, 1.0, 0.0).astype(F32)
            rows_out[position, o * 16 : (o + 1) * 16, :] = (found.astype(F32) * keep).astype(BF16)
            lane_kind = jnp.where(lane == o, kind, lane_kind)
        total = jnp.zeros((CELL, LANES), F32)
        for q in range(table_t.shape[0]):
            total = jnp.where(lane_kind == q, table_t[q].astype(F32), total)
        columns_out[position] = total.astype(BF16)
        return carry

    lax.fori_loop(0, 8, cell, 0)
    mix_out[...] = jnp.zeros_like(mix_out)

    def vertex(v, carry):
        kind = kinds[v]
        block = coupling[jnp.maximum(kind, 0)]
        keep = jnp.where(kind >= 0, 1.0, 0.0).astype(F32)
        block = jnp.where(lane_wide == v % 8, block * keep, 0.0)
        mix_out[v // 8, pl.ds(pl.multiple_of((v % 8) * 16, 16), 16), :] = block
        return carry

    lax.fori_loop(0, 27, vertex, 0)


def make_tables(kinds, table, table_t, coupling):
    return pl.pallas_call(
        tables_kernel,
        out_shape=(
            shape((8, 128, CELL), BF16),
            shape((8, CELL, LANES), BF16),
            shape((4, LANES, LANES), F32),
        ),
        in_specs=[SMEM, VMEM, VMEM, VMEM],
        out_specs=(VMEM, VMEM, VMEM),
        cost_estimate=cost(1e7, 6e6),
        name="tables",
    )(kinds, table, table_t, coupling)


def first_rows_kernel(psi, rows_out, wide, narrow):
    wide[...] = psi[...].reshape(4096, LANES).astype(F32)
    rows = wide[pl.ds(0, 256, stride=16), :]
    narrow[...] = jnp.zeros_like(narrow)
    for x in range(16):
        narrow[x * SIDE : x * SIDE + 16, :] = rows[x * 16 : x * 16 + 16]
    rows_out[...] = narrow[...]


def first_rows(psi):
    return pl.pallas_call(
        first_rows_kernel,
        out_shape=shape((FACE, LANES), F32),
        in_specs=[VMEM],
        out_specs=VMEM,
        scratch_shapes=[pltpu.VMEM((4096, LANES), F32), pltpu.VMEM((FACE, LANES), F32)],
        cost_estimate=cost(1e6, 1.2e6),
        name="first_rows",
    )(psi)


def first_y_kernel(psi_y, from_x, out):
    out[0:256, :] = psi_y[...].reshape(256, LANES)
    out[256:272, :] = from_x[0:16, :]


def first_y(psi, from_x):
    return pl.pallas_call(
        first_y_kernel,
        grid=(1,),
        out_shape=shape((272, LANES), BF16),
        in_specs=[
            pl.BlockSpec((16, 1, 16, LANES), lambda i: (0, 0, 0, 0)),
            pl.BlockSpec((256, LANES), lambda i: (0, 0)),
        ],
        out_specs=pl.BlockSpec((272, LANES), lambda i: (0, 0)),
        cost_estimate=cost(1e5, 2e5),
        name="first_y",
    )(psi, from_x)


def first_z_kernel(rows, from_x, from_y, out, wide_x, wide_y, face):
    wide_x[...] = from_x[...].astype(F32)
    wide_y[...] = from_y[...].astype(F32)
    face[...] = rows[...]
    face[16 * SIDE : 16 * SIDE + 16, :] = wide_x[pl.ds(0, 16, stride=16), :]
    face[pl.ds(16, SIDE, stride=SIDE), :] = wide_y[pl.ds(0, SIDE, stride=16), :]
    out[...] = face[...].astype(BF16)


def first_z(rows, from_x, from_y):
    return pl.pallas_call(
        first_z_kernel,
        out_shape=shape((FACE, LANES), BF16),
        in_specs=[VMEM] * 3,
        out_specs=VMEM,
        scratch_shapes=[
            pltpu.VMEM((256, LANES), F32),
            pltpu.VMEM((272, LANES), F32),
            pltpu.VMEM((FACE, LANES), F32),
        ],
        cost_estimate=cost(1e5, 4e5),
        name="first_z",
    )(rows, from_x, from_y)


def cells_and_coefs(field, cell32, rows, cells_out, coefs_out, low_out, high_out):
    coefs_out[...] = jnp.zeros_like(coefs_out)

    def cell(position, carry):
        a, b, c = position // 4, (position // 2) % 2, position % 2
        base = cell_base(a, b, c)
        for x in range(9):
            for y in range(9):
                at = (x * 9 + y) * 9
                cell32[at : at + 9, :] = field[pl.ds(line_start(base, x, y), 9), :]
        values = cell32[0:CELL, :].astype(BF16)
        cells_out[position] = values
        part = jnp.dot(rows[position], values, preferred_element_type=F32)
        for o in range(8):
            i, j, k = o // 4, (o // 2) % 2, o % 2
            vertex = (a + i) * 9 + (b + j) * 3 + c + k
            spot = pl.ds(pl.multiple_of(vertex * 16, 16), 16)
            coefs_out[spot, :] += part[o * 16 : (o + 1) * 16]
        return carry

    lax.fori_loop(0, 8, cell, 0)
    low_out[...] = coefs_out[0:144, :].astype(BF16)
    high_out[...] = coefs_out[288:432, :].astype(BF16)


COEF_SHAPES = (
    shape((ROWS, LANES), BF16),
    shape((8, CELL, LANES), BF16),
    shape((432, LANES), F32),
    shape((144, LANES), BF16),
    shape((144, LANES), BF16),
)


def begin_kernel(psi, from_x, from_y, from_z, rows, field_out, cells_out, coefs_out, low_out, high_out, field, cell32, wide):
    field[...] = jnp.zeros_like(field)

    def slab(x, carry):
        for y in range(16):
            start = pl.multiple_of(x * SLAB + y * ZPAD, 8)
            field[pl.ds(start, 16), :] = psi[x, y].astype(F32)
        return carry

    lax.fori_loop(0, 16, slab, 0)
    for y in range(16):
        at = 16 * SLAB + y * ZPAD
        field[at : at + 16, :] = from_x[y * 16 : y * 16 + 16, :].astype(F32)
    for x in range(SIDE):
        at = x * SLAB + 16 * ZPAD
        field[at : at + 16, :] = from_y[x * 16 : x * 16 + 16, :].astype(F32)
    wide[...] = from_z[...].astype(F32)
    field[pl.ds(16, PLANE, stride=ZPAD), :] = wide[0:PLANE, :]

    def chunk(n, carry):
        spot = pl.ds(pl.multiple_of(n * CHUNK, 16), CHUNK)
        field_out[spot, :] = field[spot, :].astype(BF16)
        return carry

    lax.fori_loop(0, ROWS // CHUNK, chunk, 0)
    cells_and_coefs(field, cell32, rows, cells_out, coefs_out, low_out, high_out)


def begin(psi, from_x, from_y, from_z, rows):
    return pl.pallas_call(
        begin_kernel,
        out_shape=COEF_SHAPES,
        in_specs=[VMEM] * 5,
        out_specs=(VMEM,) * 5,
        scratch_shapes=[
            pltpu.VMEM((ROWS, LANES), F32),
            pltpu.VMEM((736, LANES), F32),
            pltpu.VMEM((FACE, LANES), F32),
        ],
        cost_estimate=cost(2e8, 8e6),
        name="begin",
    )(psi, from_x, from_y, from_z, rows)


def add_coefs_kernel(axis, coefs, from_low, from_high, coefs_out, low_out, high_out):
    coefs_out[...] = coefs[...]
    if axis == 0:
        coefs_out[0:144, :] += from_low[...].astype(F32)
        coefs_out[288:432, :] += from_high[...].astype(F32)
        for x in range(3):
            low_out[x * 48 : x * 48 + 48, :] = coefs_out[x * 144 : x * 144 + 48, :].astype(BF16)
            high_out[x * 48 : x * 48 + 48, :] = coefs_out[x * 144 + 96 : x * 144 + 144, :].astype(BF16)
    else:
        for x in range(3):
            coefs_out[x * 144 : x * 144 + 48, :] += from_low[x * 48 : x * 48 + 48, :].astype(F32)
            coefs_out[x * 144 + 96 : x * 144 + 144, :] += from_high[x * 48 : x * 48 + 48, :].astype(F32)
        for n in range(9):
            low_out[n * 16 : n * 16 + 16, :] = coefs_out[n * 48 : n * 48 + 16, :].astype(BF16)
            high_out[n * 16 : n * 16 + 16, :] = coefs_out[n * 48 + 32 : n * 48 + 48, :].astype(BF16)


def add_coefs(axis, coefs, from_low, from_high):
    return pl.pallas_call(
        functools.partial(add_coefs_kernel, axis),
        out_shape=(shape((432, LANES), F32), shape((144, LANES), BF16), shape((144, LANES), BF16)),
        in_specs=[VMEM] * 3,
        out_specs=(VMEM,) * 3,
        cost_estimate=cost(1e5, 6e5),
        name="add_coefs_" + str(axis),
    )(coefs, from_low, from_high)


def local_kernel(ham, values, out):
    out[0] = jnp.dot(ham[0], values[0], preferred_element_type=F32)


def local_part(ham, values, first, count):
    return pl.pallas_call(
        local_kernel,
        grid=(count,),
        out_shape=shape((count, CELL, LANES), F32),
        in_specs=[
            pl.BlockSpec((1, CELL, CELL), lambda n: (n + first, 0, 0)),
            pl.BlockSpec((1, CELL, LANES), lambda n: (n + first, 0, 0)),
        ],
        out_specs=pl.BlockSpec((1, CELL, LANES), lambda n: (n, 0, 0)),
        cost_estimate=cost(count * 1.4e8, count * 1.6e6),
        name="local_part",
    )(ham, values)


def project_kernel(coefs, from_low, from_high, mix, columns, local, summed, xlow, xhigh, ylow, yhigh, zlow, zhigh, total, weights, cell32, face):
    position = pl.program_id(0)

    @pl.when(position == 0)
    def _():
        total[0:432, :] = coefs[...]
        total[432:512, :] = jnp.zeros((80, LANES), F32)
        for n in range(9):
            total[n * 48 : n * 48 + 16, :] += from_low[n * 16 : n * 16 + 16, :].astype(F32)
            total[n * 48 + 32 : n * 48 + 48, :] += from_high[n * 16 : n * 16 + 16, :].astype(F32)
        for g in range(4):
            spot = slice(g * 128, g * 128 + 128)
            weights[spot, :] = jnp.dot(
                mix[g], total[spot, :], precision=HIGHEST, preferred_element_type=F32
            ).astype(BF16)
        summed[...] = jnp.zeros_like(summed)

    a, b, c = position // 4, (position // 2) % 2, position % 2
    pieces = []
    for o in range(8):
        i, j, k = o // 4, (o // 2) % 2, o % 2
        vertex = (a + i) * 9 + (b + j) * 3 + c + k
        pieces.append(weights[pl.ds(pl.multiple_of(vertex * 16, 16), 16), :])
    corner = jnp.concatenate(pieces, axis=0)
    cell32[0:CELL, :] = local[0] + jnp.dot(columns[0], corner, preferred_element_type=F32)
    base = cell_base(a, b, c)
    for x in range(9):
        for y in range(9):
            at = (x * 9 + y) * 9
            summed[pl.ds(line_start(base, x, y), 9), :] += cell32[at : at + 9, :]

    @pl.when(position == pl.num_programs(0) - 1)
    def _():
        face[...] = jnp.zeros_like(face)
        for source, out in ((0, xlow), (16 * SLAB, xhigh)):
            for y in range(SIDE):
                face[y * SIDE : (y + 1) * SIDE, :] = summed[source + y * ZPAD : source + y * ZPAD + SIDE, :]
            out[...] = face[...].astype(BF16)
        for source, out in ((0, ylow), (16 * ZPAD, yhigh)):
            for x in range(SIDE):
                face[x * SIDE : (x + 1) * SIDE, :] = summed[source + x * SLAB : source + x * SLAB + SIDE, :]
            out[...] = face[...]
        for source, out in ((0, zlow), (16, zhigh)):
            face[0:PLANE, :] = summed[pl.ds(source, PLANE, stride=ZPAD), :]
            out[...] = face[...]


def project(coefs, from_low, from_high, mix, columns, local):
    whole = lambda *dims: pl.BlockSpec(dims, lambda n: (0,) * len(dims))
    face_bf, face_32 = shape((FACE, LANES), BF16), shape((FACE, LANES), F32)
    return pl.pallas_call(
        project_kernel,
        grid=(8,),
        out_shape=(shape((ROWS, LANES), F32), face_bf, face_bf, face_32, face_32, face_32, face_32),
        in_specs=[
            whole(432, LANES),
            whole(144, LANES),
            whole(144, LANES),
            whole(4, LANES, LANES),
            pl.BlockSpec((1, CELL, LANES), lambda n: (n, 0, 0)),
            pl.BlockSpec((1, CELL, LANES), lambda n: (n, 0, 0)),
        ],
        out_specs=(whole(ROWS, LANES),) + (whole(FACE, LANES),) * 6,
        scratch_shapes=[
            pltpu.VMEM((512, LANES), F32),
            pltpu.VMEM((512, LANES), BF16),
            pltpu.VMEM((736, LANES), F32),
            pltpu.VMEM((FACE, LANES), F32),
        ],
        cost_estimate=cost(2e8, 9e6),
        name="project",
    )(coefs, from_low, from_high, mix, columns, local)


def after_x_kernel(both, *refs):
    if both:
        from_low, from_high, ylow, yhigh, zlow, zhigh, ylow_out, yhigh_out, zlow_out, zhigh_out, low, high, face = refs
    else:
        from_low, yhigh, zhigh, yhigh_out, zhigh_out, low, face = refs
    low[...] = from_low[...].astype(F32)
    if both:
        high[...] = from_high[...].astype(F32)
    last = 16 * SIDE
    work = [(yhigh, yhigh_out, zhigh, zhigh_out, last, 16)]
    if both:
        work.append((ylow, ylow_out, zlow, zlow_out, 0, 0))
    for yin, yout, zin, zout, row, column in work:
        face[...] = yin[...]
        face[0:SIDE, :] += low[row : row + SIDE, :]
        if both:
            face[last : last + SIDE, :] += high[row : row + SIDE, :]
        yout[...] = face[...].astype(BF16)
        zout[...] = zin[...]
        zout[0:SIDE, :] += low[pl.ds(column, SIDE, stride=SIDE), :]
        if both:
            zout[last : last + SIDE, :] += high[pl.ds(column, SIDE, stride=SIDE), :]


def after_x(from_low, from_high, faces):
    both = from_high is not None
    face_bf, face_32 = shape((FACE, LANES), BF16), shape((FACE, LANES), F32)
    received = [from_low, from_high] if both else [from_low]
    outs = (face_bf, face_bf, face_32, face_32) if both else (face_bf, face_32)
    return pl.pallas_call(
        functools.partial(after_x_kernel, both),
        out_shape=outs,
        in_specs=[VMEM] * (len(received) + len(faces)),
        out_specs=(VMEM,) * len(outs),
        scratch_shapes=[pltpu.VMEM((FACE, LANES), F32)] * (3 if both else 2),
        cost_estimate=cost(1e5, 1e6),
        name="after_x",
    )(*received, *faces)


def after_y_kernel(both, *refs):
    if both:
        from_low, from_high, zlow, zhigh, zlow_out, zhigh_out, low, high, face = refs
    else:
        from_low, zhigh, zhigh_out, low, face = refs
    low[...] = from_low[...].astype(F32)
    if both:
        high[...] = from_high[...].astype(F32)
    work = [(zhigh, zhigh_out, 16)]
    if both:
        work.append((zlow, zlow_out, 0))
    for zin, zout, column in work:
        face[...] = zin[...]
        face[pl.ds(0, SIDE, stride=SIDE), :] += low[pl.ds(column, SIDE, stride=SIDE), :]
        if both:
            face[pl.ds(16, SIDE, stride=SIDE), :] += high[pl.ds(column, SIDE, stride=SIDE), :]
        zout[...] = face[...].astype(BF16)


def after_y(from_low, from_high, faces):
    both = from_high is not None
    face_bf = shape((FACE, LANES), BF16)
    received = [from_low, from_high] if both else [from_low]
    outs = (face_bf,) * len(faces)
    return pl.pallas_call(
        functools.partial(after_y_kernel, both),
        out_shape=outs,
        in_specs=[VMEM] * (len(received) + len(faces)),
        out_specs=(VMEM,) * len(outs),
        scratch_shapes=[pltpu.VMEM((FACE, LANES), F32)] * (3 if both else 2),
        cost_estimate=cost(1e5, 6e5),
        name="after_y",
    )(*received, *faces)


def add_faces(field, wide, xs, ys, zs):
    for ref, start in zip(xs, (0, 16 * SLAB)):
        wide[...] = ref[...].astype(F32)
        for y in range(SIDE):
            at = start + y * ZPAD
            field[at : at + SIDE, :] += wide[y * SIDE : (y + 1) * SIDE, :]
    for ref, start in zip(ys, (0, 16 * ZPAD)):
        wide[...] = ref[...].astype(F32)
        for x in range(SIDE):
            at = start + x * SLAB
            field[at : at + SIDE, :] += wide[x * SIDE : (x + 1) * SIDE, :]
    for ref, start in zip(zs, (0, 16)):
        wide[...] = ref[...].astype(F32)
        field[pl.ds(start, PLANE, stride=ZPAD), :] += wide[0:PLANE, :]


def advance_kernel(first, *refs):
    if first:
        summed, xl, xh, yl, yh, zl, zh, now, rows = refs[:9]
        before = None
        refs = refs[9:]
    else:
        summed, xl, xh, yl, yh, zl, zh, now, before, rows = refs[:10]
        refs = refs[10:]
    field_out, cells_out, coefs_out, low_out, high_out, field, cell32, wide = refs
    field[...] = summed[...]
    add_faces(field, wide, (xl, xh), (yl, yh), (zl, zh))

    def chunk(n, carry):
        spot = pl.ds(pl.multiple_of(n * CHUNK, 16), CHUNK)
        value = field[spot, :] - now[spot, :].astype(F32)
        if before is not None:
            value = 2.0 * value - before[spot, :].astype(F32)
        rounded = value.astype(BF16)
        field_out[spot, :] = rounded
        field[spot, :] = rounded.astype(F32)
        return carry

    lax.fori_loop(0, ROWS // CHUNK, chunk, 0)
    cells_and_coefs(field, cell32, rows, cells_out, coefs_out, low_out, high_out)


def advance(summed, received, now, before, rows):
    args = [summed, *received, now] + ([] if before is None else [before]) + [rows]
    return pl.pallas_call(
        functools.partial(advance_kernel, before is None),
        out_shape=COEF_SHAPES,
        in_specs=[VMEM] * len(args),
        out_specs=(VMEM,) * 5,
        scratch_shapes=[
            pltpu.VMEM((ROWS, LANES), F32),
            pltpu.VMEM((736, LANES), F32),
            pltpu.VMEM((FACE, LANES), F32),
        ],
        cost_estimate=cost(2e8, 1.2e7),
        name="advance",
    )(*args)


def finish_kernel(summed, xl, yl, zl, now, before, out, field, wide):
    field[...] = summed[...]
    add_faces(field, wide, (xl,), (yl,), (zl,))

    def chunk(n, carry):
        spot = pl.ds(pl.multiple_of(n * CHUNK, 16), CHUNK)
        value = field[spot, :] - now[spot, :].astype(F32)
        field[spot, :] = 2.0 * value - before[spot, :].astype(F32)
        return carry

    lax.fori_loop(0, ROWS // CHUNK, chunk, 0)

    def slab(x, carry):
        for y in range(16):
            start = pl.multiple_of(x * SLAB + y * ZPAD, 8)
            out[x, y] = field[pl.ds(start, 16), :].astype(BF16)
        return carry

    lax.fori_loop(0, 16, slab, 0)


def finish(summed, received, now, before):
    return pl.pallas_call(
        finish_kernel,
        out_shape=shape((16, 16, 16, LANES), BF16),
        in_specs=[VMEM] * 6,
        out_specs=VMEM,
        scratch_shapes=[pltpu.VMEM((ROWS, LANES), F32), pltpu.VMEM((FACE, LANES), F32)],
        cost_estimate=cost(1e7, 8e6),
        name="finish",
    )(summed, *received, now, before)


def gram_kernel(x0, x1, x2, x3, own, m1, m2, m3):
    blocks = [x0[...], x1[...], x2[...], x3[...]]
    for row, left in enumerate(blocks):
        turned = left.T
        for column, out in ((0, own), (3, m1), (2, m2), (1, m3)):
            part = jnp.dot(turned, blocks[column], preferred_element_type=F32)
            out[row * 128 : row * 128 + 128, :] = part.astype(out.dtype)


def gram(blocks):
    return pl.pallas_call(
        gram_kernel,
        out_shape=(shape((512, LANES), F32),) + (shape((512, LANES), BF16),) * 3,
        in_specs=[VMEM] * 4,
        out_specs=(VMEM,) * 4,
        cost_estimate=cost(6e8, 2e6),
        name="gram",
    )(*blocks)


def collect_kernel(band, own, m1, m2, m3, out):
    for row in range(4):
        total = own[row * 128 : row * 128 + 128, :]
        for offset, ref in ((1, m1), (2, m2), (3, m3)):
            source = (row - offset) % 4
            total = total + ref[source * 128 : source * 128 + 128, :].astype(F32)
        place = (band[0] + 4 - row) % 4
        out[pl.ds(place * 16, 16)] = total.reshape(16, 8, LANES).astype(BF16)


def collect(band, own, received):
    return pl.pallas_call(
        collect_kernel,
        out_shape=shape((64, 8, LANES), BF16),
        in_specs=[SMEM] + [VMEM] * 4,
        out_specs=VMEM,
        cost_estimate=cost(1e6, 1e6),
        name="collect",
    )(band, own, *received)


def local(psi, cell_ham, proj_table, coupling, atom_kind):
    devices = lax.axis_size("cells")
    side = cube_root(devices)
    offsets = (1, side, side * side)

    def upward(x, axis):
        return shifted(x, "cells", offsets[axis])

    def downward(x, axis):
        return shifted(x, "cells", -offsets[axis])

    from_x = downward(psi[0].reshape(256, LANES), 0)
    kinds = atom_kind
    for axis in range(3):
        arrived = downward(lax.slice_in_dim(kinds, 0, 1, axis=axis), axis)
        kinds = jnp.concatenate([kinds, arrived], axis=axis)
    table = proj_table.reshape(4, 128, CELL)
    rows, columns, mix = make_tables(
        kinds.reshape(27),
        table,
        jnp.transpose(table, (0, 2, 1)),
        jnp.tile(coupling, (1, 1, 8)),
    )
    z_rows = first_rows(psi)
    from_y = downward(first_y(psi, from_x), 1)
    from_z = downward(first_z(z_rows, from_x, from_y), 2)

    def both_ways(low, high, axis):
        return upward(high, axis), downward(low, axis)

    def apply_operator(values, coefs, low, high, last):
        arrived = both_ways(low, high, 0)
        part = local_part(cell_ham, values, 0, 8)
        coefs, low, high = add_coefs(0, coefs, *arrived)
        coefs, low, high = add_coefs(1, coefs, *both_ways(low, high, 1))
        arrived = both_ways(low, high, 2)
        summed, xlow, xhigh, ylow, yhigh, zlow, zhigh = project(coefs, *arrived, mix, columns, part)
        if last:
            xs = upward(xhigh, 0)
            yhigh, zhigh = after_x(xs, None, (yhigh, zhigh))
            ys = upward(yhigh, 1)
            (zhigh,) = after_y(ys, None, (zhigh,))
            return summed, (xs, ys, upward(zhigh, 2))
        xs = both_ways(xlow, xhigh, 0)
        ylow, yhigh, zlow, zhigh = after_x(*xs, (ylow, yhigh, zlow, zhigh))
        ys = both_ways(ylow, yhigh, 1)
        zhigh, zlow = after_y(*ys, (zlow, zhigh))[::-1]
        return summed, (*xs, *ys, *both_ways(zlow, zhigh, 2))

    y0, values, coefs, low, high = begin(psi, from_x, from_y, from_z, rows)
    summed, received = apply_operator(values, coefs, low, high, False)
    y1, values, coefs, low, high = advance(summed, received, y0, None, rows)
    summed, received = apply_operator(values, coefs, low, high, False)
    y2, values, coefs, low, high = advance(summed, received, y1, y0, rows)
    summed, received = apply_operator(values, coefs, low, high, True)
    filtered = finish(summed, received, y2, y1)

    groups = lax.axis_size("bands")
    band = lax.axis_index("bands")
    quarters = filtered.reshape(groups, -1, LANES)
    blocks = []
    for offset in range(groups):
        block = lax.dynamic_index_in_dim(quarters, (band + offset) % groups, 0, keepdims=False)
        blocks.append(block if offset == 0 else shifted(block, "bands", offset))
    own, *messages = gram(blocks)
    messages = [shifted(message, "bands", n + 1) for n, message in enumerate(messages)]
    terms = collect(band.astype(jnp.int32).reshape(1), own, messages)
    terms = lax.all_to_all(terms, "cells", 0, 0)
    inverse_count = 1.0 / (quarters.shape[0] * quarters.shape[1] * devices)
    correlation = jnp.sum(terms.astype(F32), axis=0) * inverse_count
    return filtered, correlation


def solution(mesh):
    in_specs = (
        P("cells", None, None, "bands"),
        P("cells", None, None),
        P(),
        P(),
        P("cells", None, None),
    )
    out_specs = (P("cells", None, None, "bands"), P("cells", "bands"))
    return jax.shard_map(local, mesh=mesh, in_specs=in_specs, out_specs=out_specs, check_vma=False)
```

```python
import functools

import jax
import jax.numpy as jnp
from jax import lax
from jax.experimental import pallas as pl
from jax.experimental.pallas import tpu as pltpu
from jax.sharding import PartitionSpec as P


F32 = jnp.float32
BF16 = jnp.bfloat16
HIGHEST = lax.Precision.HIGHEST

SIDE = 17
ZPAD = 24
SLAB = SIDE * ZPAD
ROWS = 6944
CHUNK = 496
FACE = 304
PLANE = SIDE * SIDE
CELL = 729
LANES = 128


def shifted(x, axis, by):
    devices = lax.axis_size(axis)
    return lax.ppermute(x, axis, [(i, (i + by) % devices) for i in range(devices)])


def cube_root(amount):
    result = 1
    while (result + 1) ** 3 <= amount:
        result = result + 1
    return result


def cost(flops, nbytes):
    return pl.CostEstimate(flops=int(flops), bytes_accessed=int(nbytes), transcendentals=0)


def shape(dims, dtype):
    return jax.ShapeDtypeStruct(dims, dtype)


VMEM = pl.BlockSpec(memory_space=pltpu.VMEM)
LARGE = pltpu.CompilerParams(vmem_limit_bytes=36 * 2**20)
SMALL = pltpu.CompilerParams(vmem_limit_bytes=12 * 2**20)
SMEM = pl.BlockSpec(memory_space=pltpu.SMEM)


def cell_base(a, b, c):
    return a * (8 * SLAB) + b * (8 * ZPAD) + c * 8


def line_start(base, x, y):
    return pl.multiple_of(base + (x * SLAB + y * ZPAD), 8)


def corner_kinds(kinds, a, b, c, lane):
    found = jnp.full((1, LANES), -1, jnp.int32)
    for o in range(8):
        i, j, k = o // 4, (o // 2) % 2, o % 2
        found = jnp.where(lane == o, kinds[((a + i) * 5 + b + j) * 5 + c + k], found)
    return found


def tables_kernel(kinds, table, table_t, coupling, rows_out, columns_out, mix_out, faces_out, edges_out, points_out, picked):
    species = table_t.shape[0]
    lane = lax.broadcasted_iota(jnp.int32, (1, LANES), 1) // 16
    lane_wide = lax.broadcasted_iota(jnp.int32, (16, LANES), 1) // 16

    def choose(values, lane_kind):
        total = jnp.where(lane_kind == 0, values[0], 0.0)
        for q in range(1, species):
            total = jnp.where(lane_kind == q, values[q], total)
        return total.astype(BF16)

    def cell(position, carry):
        a, b, c = position // 4, (position // 2) % 2, position % 2
        for o in range(8):
            i, j, k = o // 4, (o // 2) % 2, o % 2
            kind = kinds[((a + i + 1) * 5 + b + j + 1) * 5 + c + k + 1]
            found = table[jnp.maximum(kind, 0), o * 16 : (o + 1) * 16, :]
            keep = jnp.where(kind >= 0, 1.0, 0.0).astype(F32)
            rows_out[position, o * 16 : (o + 1) * 16, :] = (found.astype(F32) * keep).astype(BF16)
        lane_kind = corner_kinds(kinds, a + 1, b + 1, c + 1, lane)
        columns_out[position] = choose([table_t[q, 0:CELL] for q in range(species)], lane_kind)
        return carry

    lax.fori_loop(0, 8, cell, 0)
    mix_out[...] = jnp.zeros_like(mix_out)

    def vertex(v, carry):
        kind = kinds[(v // 9 + 1) * 25 + ((v // 3) % 3 + 1) * 5 + v % 3 + 1]
        block = coupling[jnp.maximum(kind, 0)]
        keep = jnp.where(kind >= 0, 1.0, 0.0).astype(F32)
        block = jnp.where(lane_wide == v % 8, block * keep, 0.0)
        mix_out[v // 8, pl.ds(pl.multiple_of((v % 8) * 16, 16), 16), :] = block
        return carry

    lax.fori_loop(0, 27, vertex, 0)
    for axis in range(3):
        for s in range(2):
            near = 8 - 8 * s
            for q in range(species):
                if axis == 0:
                    picked[q, 0:81] = table_t[q, near * 81 : near * 81 + 81]
                elif axis == 1:
                    for x in range(9):
                        picked[q, x * 9 : x * 9 + 9] = table_t[q, x * 81 + near * 9 : x * 81 + near * 9 + 9]
                else:
                    picked[q, 0:81] = table_t[q, pl.ds(near, 81, stride=9)]

            def face(n, carry, axis=axis, s=s):
                spot = [n // 2 + 1, n % 2 + 1]
                spot.insert(axis, 3 * s)
                lane_kind = corner_kinds(kinds, *spot, lane)
                faces_out[axis * 8 + s * 4 + n] = choose([picked[q, 0:81] for q in range(species)], lane_kind)
                return carry

            lax.fori_loop(0, 4, face, 0)
    for axis in range(3):
        for s in range(2):
            for t in range(2):
                first, second = 8 - 8 * s, 8 - 8 * t
                for u in range(2):
                    spot = [3 * s, 3 * t]
                    spot.insert(axis, u + 1)
                    start, stride = ((first * 9 + second, 81), (first * 81 + second, 9), (first * 81 + second * 9, 1))[axis]
                    lane_kind = corner_kinds(kinds, *spot, lane)
                    place = slice(start, start + 9) if stride == 1 else pl.ds(start, 9, stride=stride)
                    edges_out[axis * 8 + s * 4 + t * 2 + u, 0:9] = choose([table_t[q, place] for q in range(species)], lane_kind)
    for n in range(8):
        s, t, w = n // 4, (n // 2) % 2, n % 2
        at = (8 - 8 * s) * 81 + (8 - 8 * t) * 9 + 8 - 8 * w
        lane_kind = corner_kinds(kinds, 3 * s, 3 * t, 3 * w, lane)
        points_out[n, 0:1] = choose([table_t[q, at : at + 1] for q in range(species)], lane_kind)


def make_tables(kinds, table, table_t, coupling):
    species = table.shape[0]
    return pl.pallas_call(
        tables_kernel,
        out_shape=(
            shape((8, 128, CELL), BF16),
            shape((8, CELL, LANES), BF16),
            shape((4, LANES, LANES), F32),
            shape((24, 81, LANES), BF16),
            shape((24, 9, LANES), BF16),
            shape((8, 1, LANES), BF16),
        ),
        in_specs=[SMEM, VMEM, VMEM, VMEM],
        out_specs=(VMEM,) * 6,
        scratch_shapes=[pltpu.VMEM((species, 88, LANES), F32)],
        cost_estimate=cost(1e7, 6e6),
        name="tables",
    )(kinds, table, table_t, coupling)


def first_rows_kernel(psi, rows_out, wide, narrow):
    wide[...] = psi[...].reshape(4096, LANES).astype(F32)
    rows = wide[pl.ds(0, 256, stride=16), :]
    narrow[...] = jnp.zeros_like(narrow)
    for x in range(16):
        narrow[x * SIDE : x * SIDE + 16, :] = rows[x * 16 : x * 16 + 16]
    rows_out[...] = narrow[...]


def first_rows(psi):
    return pl.pallas_call(
        first_rows_kernel,
        out_shape=shape((FACE, LANES), F32),
        in_specs=[VMEM],
        out_specs=VMEM,
        scratch_shapes=[pltpu.VMEM((4096, LANES), F32), pltpu.VMEM((FACE, LANES), F32)],
        cost_estimate=cost(1e6, 1.2e6),
        name="first_rows",
    )(psi)


def first_y_kernel(psi_y, from_x, out):
    out[0:256, :] = psi_y[...].reshape(256, LANES)
    out[256:272, :] = from_x[0:16, :]


def first_y(psi, from_x):
    return pl.pallas_call(
        first_y_kernel,
        grid=(1,),
        out_shape=shape((272, LANES), BF16),
        in_specs=[
            pl.BlockSpec((16, 1, 16, LANES), lambda i: (0, 0, 0, 0)),
            pl.BlockSpec((256, LANES), lambda i: (0, 0)),
        ],
        out_specs=pl.BlockSpec((272, LANES), lambda i: (0, 0)),
        cost_estimate=cost(1e5, 2e5),
        name="first_y",
    )(psi, from_x)


def first_z_kernel(rows, from_x, from_y, out, wide_x, wide_y, face):
    wide_x[...] = from_x[...].astype(F32)
    wide_y[...] = from_y[...].astype(F32)
    face[...] = rows[...]
    face[16 * SIDE : 16 * SIDE + 16, :] = wide_x[pl.ds(0, 16, stride=16), :]
    face[pl.ds(16, SIDE, stride=SIDE), :] = wide_y[pl.ds(0, SIDE, stride=16), :]
    out[...] = face[...].astype(BF16)


def first_z(rows, from_x, from_y):
    return pl.pallas_call(
        first_z_kernel,
        out_shape=shape((FACE, LANES), BF16),
        in_specs=[VMEM] * 3,
        out_specs=VMEM,
        scratch_shapes=[
            pltpu.VMEM((256, LANES), F32),
            pltpu.VMEM((272, LANES), F32),
            pltpu.VMEM((FACE, LANES), F32),
        ],
        cost_estimate=cost(1e5, 4e5),
        name="first_z",
    )(rows, from_x, from_y)


def begin_kernel(psi, from_x, from_y, from_z, field_out, field, wide):
    field[...] = jnp.zeros_like(field)

    def slab(x, carry):
        for y in range(16):
            start = pl.multiple_of(x * SLAB + y * ZPAD, 8)
            field[pl.ds(start, 16), :] = psi[x, y].astype(F32)
        return carry

    lax.fori_loop(0, 16, slab, 0)
    for y in range(16):
        at = 16 * SLAB + y * ZPAD
        field[at : at + 16, :] = from_x[y * 16 : y * 16 + 16, :].astype(F32)
    for x in range(SIDE):
        at = x * SLAB + 16 * ZPAD
        field[at : at + 16, :] = from_y[x * 16 : x * 16 + 16, :].astype(F32)
    wide[...] = from_z[...].astype(F32)
    field[pl.ds(16, PLANE, stride=ZPAD), :] = wide[0:PLANE, :]

    def chunk(n, carry):
        spot = pl.ds(pl.multiple_of(n * CHUNK, 16), CHUNK)
        field_out[spot, :] = field[spot, :].astype(BF16)
        return carry

    lax.fori_loop(0, ROWS // CHUNK, chunk, 0)


def begin(psi, from_x, from_y, from_z):
    return pl.pallas_call(
        begin_kernel,
        out_shape=shape((ROWS, LANES), BF16),
        in_specs=[VMEM] * 4,
        out_specs=VMEM,
        scratch_shapes=[pltpu.VMEM((ROWS, LANES), F32), pltpu.VMEM((FACE, LANES), F32)],
        cost_estimate=cost(1e7, 4e6),
        compiler_params=LARGE,
        name="begin",
    )(psi, from_x, from_y, from_z)


MESSAGE_Y = FACE + 288
MESSAGE_Z = FACE + 480
MESSAGE_X = FACE + 800


def send(odd, low, high, first, second, rows):
    first[rows, :] = jnp.where(odd, low, high).astype(BF16)
    second[rows, :] = jnp.where(odd, high, low).astype(BF16)


def receive(odd, first, second, rows):
    one, two = first[rows, :].astype(F32), second[rows, :].astype(F32)
    return jnp.where(odd, one, two), jnp.where(odd, two, one)


def apply_kernel(odd, now, ham, rows, mix, summed, send_one, send_two, zlow, zhigh, xlow, xhigh, weights, field, cell32, total, low, high):
    position = pl.program_id(0)

    @pl.when(position == 0)
    def _():
        def chunk(n, carry):
            spot = pl.ds(pl.multiple_of(n * CHUNK, 16), CHUNK)
            field[spot, :] = now[spot, :].astype(F32)
            summed[spot, :] = jnp.zeros((CHUNK, LANES), F32)
            return carry

        lax.fori_loop(0, ROWS // CHUNK, chunk, 0)
        total[...] = jnp.zeros_like(total)

    a, b, c = position // 4, (position // 2) % 2, position % 2
    base = cell_base(a, b, c)
    for x in range(9):
        for y in range(9):
            at = (x * 9 + y) * 9
            cell32[at : at + 9, :] = field[pl.ds(line_start(base, x, y), 9), :]
    values = cell32[0:CELL, :].astype(BF16)
    part = jnp.dot(rows[0], values, preferred_element_type=F32)
    for o in range(8):
        i, j, k = o // 4, (o // 2) % 2, o % 2
        vertex = (a + i) * 9 + (b + j) * 3 + c + k
        total[pl.ds(pl.multiple_of(vertex * 16, 16), 16), :] += part[o * 16 : (o + 1) * 16]
    cell32[0:CELL, :] = jnp.dot(ham[0], values, preferred_element_type=F32)
    for x in range(9):
        for y in range(9):
            at = (x * 9 + y) * 9
            summed[pl.ds(line_start(base, x, y), 9), :] += cell32[at : at + 9, :]

    @pl.when(position == pl.num_programs(0) - 1)
    def _():
        turn = odd[1] == 1
        for g in range(4):
            spot = slice(g * 128, g * 128 + 128)
            total[spot, :] = jnp.dot(mix[g], total[spot, :], precision=HIGHEST, preferred_element_type=F32)
        weights[...] = total[0:432, :]
        for source, out in ((0, low), (16 * ZPAD, high)):
            for x in range(SIDE):
                out[x * SIDE : (x + 1) * SIDE, :] = summed[source + x * SLAB : source + x * SLAB + SIDE, :]
            out[PLANE:FACE, :] = jnp.zeros((FACE - PLANE, LANES), F32)
        send(turn, low[...], high[...], send_one, send_two, slice(0, FACE))
        for p in range(2):
            for x in range(3):
                at = FACE + (p * 3 + x) * 48
                down = total[x * 144 + p * 48 : x * 144 + p * 48 + 48, :]
                up = total[x * 144 + (p + 1) * 48 : x * 144 + (p + 1) * 48 + 48, :]
                send(turn, down, up, send_one, send_two, slice(at, at + 48))
        for source, out in ((0, zlow), (16, zhigh)):
            out[0:PLANE, :] = summed[pl.ds(source, PLANE, stride=ZPAD), :]
            out[PLANE:FACE, :] = jnp.zeros((FACE - PLANE, LANES), F32)
        for source, out in ((0, xlow), (16 * SLAB, xhigh)):
            for y in range(SIDE):
                out[y * SIDE : (y + 1) * SIDE, :] = summed[source + y * ZPAD : source + y * ZPAD + SIDE, :]
            out[PLANE:FACE, :] = jnp.zeros((FACE - PLANE, LANES), F32)


def apply_cells(odd, now, ham, rows, mix):
    whole = lambda *dims: pl.BlockSpec(dims, lambda n: (0,) * len(dims))
    face_32 = shape((FACE, LANES), F32)
    message = shape((MESSAGE_Y, LANES), BF16)
    return pl.pallas_call(
        apply_kernel,
        grid=(8,),
        out_shape=(shape((ROWS, LANES), F32), message, message) + (face_32,) * 4 + (shape((432, LANES), F32),),
        in_specs=[
            SMEM,
            whole(ROWS, LANES),
            pl.BlockSpec((1, CELL, CELL), lambda n: (n, 0, 0)),
            pl.BlockSpec((1, 128, CELL), lambda n: (n, 0, 0)),
            whole(4, LANES, LANES),
        ],
        out_specs=(whole(ROWS, LANES), whole(MESSAGE_Y, LANES), whole(MESSAGE_Y, LANES))
        + (whole(FACE, LANES),) * 4
        + (whole(432, LANES),),
        scratch_shapes=[
            pltpu.VMEM((ROWS, LANES), F32),
            pltpu.VMEM((736, LANES), F32),
            pltpu.VMEM((512, LANES), F32),
            pltpu.VMEM((FACE, LANES), F32),
            pltpu.VMEM((FACE, LANES), F32),
        ],
        cost_estimate=cost(1.3e9, 1.6e7),
        compiler_params=LARGE,
        name="apply_cells",
    )(odd, now, ham, rows, mix)


def after_y_kernel(odd, one, two, zlow, zhigh, xlow, xhigh, weights, send_one, send_two, xlow_out, xhigh_out, weights_out, low, high, face_low, face_high):
    low[...], high[...] = receive(odd[1] == 1, one, two, slice(0, FACE))
    turn = odd[2] == 1
    last = 16 * SIDE
    for face, source, column in ((face_low, zlow, 0), (face_high, zhigh, 16)):
        face[...] = source[...]
        face[pl.ds(0, SIDE, stride=SIDE), :] += low[pl.ds(column, SIDE, stride=SIDE), :]
        face[pl.ds(16, SIDE, stride=SIDE), :] += high[pl.ds(column, SIDE, stride=SIDE), :]
    send(turn, face_low[...], face_high[...], send_one, send_two, slice(0, FACE))
    for out, source, row in ((xlow_out, xlow, 0), (xhigh_out, xhigh, last)):
        out[...] = source[...]
        out[0:SIDE, :] += low[row : row + SIDE, :]
        out[last : last + SIDE, :] += high[row : row + SIDE, :]
    for x in range(3):
        weights_out[x * 240 + 48 : x * 240 + 192, :] = weights[x * 144 : x * 144 + 144, :]
        for p in range(2):
            at = FACE + (p * 3 + x) * 48
            below, above = receive(odd[1] == 1, one, two, slice(at, at + 48))
            if p == 0:
                weights_out[x * 240 : x * 240 + 48, :] = below
                weights_out[x * 240 + 144 : x * 240 + 192, :] += above
            else:
                weights_out[x * 240 + 48 : x * 240 + 96, :] += below
                weights_out[x * 240 + 192 : x * 240 + 240, :] = above
    for p in range(2):
        for n in range(15):
            at = FACE + (p * 15 + n) * 16
            down = weights_out[n * 48 + p * 16 : n * 48 + p * 16 + 16, :]
            up = weights_out[n * 48 + p * 16 + 16 : n * 48 + p * 16 + 32, :]
            send(turn, down, up, send_one, send_two, slice(at, at + 16))


def after_y(odd, one, two, zlow, zhigh, xlow, xhigh, weights):
    face_32 = shape((FACE, LANES), F32)
    message = shape((MESSAGE_Z, LANES), BF16)
    return pl.pallas_call(
        after_y_kernel,
        out_shape=(message, message, face_32, face_32, shape((720, LANES), F32)),
        in_specs=[SMEM] + [VMEM] * 7,
        out_specs=(VMEM,) * 5,
        scratch_shapes=[pltpu.VMEM((FACE, LANES), F32)] * 4,
        cost_estimate=cost(1e5, 2e6),
        compiler_params=SMALL,
        name="after_y",
    )(odd, one, two, zlow, zhigh, xlow, xhigh, weights)


def after_z_kernel(odd, one, two, xlow, xhigh, weights, send_one, send_two, weights_out, low, high, face_low, face_high):
    low[...], high[...] = receive(odd[2] == 1, one, two, slice(0, FACE))
    turn = odd[0] == 1
    for face, source, row in ((face_low, xlow, 0), (face_high, xhigh, 16 * SIDE)):
        face[...] = source[...]
        face[pl.ds(0, SIDE, stride=SIDE), :] += low[row : row + SIDE, :]
        face[pl.ds(16, SIDE, stride=SIDE), :] += high[row : row + SIDE, :]
    send(turn, face_low[...], face_high[...], send_one, send_two, slice(0, FACE))
    for n in range(15):
        weights_out[n * 80 + 16 : n * 80 + 64, :] = weights[n * 48 : n * 48 + 48, :]
        for p in range(2):
            at = FACE + (p * 15 + n) * 16
            below, above = receive(odd[2] == 1, one, two, slice(at, at + 16))
            if p == 0:
                weights_out[n * 80 : n * 80 + 16, :] = below
                weights_out[n * 80 + 48 : n * 80 + 64, :] += above
            else:
                weights_out[n * 80 + 16 : n * 80 + 32, :] += below
                weights_out[n * 80 + 64 : n * 80 + 80, :] = above
    for p in range(2):
        at = FACE + p * 400
        down, up = weights_out[p * 400 : p * 400 + 400, :], weights_out[p * 400 + 400 : p * 400 + 800, :]
        send(turn, down, up, send_one, send_two, slice(at, at + 400))


def after_z(odd, one, two, xlow, xhigh, weights):
    message = shape((MESSAGE_X, LANES), BF16)
    return pl.pallas_call(
        after_z_kernel,
        out_shape=(message, message, shape((1200, LANES), F32)),
        in_specs=[SMEM] + [VMEM] * 5,
        out_specs=(VMEM,) * 3,
        scratch_shapes=[pltpu.VMEM((FACE, LANES), F32)] * 4,
        cost_estimate=cost(1e5, 2e6),
        compiler_params=SMALL,
        name="after_z",
    )(odd, one, two, xlow, xhigh, weights)


def corner_weights(weights, a, b, c):
    pieces = []
    for o in range(8):
        i, j, k = o // 4, (o // 2) % 2, o % 2
        vertex = ((a + i) * 5 + b + j) * 5 + c + k
        pieces.append(weights[pl.ds(pl.multiple_of(vertex * 16, 16), 16), :])
    return jnp.concatenate(pieces, axis=0)


def advance_kernel(first, last, *refs):
    odd, summed, y1, y2, z1, z2, x1, x2, w75, columns, faces, edges, points, now = refs[:14]
    refs = refs[14:]
    before = None
    if not first:
        before = refs[0]
        refs = refs[1:]
    out, field, cell32, weights, xs, ys, zs = refs
    for ref, one, two, axis in ((xs, x1, x2, 0), (ys, y1, y2, 1), (zs, z1, z2, 2)):
        low, high = receive(odd[axis] == 1, one, two, slice(0, FACE))
        ref[0:FACE, :] = low
        ref[FACE : 2 * FACE, :] = high
    for p in range(2):
        at = FACE + p * 400
        below, above = receive(odd[0] == 1, x1, x2, slice(at, at + 400))
        if p == 0:
            weights[0:400, :] = below.astype(BF16)
            weights[1200:1600, :] = (w75[800:1200, :] + above).astype(BF16)
        else:
            weights[400:800, :] = (w75[0:400, :] + below).astype(BF16)
            weights[1600:2000, :] = above.astype(BF16)
    weights[800:1200, :] = w75[400:800, :].astype(BF16)

    def copy(n, carry):
        spot = pl.ds(pl.multiple_of(n * CHUNK, 16), CHUNK)
        field[spot, :] = summed[spot, :]
        return carry

    lax.fori_loop(0, ROWS // CHUNK, copy, 0)

    def cell(position, carry):
        a, b, c = position // 4, (position // 2) % 2, position % 2
        corner = corner_weights(weights, a + 1, b + 1, c + 1)
        cell32[0:CELL, :] = jnp.dot(columns[position], corner, preferred_element_type=F32)
        base = cell_base(a, b, c)
        for x in range(9):
            for y in range(9):
                at = (x * 9 + y) * 9
                field[pl.ds(line_start(base, x, y), 9), :] += cell32[at : at + 9, :]
        return carry

    lax.fori_loop(0, 8, cell, 0)

    for axis, ref in enumerate((xs, ys, zs)):

        def face(n, carry, axis=axis, ref=ref):
            s, u, v = n // 4, (n // 2) % 2, n % 2
            spot = [u + 1, v + 1]
            spot.insert(axis, 3 * s)
            cell32[0:81, :] = jnp.dot(
                faces[axis * 8 + n], corner_weights(weights, *spot), preferred_element_type=F32
            )
            view = ref.at[pl.ds(pl.multiple_of(s * FACE + u * 136 + v * 8, 8), 152)]
            for row in range(9):
                view[row * SIDE : row * SIDE + 9, :] += cell32[row * 9 : row * 9 + 9, :]
            return carry

        lax.fori_loop(0, 8, face, 0)

    for axis in range(3):

        def edge(n, carry, axis=axis):
            s, t, u = n // 4, (n // 2) % 2, n % 2
            spot = [3 * s, 3 * t]
            spot.insert(axis, u + 1)
            term = jnp.dot(edges[axis * 8 + n], corner_weights(weights, *spot), preferred_element_type=F32)
            if axis == 2:
                view = xs.at[pl.ds(pl.multiple_of(s * FACE + t * 272 + u * 8, 8), 16)]
                view[0:9, :] += term
            else:
                ref = xs if axis == 1 else ys
                view = ref.at[pl.ds(pl.multiple_of(s * FACE + u * 136 + t * 16, 8), 152)]
                view[pl.ds(0, 9, stride=SIDE), :] += term
            return carry

        lax.fori_loop(0, 8, edge, 0)

    def point(n, carry):
        s, t, w = n // 4, (n // 2) % 2, n % 2
        term = jnp.dot(points[n], corner_weights(weights, 3 * s, 3 * t, 3 * w), preferred_element_type=F32)
        view = xs.at[pl.ds(pl.multiple_of(s * FACE + t * 272 + w * 16, 8), 8)]
        view[0:1, :] += term
        return carry

    lax.fori_loop(0, 8, point, 0)

    for s in range(2):
        for y in range(SIDE):
            at = s * 16 * SLAB + y * ZPAD
            field[at : at + SIDE, :] += xs[s * FACE + y * SIDE : s * FACE + (y + 1) * SIDE, :]
        for x in range(SIDE):
            at = s * 16 * ZPAD + x * SLAB
            field[at : at + SIDE, :] += ys[s * FACE + x * SIDE : s * FACE + (x + 1) * SIDE, :]
        field[pl.ds(s * 16, PLANE, stride=ZPAD), :] += zs[s * FACE : s * FACE + PLANE, :]

    def chunk(n, carry):
        spot = pl.ds(pl.multiple_of(n * CHUNK, 16), CHUNK)
        value = field[spot, :] - now[spot, :].astype(F32)
        if before is not None:
            value = 2.0 * value - before[spot, :].astype(F32)
        if last:
            field[spot, :] = value
        else:
            out[spot, :] = value.astype(BF16)
        return carry

    lax.fori_loop(0, ROWS // CHUNK, chunk, 0)
    if last:

        def slab(x, carry):
            for y in range(16):
                start = pl.multiple_of(x * SLAB + y * ZPAD, 8)
                out[x, y] = field[pl.ds(start, 16), :].astype(BF16)
            return carry

        lax.fori_loop(0, 16, slab, 0)


def advance(odd, summed, messages, w75, tables, now, before, last):
    args = [odd, summed, *messages, w75, *tables, now] + ([] if before is None else [before])
    return pl.pallas_call(
        functools.partial(advance_kernel, before is None, last),
        out_shape=shape((16, 16, 16, LANES) if last else (ROWS, LANES), BF16),
        in_specs=[SMEM] + [VMEM] * (len(args) - 1),
        out_specs=VMEM,
        scratch_shapes=[
            pltpu.VMEM((ROWS, LANES), F32),
            pltpu.VMEM((736, LANES), F32),
            pltpu.VMEM((2000, LANES), BF16),
        ]
        + [pltpu.VMEM((2 * FACE, LANES), F32)] * 3,
        cost_estimate=cost(3e8, 1.2e7),
        compiler_params=LARGE,
        name="advance",
    )(*args)


def gram_kernel(x0, x1, x2, x3, own, m1, m2, m3):
    blocks = [x0[...], x1[...], x2[...], x3[...]]
    for row, left in enumerate(blocks):
        turned = left.T
        for column, out in ((0, own), (3, m1), (2, m2), (1, m3)):
            part = jnp.dot(turned, blocks[column], preferred_element_type=F32)
            out[row * 128 : row * 128 + 128, :] = part.astype(out.dtype)


def gram(blocks):
    return pl.pallas_call(
        gram_kernel,
        out_shape=(shape((512, LANES), F32),) + (shape((512, LANES), BF16),) * 3,
        in_specs=[VMEM] * 4,
        out_specs=(VMEM,) * 4,
        cost_estimate=cost(6e8, 2e6),
        name="gram",
    )(*blocks)


def collect_kernel(band, own, m1, m2, m3, out):
    for row in range(4):
        total = own[row * 128 : row * 128 + 128, :]
        for offset, ref in ((1, m1), (2, m2), (3, m3)):
            source = (row - offset) % 4
            total = total + ref[source * 128 : source * 128 + 128, :].astype(F32)
        place = (band[0] + 4 - row) % 4
        out[pl.ds(place * 16, 16)] = total.reshape(16, 8, LANES).astype(BF16)


def collect(band, own, received):
    return pl.pallas_call(
        collect_kernel,
        out_shape=shape((64, 8, LANES), BF16),
        in_specs=[SMEM] + [VMEM] * 4,
        out_specs=VMEM,
        cost_estimate=cost(1e6, 1e6),
        name="collect",
    )(band, own, *received)


def local(psi, cell_ham, proj_table, coupling, atom_kind):
    devices = lax.axis_size("cells")
    side = cube_root(devices)
    offsets = (1, side, side * side)
    block = lax.axis_index("cells")
    odd = jnp.stack([(block // offset) % 2 for offset in offsets]).astype(jnp.int32)

    def upward(x, axis):
        return shifted(x, "cells", offsets[axis])

    def downward(x, axis):
        return shifted(x, "cells", -offsets[axis])

    def swap(messages, axis):
        offset = offsets[axis]
        arrived = []
        for start, message in enumerate(messages):
            pairs = []
            for i in range(devices):
                forward = (i // offset) % 2 == start
                pairs.append((i, (i + offset) % devices if forward else (i - offset) % devices))
            arrived.append(lax.ppermute(message, "cells", pairs))
        return arrived

    from_x = downward(psi[0].reshape(256, LANES), 0)
    kinds = atom_kind
    for axis in range(3):
        below = upward(lax.slice_in_dim(kinds, 1, 2, axis=axis), axis)
        above = downward(kinds, axis)
        kinds = jnp.concatenate([below, kinds, above], axis=axis)
    table = proj_table.reshape(4, 128, CELL)
    rows, columns, mix, *ring = make_tables(
        kinds.reshape(125),
        table,
        jnp.transpose(table, (0, 2, 1)).astype(F32),
        jnp.tile(coupling, (1, 1, 8)),
    )
    z_rows = first_rows(psi)
    from_y = downward(first_y(psi, from_x), 1)
    from_z = downward(first_z(z_rows, from_x, from_y), 2)

    def step(now, before, last):
        summed, one, two, zlow, zhigh, xlow, xhigh, weights = apply_cells(odd, now, cell_ham, rows, mix)
        ys = swap((one, two), 1)
        one, two, xlow, xhigh, weights = after_y(odd, *ys, zlow, zhigh, xlow, xhigh, weights)
        zs = swap((one, two), 2)
        one, two, weights = after_z(odd, *zs, xlow, xhigh, weights)
        xs = swap((one, two), 0)
        return advance(odd, summed, (*ys, *zs, *xs), weights, (columns, *ring), now, before, last)

    y0 = begin(psi, from_x, from_y, from_z)
    y1 = step(y0, None, False)
    y2 = step(y1, y0, False)
    filtered = step(y2, y1, True)

    groups = lax.axis_size("bands")
    band = lax.axis_index("bands")
    quarters = filtered.reshape(groups, -1, LANES)
    blocks = []
    for offset in range(groups):
        block = lax.dynamic_index_in_dim(quarters, (band + offset) % groups, 0, keepdims=False)
        blocks.append(block if offset == 0 else shifted(block, "bands", offset))
    own, *messages = gram(blocks)
    messages = [shifted(message, "bands", n + 1) for n, message in enumerate(messages)]
    terms = collect(band.astype(jnp.int32).reshape(1), own, messages)
    terms = lax.all_to_all(terms, "cells", 0, 0)
    inverse_count = 1.0 / (quarters.shape[0] * quarters.shape[1] * devices)
    correlation = jnp.sum(terms.astype(F32), axis=0) * inverse_count
    return filtered, correlation


def solution(mesh):
    in_specs = (
        P("cells", None, None, "bands"),
        P("cells", None, None),
        P(),
        P(),
        P("cells", None, None),
    )
    out_specs = (P("cells", None, None, "bands"), P("cells", "bands"))
    return jax.shard_map(local, mesh=mesh, in_specs=in_specs, out_specs=out_specs, check_vma=False)
```

```python
import functools

import jax
import jax.numpy as jnp
from jax import lax
from jax.experimental import pallas as pl
from jax.experimental.pallas import tpu as pltpu
from jax.sharding import PartitionSpec as P


F32 = jnp.float32
BF16 = jnp.bfloat16
HIGHEST = lax.Precision.HIGHEST

SIDE = 17
ZPAD = 24
SLAB = SIDE * ZPAD
ROWS = 6944
CHUNK = 496
FACE = 304
PLANE = SIDE * SIDE
CELL = 729
LANES = 128


def shifted(x, axis, by):
    devices = lax.axis_size(axis)
    return lax.ppermute(x, axis, [(i, (i + by) % devices) for i in range(devices)])


def cube_root(amount):
    result = 1
    while (result + 1) ** 3 <= amount:
        result = result + 1
    return result


def cost(flops, nbytes):
    return pl.CostEstimate(flops=int(flops), bytes_accessed=int(nbytes), transcendentals=0)


def shape(dims, dtype):
    return jax.ShapeDtypeStruct(dims, dtype)


VMEM = pl.BlockSpec(memory_space=pltpu.VMEM)
LARGE = pltpu.CompilerParams(vmem_limit_bytes=20 * 2**20)
SMALL = pltpu.CompilerParams(vmem_limit_bytes=12 * 2**20)
SMEM = pl.BlockSpec(memory_space=pltpu.SMEM)


def cell_base(a, b, c):
    return a * (8 * SLAB) + b * (8 * ZPAD) + c * 8


def line_start(base, x, y):
    return pl.multiple_of(base + (x * SLAB + y * ZPAD), 8)


def corner_kinds(kinds, a, b, c, lane):
    found = jnp.full((1, LANES), -1, jnp.int32)
    for o in range(8):
        i, j, k = o // 4, (o // 2) % 2, o % 2
        found = jnp.where(lane == o, kinds[((a + i) * 5 + b + j) * 5 + c + k], found)
    return found


def first_tables_kernel(kinds, table, coupling, rows_out, mix_out):
    lane_wide = lax.broadcasted_iota(jnp.int32, (16, LANES), 1) // 16

    def cell(position, carry):
        a, b, c = position // 4, (position // 2) % 2, position % 2
        for o in range(8):
            i, j, k = o // 4, (o // 2) % 2, o % 2
            kind = kinds[((a + i + 1) * 5 + b + j + 1) * 5 + c + k + 1]
            found = table[jnp.maximum(kind, 0), o * 16 : (o + 1) * 16, :]
            keep = jnp.where(kind >= 0, 1.0, 0.0).astype(F32)
            rows_out[position, o * 16 : (o + 1) * 16, :] = (found.astype(F32) * keep).astype(BF16)
        return carry

    lax.fori_loop(0, 8, cell, 0)
    mix_out[...] = jnp.zeros_like(mix_out)

    def vertex(v, carry):
        kind = kinds[(v // 9 + 1) * 25 + ((v // 3) % 3 + 1) * 5 + v % 3 + 1]
        block = coupling[jnp.maximum(kind, 0)]
        keep = jnp.where(kind >= 0, 1.0, 0.0).astype(F32)
        block = jnp.where(lane_wide == v % 8, block * keep, 0.0)
        mix_out[v // 8, pl.ds(pl.multiple_of((v % 8) * 16, 16), 16), :] = block
        return carry

    lax.fori_loop(0, 27, vertex, 0)


def first_tables(kinds, table, coupling):
    return pl.pallas_call(
        first_tables_kernel,
        out_shape=(shape((8, 128, CELL), BF16), shape((4, LANES, LANES), F32)),
        in_specs=[SMEM, VMEM, VMEM],
        out_specs=(VMEM,) * 2,
        cost_estimate=cost(1e6, 3e6),
        compiler_params=SMALL,
        name="first_tables",
    )(kinds, table, coupling)


def tables_kernel(kinds, table_t, after, columns_out, faces_out, edges_out, points_out, picked):
    del after
    species = table_t.shape[0]
    lane = lax.broadcasted_iota(jnp.int32, (1, LANES), 1) // 16

    def choose(values, lane_kind):
        total = jnp.where(lane_kind == 0, values[0], 0.0)
        for q in range(1, species):
            total = jnp.where(lane_kind == q, values[q], total)
        return total.astype(BF16)

    def cell(position, carry):
        a, b, c = position // 4, (position // 2) % 2, position % 2
        lane_kind = corner_kinds(kinds, a + 1, b + 1, c + 1, lane)
        columns_out[position] = choose([table_t[q, 0:CELL] for q in range(species)], lane_kind)
        return carry

    lax.fori_loop(0, 8, cell, 0)
    for axis in range(3):
        for s in range(2):
            near = 8 - 8 * s
            for q in range(species):
                if axis == 0:
                    picked[q, 0:81] = table_t[q, near * 81 : near * 81 + 81]
                elif axis == 1:
                    for x in range(9):
                        picked[q, x * 9 : x * 9 + 9] = table_t[q, x * 81 + near * 9 : x * 81 + near * 9 + 9]
                else:
                    picked[q, 0:81] = table_t[q, pl.ds(near, 81, stride=9)]

            def face(n, carry, axis=axis, s=s):
                spot = [n // 2 + 1, n % 2 + 1]
                spot.insert(axis, 3 * s)
                lane_kind = corner_kinds(kinds, *spot, lane)
                faces_out[axis * 8 + s * 4 + n] = choose([picked[q, 0:81] for q in range(species)], lane_kind)
                return carry

            lax.fori_loop(0, 4, face, 0)
    for axis in range(3):
        for s in range(2):
            for t in range(2):
                first, second = 8 - 8 * s, 8 - 8 * t
                for u in range(2):
                    spot = [3 * s, 3 * t]
                    spot.insert(axis, u + 1)
                    start, stride = ((first * 9 + second, 81), (first * 81 + second, 9), (first * 81 + second * 9, 1))[axis]
                    lane_kind = corner_kinds(kinds, *spot, lane)
                    place = slice(start, start + 9) if stride == 1 else pl.ds(start, 9, stride=stride)
                    edges_out[axis * 8 + s * 4 + t * 2 + u, 0:9] = choose([table_t[q, place] for q in range(species)], lane_kind)
    for n in range(8):
        s, t, w = n // 4, (n // 2) % 2, n % 2
        at = (8 - 8 * s) * 81 + (8 - 8 * t) * 9 + 8 - 8 * w
        lane_kind = corner_kinds(kinds, 3 * s, 3 * t, 3 * w, lane)
        points_out[n, 0:1] = choose([table_t[q, at : at + 1] for q in range(species)], lane_kind)


def make_tables(kinds, table_t, after):
    species = table_t.shape[0]
    return pl.pallas_call(
        tables_kernel,
        out_shape=(
            shape((8, CELL, LANES), BF16),
            shape((24, 81, LANES), BF16),
            shape((24, 9, LANES), BF16),
            shape((8, 1, LANES), BF16),
        ),
        in_specs=[SMEM, VMEM, pl.BlockSpec(memory_space=pl.ANY)],
        out_specs=(VMEM,) * 4,
        scratch_shapes=[pltpu.VMEM((species, 88, LANES), F32)],
        cost_estimate=cost(1e7, 6e6),
        compiler_params=SMALL,
        name="tables",
    )(kinds, table_t, after)


def first_rows_kernel(psi, rows_out, wide, narrow):
    wide[...] = psi[...].reshape(4096, LANES).astype(F32)
    rows = wide[pl.ds(0, 256, stride=16), :]
    narrow[...] = jnp.zeros_like(narrow)
    for x in range(16):
        narrow[x * SIDE : x * SIDE + 16, :] = rows[x * 16 : x * 16 + 16]
    rows_out[...] = narrow[...]


def first_rows(psi):
    return pl.pallas_call(
        first_rows_kernel,
        out_shape=shape((FACE, LANES), F32),
        in_specs=[VMEM],
        out_specs=VMEM,
        scratch_shapes=[pltpu.VMEM((4096, LANES), F32), pltpu.VMEM((FACE, LANES), F32)],
        cost_estimate=cost(1e6, 1.2e6),
        compiler_params=SMALL,
        name="first_rows",
    )(psi)


def first_y_kernel(psi_y, from_x, out):
    out[0:256, :] = psi_y[...].reshape(256, LANES)
    out[256:272, :] = from_x[0:16, :]


def first_y(psi, from_x):
    return pl.pallas_call(
        first_y_kernel,
        grid=(1,),
        out_shape=shape((272, LANES), BF16),
        in_specs=[
            pl.BlockSpec((16, 1, 16, LANES), lambda i: (0, 0, 0, 0)),
            pl.BlockSpec((256, LANES), lambda i: (0, 0)),
        ],
        out_specs=pl.BlockSpec((272, LANES), lambda i: (0, 0)),
        cost_estimate=cost(1e5, 2e5),
        compiler_params=SMALL,
        name="first_y",
    )(psi, from_x)


def first_z_kernel(rows, from_x, from_y, out, wide_x, wide_y, face):
    wide_x[...] = from_x[...].astype(F32)
    wide_y[...] = from_y[...].astype(F32)
    face[...] = rows[...]
    face[16 * SIDE : 16 * SIDE + 16, :] = wide_x[pl.ds(0, 16, stride=16), :]
    face[pl.ds(16, SIDE, stride=SIDE), :] = wide_y[pl.ds(0, SIDE, stride=16), :]
    out[...] = face[...].astype(BF16)


def first_z(rows, from_x, from_y):
    return pl.pallas_call(
        first_z_kernel,
        out_shape=shape((FACE, LANES), BF16),
        in_specs=[VMEM] * 3,
        out_specs=VMEM,
        scratch_shapes=[
            pltpu.VMEM((256, LANES), F32),
            pltpu.VMEM((272, LANES), F32),
            pltpu.VMEM((FACE, LANES), F32),
        ],
        cost_estimate=cost(1e5, 4e5),
        compiler_params=SMALL,
        name="first_z",
    )(rows, from_x, from_y)


def begin_kernel(psi, from_x, from_y, from_z, field_out, field, wide):
    field[...] = jnp.zeros_like(field)

    def slab(x, carry):
        for y in range(16):
            start = pl.multiple_of(x * SLAB + y * ZPAD, 8)
            field[pl.ds(start, 16), :] = psi[x, y].astype(F32)
        return carry

    lax.fori_loop(0, 16, slab, 0)
    for y in range(16):
        at = 16 * SLAB + y * ZPAD
        field[at : at + 16, :] = from_x[y * 16 : y * 16 + 16, :].astype(F32)
    for x in range(SIDE):
        at = x * SLAB + 16 * ZPAD
        field[at : at + 16, :] = from_y[x * 16 : x * 16 + 16, :].astype(F32)
    wide[...] = from_z[...].astype(F32)
    field[pl.ds(16, PLANE, stride=ZPAD), :] = wide[0:PLANE, :]

    def chunk(n, carry):
        spot = pl.ds(pl.multiple_of(n * CHUNK, 16), CHUNK)
        field_out[spot, :] = field[spot, :].astype(BF16)
        return carry

    lax.fori_loop(0, ROWS // CHUNK, chunk, 0)


def begin(psi, from_x, from_y, from_z):
    return pl.pallas_call(
        begin_kernel,
        out_shape=shape((ROWS, LANES), BF16),
        in_specs=[VMEM] * 4,
        out_specs=VMEM,
        scratch_shapes=[pltpu.VMEM((ROWS, LANES), F32), pltpu.VMEM((FACE, LANES), F32)],
        cost_estimate=cost(1e7, 4e6),
        compiler_params=LARGE,
        name="begin",
    )(psi, from_x, from_y, from_z)


MESSAGE_Y = FACE + 288
MESSAGE_Z = FACE + 480
MESSAGE_X = FACE + 800


def send(odd, low, high, first, second, rows):
    first[rows, :] = jnp.where(odd, low, high).astype(BF16)
    second[rows, :] = jnp.where(odd, high, low).astype(BF16)


def receive(odd, first, second, rows):
    one, two = first[rows, :].astype(F32), second[rows, :].astype(F32)
    return jnp.where(odd, one, two), jnp.where(odd, two, one)


def apply_kernel(odd, now, ham, rows, mix, terms, send_one, send_two, zface, xface, weights, field, cell32, total, yface):
    position = pl.program_id(0)

    @pl.when(position == 0)
    def _():
        def chunk(n, carry):
            spot = pl.ds(pl.multiple_of(n * CHUNK, 16), CHUNK)
            field[spot, :] = now[spot, :].astype(F32)
            return carry

        lax.fori_loop(0, ROWS // CHUNK, chunk, 0)
        for ref in (total, xface, yface, zface):
            ref[...] = jnp.zeros_like(ref)

    a, b, c = position // 4, (position // 2) % 2, position % 2
    base = cell_base(a, b, c)
    for x in range(9):
        for y in range(9):
            at = (x * 9 + y) * 9
            cell32[at : at + 9, :] = field[pl.ds(line_start(base, x, y), 9), :]
    values = cell32[0:CELL, :].astype(BF16)
    part = jnp.dot(rows[0], values, preferred_element_type=F32)
    for o in range(8):
        i, j, k = o // 4, (o // 2) % 2, o % 2
        vertex = (a + i) * 9 + (b + j) * 3 + c + k
        total[pl.ds(pl.multiple_of(vertex * 16, 16), 16), :] += part[o * 16 : (o + 1) * 16]
    result = jnp.dot(ham[0], values, preferred_element_type=F32)
    terms[0] = result
    cell32[0:CELL, :] = result
    target = xface.at[pl.ds(pl.multiple_of(a * FACE + b * 136 + c * 8, 8), 152)]
    source = cell32.at[pl.ds(pl.multiple_of(a * 648, 8), 88)]
    for y in range(9):
        target[y * SIDE : y * SIDE + 9, :] += source[y * 9 : y * 9 + 9, :]
    target = yface.at[pl.ds(pl.multiple_of(b * FACE + a * 136 + c * 8, 8), 152)]
    source = cell32.at[pl.ds(pl.multiple_of(b * 72, 8), 664)]
    for x in range(9):
        target[x * SIDE : x * SIDE + 9, :] += source[x * 81 : x * 81 + 9, :]
    target = zface.at[pl.ds(pl.multiple_of(c * FACE + a * 136 + b * 8, 8), 152)]
    source = cell32.at[pl.ds(pl.multiple_of(c * 8, 8), 728)]
    for x in range(9):
        target[x * SIDE : x * SIDE + 9, :] += source[pl.ds(x * 81, 9, stride=9), :]

    @pl.when(position == pl.num_programs(0) - 1)
    def _():
        turn = odd[1] == 1
        for g in range(4):
            spot = slice(g * 128, g * 128 + 128)
            total[spot, :] = jnp.dot(mix[g], total[spot, :], precision=HIGHEST, preferred_element_type=F32)
        weights[...] = total[0:432, :]
        send(turn, yface[0:FACE, :], yface[FACE : 2 * FACE, :], send_one, send_two, slice(0, FACE))
        for p in range(2):
            for x in range(3):
                at = FACE + (p * 3 + x) * 48
                down = total[x * 144 + p * 48 : x * 144 + p * 48 + 48, :]
                up = total[x * 144 + (p + 1) * 48 : x * 144 + (p + 1) * 48 + 48, :]
                send(turn, down, up, send_one, send_two, slice(at, at + 48))


def apply_cells(odd, now, ham, rows, mix):
    whole = lambda *dims: pl.BlockSpec(dims, lambda n: (0,) * len(dims))
    faces = shape((2 * FACE, LANES), F32)
    message = shape((MESSAGE_Y, LANES), BF16)
    return pl.pallas_call(
        apply_kernel,
        grid=(8,),
        out_shape=(shape((8, CELL, LANES), F32), message, message, faces, faces, shape((432, LANES), F32)),
        in_specs=[
            SMEM,
            whole(ROWS, LANES),
            pl.BlockSpec((1, CELL, CELL), lambda n: (n, 0, 0)),
            pl.BlockSpec((1, 128, CELL), lambda n: (n, 0, 0)),
            whole(4, LANES, LANES),
        ],
        out_specs=(
            pl.BlockSpec((1, CELL, LANES), lambda n: (n, 0, 0)),
            whole(MESSAGE_Y, LANES),
            whole(MESSAGE_Y, LANES),
            whole(2 * FACE, LANES),
            whole(2 * FACE, LANES),
            whole(432, LANES),
        ),
        scratch_shapes=[
            pltpu.VMEM((ROWS, LANES), F32),
            pltpu.VMEM((736, LANES), F32),
            pltpu.VMEM((512, LANES), F32),
            pltpu.VMEM((2 * FACE, LANES), F32),
        ],
        cost_estimate=cost(1.3e9, 1.6e7),
        compiler_params=LARGE,
        name="apply_cells",
    )(odd, now, ham, rows, mix)


def assemble_kernel(first, terms, now, *refs):
    before = None if first else refs[0]
    field = refs[-1]
    scale = 1.0 if first else 2.0

    def chunk(n, carry):
        spot = pl.ds(pl.multiple_of(n * CHUNK, 16), CHUNK)
        value = -scale * now[spot, :].astype(F32)
        if before is not None:
            value = value - before[spot, :].astype(F32)
        field[spot, :] = value
        return carry

    lax.fori_loop(0, ROWS // CHUNK, chunk, 0)

    def cell(position, carry):
        a, b, c = position // 4, (position // 2) % 2, position % 2
        base = cell_base(a, b, c)
        for x in range(9):
            for y in range(9):
                at = (x * 9 + y) * 9
                field[pl.ds(line_start(base, x, y), 9), :] += scale * terms[position, at : at + 9, :]
        return carry

    lax.fori_loop(0, 8, cell, 0)


def assemble(terms, now, before):
    args = [terms, now] + ([] if before is None else [before])
    return pl.pallas_call(
        functools.partial(assemble_kernel, before is None),
        out_shape=shape((ROWS, LANES), F32),
        in_specs=[VMEM] * len(args),
        out_specs=VMEM,
        cost_estimate=cost(1e7, 1.2e7),
        compiler_params=SMALL,
        name="assemble",
    )(*args)


def after_y_kernel(odd, one, two, zface, xface, weights, send_one, send_two, xface_out, weights_out, low, high, face_low, face_high):
    low[...], high[...] = receive(odd[1] == 1, one, two, slice(0, FACE))
    turn = odd[2] == 1
    last = 16 * SIDE
    for face, start, column in ((face_low, 0, 0), (face_high, FACE, 16)):
        face[...] = zface[start : start + FACE, :]
        face[pl.ds(0, SIDE, stride=SIDE), :] += low[pl.ds(column, SIDE, stride=SIDE), :]
        face[pl.ds(16, SIDE, stride=SIDE), :] += high[pl.ds(column, SIDE, stride=SIDE), :]
    send(turn, face_low[...], face_high[...], send_one, send_two, slice(0, FACE))
    xface_out[...] = xface[...]
    for start, row in ((0, 0), (FACE, last)):
        xface_out[start : start + SIDE, :] += low[row : row + SIDE, :]
        xface_out[start + last : start + last + SIDE, :] += high[row : row + SIDE, :]
    for x in range(3):
        weights_out[x * 240 + 48 : x * 240 + 192, :] = weights[x * 144 : x * 144 + 144, :]
        for p in range(2):
            at = FACE + (p * 3 + x) * 48
            below, above = receive(odd[1] == 1, one, two, slice(at, at + 48))
            if p == 0:
                weights_out[x * 240 : x * 240 + 48, :] = below
                weights_out[x * 240 + 144 : x * 240 + 192, :] += above
            else:
                weights_out[x * 240 + 48 : x * 240 + 96, :] += below
                weights_out[x * 240 + 192 : x * 240 + 240, :] = above
    for p in range(2):
        for n in range(15):
            at = FACE + (p * 15 + n) * 16
            down = weights_out[n * 48 + p * 16 : n * 48 + p * 16 + 16, :]
            up = weights_out[n * 48 + p * 16 + 16 : n * 48 + p * 16 + 32, :]
            send(turn, down, up, send_one, send_two, slice(at, at + 16))


def after_y(odd, one, two, zface, xface, weights):
    message = shape((MESSAGE_Z, LANES), BF16)
    return pl.pallas_call(
        after_y_kernel,
        out_shape=(message, message, shape((2 * FACE, LANES), F32), shape((720, LANES), F32)),
        in_specs=[SMEM] + [VMEM] * 5,
        out_specs=(VMEM,) * 4,
        scratch_shapes=[pltpu.VMEM((FACE, LANES), F32)] * 4,
        cost_estimate=cost(1e5, 2e6),
        compiler_params=SMALL,
        name="after_y",
    )(odd, one, two, zface, xface, weights)


def after_z_kernel(odd, one, two, xface, weights, send_one, send_two, weights_out, low, high, face_low, face_high):
    low[...], high[...] = receive(odd[2] == 1, one, two, slice(0, FACE))
    turn = odd[0] == 1
    for face, start, row in ((face_low, 0, 0), (face_high, FACE, 16 * SIDE)):
        face[...] = xface[start : start + FACE, :]
        face[pl.ds(0, SIDE, stride=SIDE), :] += low[row : row + SIDE, :]
        face[pl.ds(16, SIDE, stride=SIDE), :] += high[row : row + SIDE, :]
    send(turn, face_low[...], face_high[...], send_one, send_two, slice(0, FACE))
    for n in range(15):
        weights_out[n * 80 + 16 : n * 80 + 64, :] = weights[n * 48 : n * 48 + 48, :]
        for p in range(2):
            at = FACE + (p * 15 + n) * 16
            below, above = receive(odd[2] == 1, one, two, slice(at, at + 16))
            if p == 0:
                weights_out[n * 80 : n * 80 + 16, :] = below
                weights_out[n * 80 + 48 : n * 80 + 64, :] += above
            else:
                weights_out[n * 80 + 16 : n * 80 + 32, :] += below
                weights_out[n * 80 + 64 : n * 80 + 80, :] = above
    for p in range(2):
        at = FACE + p * 400
        down, up = weights_out[p * 400 : p * 400 + 400, :], weights_out[p * 400 + 400 : p * 400 + 800, :]
        send(turn, down, up, send_one, send_two, slice(at, at + 400))


def after_z(odd, one, two, xface, weights):
    message = shape((MESSAGE_X, LANES), BF16)
    return pl.pallas_call(
        after_z_kernel,
        out_shape=(message, message, shape((1200, LANES), F32)),
        in_specs=[SMEM] + [VMEM] * 4,
        out_specs=(VMEM,) * 3,
        scratch_shapes=[pltpu.VMEM((FACE, LANES), F32)] * 4,
        cost_estimate=cost(1e5, 2e6),
        compiler_params=SMALL,
        name="after_z",
    )(odd, one, two, xface, weights)


def corner_weights(weights, a, b, c):
    pieces = []
    for o in range(8):
        i, j, k = o // 4, (o // 2) % 2, o % 2
        vertex = ((a + i) * 5 + b + j) * 5 + c + k
        pieces.append(weights[pl.ds(pl.multiple_of(vertex * 16, 16), 16), :])
    return jnp.concatenate(pieces, axis=0)


def advance_kernel(first, last, odd, start_field, y1, y2, z1, z2, x1, x2, w75, columns, faces, edges, points, out, *refs):
    del start_field
    parts = refs[: len(refs) - 6]
    field, cell32, weights, xs, ys, zs = refs[len(refs) - 6 :]
    scale = 1.0 if first else 2.0
    for ref, one, two, axis in ((xs, x1, x2, 0), (ys, y1, y2, 1), (zs, z1, z2, 2)):
        low, high = receive(odd[axis] == 1, one, two, slice(0, FACE))
        ref[0:FACE, :] = low
        ref[FACE : 2 * FACE, :] = high
    for p in range(2):
        at = FACE + p * 400
        below, above = receive(odd[0] == 1, x1, x2, slice(at, at + 400))
        if p == 0:
            weights[0:400, :] = below.astype(BF16)
            weights[1200:1600, :] = (w75[800:1200, :] + above).astype(BF16)
        else:
            weights[400:800, :] = (w75[0:400, :] + below).astype(BF16)
            weights[1600:2000, :] = above.astype(BF16)
    weights[800:1200, :] = w75[400:800, :].astype(BF16)

    def cell(position, carry):
        a, b, c = position // 4, (position // 2) % 2, position % 2
        corner = corner_weights(weights, a + 1, b + 1, c + 1)
        cell32[0:CELL, :] = scale * jnp.dot(columns[position], corner, preferred_element_type=F32)
        base = cell_base(a, b, c)
        for x in range(9):
            for y in range(9):
                at = (x * 9 + y) * 9
                field[pl.ds(line_start(base, x, y), 9), :] += cell32[at : at + 9, :]
        return carry

    lax.fori_loop(0, 8, cell, 0)

    for axis, ref in enumerate((xs, ys, zs)):

        def face(s, carry, axis=axis, ref=ref):
            for n in range(4):
                spot = [n // 2 + 1, n % 2 + 1]
                spot.insert(axis, 3 * s)
                cell32[n * 88 : n * 88 + 81, :] = jnp.dot(
                    faces[axis * 8 + s * 4 + n], corner_weights(weights, *spot), preferred_element_type=F32
                )
            for n in range(4):
                view = ref.at[pl.ds(pl.multiple_of(s * FACE + (n // 2) * 136 + (n % 2) * 8, 8), 152)]
                for row in range(9):
                    at = n * 88 + row * 9
                    view[row * SIDE : row * SIDE + 9, :] += cell32[at : at + 9, :]
            return carry

        lax.fori_loop(0, 2, face, 0)

    for axis in range(3):

        def edge(s, carry, axis=axis):
            terms = []
            for n in range(4):
                spot = [3 * s, 3 * (n // 2)]
                spot.insert(axis, n % 2 + 1)
                terms.append(
                    jnp.dot(edges[axis * 8 + s * 4 + n], corner_weights(weights, *spot), preferred_element_type=F32)
                )
            for n, term in enumerate(terms):
                t, u = n // 2, n % 2
                if axis == 2:
                    view = xs.at[pl.ds(pl.multiple_of(s * FACE + t * 272 + u * 8, 8), 16)]
                    view[0:9, :] += term
                else:
                    ref = xs if axis == 1 else ys
                    view = ref.at[pl.ds(pl.multiple_of(s * FACE + u * 136 + t * 16, 8), 152)]
                    view[pl.ds(0, 9, stride=SIDE), :] += term
            return carry

        lax.fori_loop(0, 2, edge, 0)

    def point(s, carry):
        terms = []
        for n in range(4):
            corner = corner_weights(weights, 3 * s, 3 * (n // 2), 3 * (n % 2))
            terms.append(jnp.dot(points[s * 4 + n], corner, preferred_element_type=F32))
        for n, term in enumerate(terms):
            view = xs.at[pl.ds(pl.multiple_of(s * FACE + (n // 2) * 272 + (n % 2) * 16, 8), 8)]
            view[0:1, :] += term
        return carry

    lax.fori_loop(0, 2, point, 0)

    for s in range(2):
        for y in range(SIDE):
            at = s * 16 * SLAB + y * ZPAD
            field[at : at + SIDE, :] += scale * xs[s * FACE + y * SIDE : s * FACE + (y + 1) * SIDE, :]
        for x in range(SIDE):
            at = s * 16 * ZPAD + x * SLAB
            field[at : at + SIDE, :] += scale * ys[s * FACE + x * SIDE : s * FACE + (x + 1) * SIDE, :]
        field[pl.ds(s * 16, PLANE, stride=ZPAD), :] += scale * zs[s * FACE : s * FACE + PLANE, :]

    if last:

        def slab(x, carry):
            for y in range(16):
                start = pl.multiple_of(x * SLAB + y * ZPAD, 8)
                out[x, y] = field[pl.ds(start, 16), :].astype(BF16)
            return carry

        lax.fori_loop(0, 16, slab, 0)
        for offset, part in enumerate(parts):
            quarter = (odd[3] + offset) % 4
            part[...] = out[pl.ds(quarter * 4, 4)].reshape(1024, LANES)
    else:

        def chunk(n, carry):
            spot = pl.ds(pl.multiple_of(n * CHUNK, 16), CHUNK)
            out[spot, :] = field[spot, :].astype(BF16)
            return carry

        lax.fori_loop(0, ROWS // CHUNK, chunk, 0)


def advance(odd, field, messages, w75, tables, first, last):
    args = [odd, field, *messages, w75, *tables]
    if last:
        outs = [shape((16, 16, 16, LANES), BF16)] + [shape((1024, LANES), BF16)] * 4
    else:
        outs = [shape((ROWS, LANES), BF16)]
    outs.append(shape((ROWS, LANES), F32))
    return pl.pallas_call(
        functools.partial(advance_kernel, first, last),
        out_shape=tuple(outs),
        in_specs=[SMEM] + [VMEM] * (len(args) - 1),
        out_specs=(VMEM,) * len(outs),
        input_output_aliases={1: len(outs) - 1},
        scratch_shapes=[pltpu.VMEM((736, LANES), F32), pltpu.VMEM((2000, LANES), BF16)]
        + [pltpu.VMEM((2 * FACE, LANES), F32)] * 3,
        cost_estimate=cost(3e8, 1.2e7),
        compiler_params=LARGE,
        name="advance",
    )(*args)[:-1]


def gram_kernel(x0, x1, x2, x3, own, m1, m2, m3):
    blocks = [x0[...], x1[...], x2[...], x3[...]]
    for row, left in enumerate(blocks):
        turned = left.T
        for column, out in ((0, own), (3, m1), (2, m2), (1, m3)):
            part = jnp.dot(turned, blocks[column], preferred_element_type=F32)
            out[row * 128 : row * 128 + 128, :] = part.astype(out.dtype)


def gram(blocks):
    return pl.pallas_call(
        gram_kernel,
        out_shape=(shape((512, LANES), F32),) + (shape((512, LANES), BF16),) * 3,
        in_specs=[VMEM] * 4,
        out_specs=(VMEM,) * 4,
        cost_estimate=cost(6e8, 2e6),
        compiler_params=LARGE,
        name="gram",
    )(*blocks)


def collect_kernel(band, own, m1, m2, m3, out):
    for row in range(4):
        total = own[row * 128 : row * 128 + 128, :]
        for offset, ref in ((1, m1), (2, m2), (3, m3)):
            source = (row - offset) % 4
            total = total + ref[source * 128 : source * 128 + 128, :].astype(F32)
        place = (band[0] + 4 - row) % 4
        out[pl.ds(place * 16, 16)] = total.reshape(16, 8, LANES).astype(BF16)


def collect(band, own, received):
    return pl.pallas_call(
        collect_kernel,
        out_shape=shape((64, 8, LANES), BF16),
        in_specs=[SMEM] + [VMEM] * 4,
        out_specs=VMEM,
        cost_estimate=cost(1e6, 1e6),
        compiler_params=SMALL,
        name="collect",
    )(band, own, *received)


def local(psi, cell_ham, proj_table, coupling, atom_kind):
    devices = lax.axis_size("cells")
    side = cube_root(devices)
    offsets = (1, side, side * side)
    block = lax.axis_index("cells")
    band = lax.axis_index("bands")
    odd = jnp.stack([(block // offset) % 2 for offset in offsets] + [band]).astype(jnp.int32)

    def upward(x, axis):
        return shifted(x, "cells", offsets[axis])

    def downward(x, axis):
        return shifted(x, "cells", -offsets[axis])

    def swap(messages, axis):
        offset = offsets[axis]
        arrived = []
        for start, message in enumerate(messages):
            pairs = []
            for i in range(devices):
                forward = (i // offset) % 2 == start
                pairs.append((i, (i + offset) % devices if forward else (i - offset) % devices))
            arrived.append(lax.ppermute(message, "cells", pairs))
        return arrived

    from_x = downward(psi[0].reshape(256, LANES), 0)
    kinds = atom_kind
    for axis in range(3):
        below = upward(lax.slice_in_dim(kinds, 1, 2, axis=axis), axis)
        above = downward(kinds, axis)
        kinds = jnp.concatenate([below, kinds, above], axis=axis)
    table = proj_table.reshape(4, 128, CELL)
    kinds = kinds.reshape(125)
    rows, mix = first_tables(kinds, table, jnp.tile(coupling, (1, 1, 8)))
    table_t = jnp.transpose(table, (0, 2, 1)).astype(F32)
    z_rows = first_rows(psi)
    from_y = downward(first_y(psi, from_x), 1)
    from_z = downward(first_z(z_rows, from_x, from_y), 2)

    def step(now, before, last, tables):
        terms, one, two, zface, xface, weights = apply_cells(odd, now, cell_ham, rows, mix)
        ys = swap((one, two), 1)
        if tables is None:
            tables = make_tables(kinds, table_t, weights)
        field = assemble(terms, now, before)
        one, two, xface, weights = after_y(odd, *ys, zface, xface, weights)
        zs = swap((one, two), 2)
        one, two, weights = after_z(odd, *zs, xface, weights)
        xs = swap((one, two), 0)
        return tables, advance(odd, field, (*ys, *zs, *xs), weights, tables, before is None, last)

    y0 = begin(psi, from_x, from_y, from_z)
    tables, (y1,) = step(y0, None, False, None)
    tables, (y2,) = step(y1, y0, False, tables)
    tables, (filtered, *blocks) = step(y2, y1, True, tables)

    blocks = [block if n == 0 else shifted(block, "bands", n) for n, block in enumerate(blocks)]
    own, *messages = gram(blocks)
    messages = [shifted(message, "bands", n + 1) for n, message in enumerate(messages)]
    terms = collect(band.astype(jnp.int32).reshape(1), own, messages)
    terms = lax.all_to_all(terms, "cells", 0, 0)
    inverse_count = 1.0 / (4096 * devices)
    correlation = jnp.sum(terms.astype(F32), axis=0) * inverse_count
    return filtered, correlation


def solution(mesh):
    in_specs = (
        P("cells", None, None, "bands"),
        P("cells", None, None),
        P(),
        P(),
        P("cells", None, None),
    )
    out_specs = (P("cells", None, None, "bands"), P("cells", "bands"))
    return jax.shard_map(local, mesh=mesh, in_specs=in_specs, out_specs=out_specs, check_vma=False)
```

```python
import functools

import jax
import jax.numpy as jnp
from jax import lax
from jax.experimental import pallas as pl
from jax.experimental.pallas import tpu as pltpu
from jax.sharding import PartitionSpec as P


F32 = jnp.float32
BF16 = jnp.bfloat16
HIGHEST = lax.Precision.HIGHEST

SIDE = 17
ZPAD = 24
SLAB = SIDE * ZPAD
ROWS = 6944
CHUNK = 496
FACE = 304
PLANE = SIDE * SIDE
CELL = 729
LANES = 128


def shifted(x, axis, by):
    devices = lax.axis_size(axis)
    return lax.ppermute(x, axis, [(i, (i + by) % devices) for i in range(devices)])


def cube_root(amount):
    result = 1
    while (result + 1) ** 3 <= amount:
        result = result + 1
    return result


def cost(flops, nbytes):
    return pl.CostEstimate(flops=int(flops), bytes_accessed=int(nbytes), transcendentals=0)


def shape(dims, dtype):
    return jax.ShapeDtypeStruct(dims, dtype)


VMEM = pl.BlockSpec(memory_space=pltpu.VMEM)
LARGE = pltpu.CompilerParams(vmem_limit_bytes=10 * 2**20)
SMALL = pltpu.CompilerParams(vmem_limit_bytes=6 * 2**20)
SMEM = pl.BlockSpec(memory_space=pltpu.SMEM)


def cell_base(a, b, c):
    return a * (8 * SLAB) + b * (8 * ZPAD) + c * 8


def line_start(base, x, y):
    return pl.multiple_of(base + (x * SLAB + y * ZPAD), 8)


def corner_kinds(kinds, a, b, c, lane):
    found = jnp.full((1, LANES), -1, jnp.int32)
    for o in range(8):
        i, j, k = o // 4, (o // 2) % 2, o % 2
        found = jnp.where(lane == o, kinds[((a + i) * 5 + b + j) * 5 + c + k], found)
    return found


def first_tables_kernel(kinds, table, coupling, rows_out, mix_out, wide):
    lane_wide = lax.broadcasted_iota(jnp.int32, (16, LANES), 1) // 16

    def cell(position, carry):
        a, b, c = position // 4, (position // 2) % 2, position % 2
        for o in range(8):
            i, j, k = o // 4, (o // 2) % 2, o % 2
            kind = kinds[((a + i + 1) * 5 + b + j + 1) * 5 + c + k + 1]
            found = table[jnp.maximum(kind, 0), o * 16 : (o + 1) * 16, :]
            keep = jnp.where(kind >= 0, 1.0, 0.0).astype(F32)
            rows_out[position, o * 16 : (o + 1) * 16, :] = (found.astype(F32) * keep).astype(BF16)
        return carry

    lax.fori_loop(0, 8, cell, 0)
    mix_out[...] = jnp.zeros_like(mix_out)
    along = lax.broadcasted_iota(jnp.int32, (16, LANES), 1) % 16
    repeat = jnp.where(along == lax.broadcasted_iota(jnp.int32, (16, LANES), 0), 1.0, 0.0).astype(F32)
    for q in range(coupling.shape[0]):
        wide[q] = jnp.dot(coupling[q], repeat, precision=HIGHEST, preferred_element_type=F32)

    def vertex(v, carry):
        kind = kinds[(v // 9 + 1) * 25 + ((v // 3) % 3 + 1) * 5 + v % 3 + 1]
        block = wide[jnp.maximum(kind, 0)]
        keep = jnp.where(kind >= 0, 1.0, 0.0).astype(F32)
        block = jnp.where(lane_wide == v % 8, block * keep, 0.0)
        mix_out[v // 8, pl.ds(pl.multiple_of((v % 8) * 16, 16), 16), :] = block
        return carry

    lax.fori_loop(0, 27, vertex, 0)


def first_tables(kinds, table, coupling):
    return pl.pallas_call(
        first_tables_kernel,
        out_shape=(shape((8, 128, CELL), BF16), shape((4, LANES, LANES), F32)),
        in_specs=[SMEM, VMEM, VMEM],
        out_specs=(VMEM,) * 2,
        scratch_shapes=[pltpu.VMEM((coupling.shape[0], 16, LANES), F32)],
        cost_estimate=cost(1e6, 3e6),
        compiler_params=SMALL,
        name="first_tables",
    )(kinds, table, coupling)


def turn_kernel(table, after, out, wide):
    del after
    wide[...] = jnp.zeros_like(wide)
    for q in range(out.shape[0]):
        wide[:, 0:CELL] = table[q].astype(F32)
        out[q] = wide[...].T


def turn(table, after):
    return pl.pallas_call(
        turn_kernel,
        out_shape=shape((table.shape[0], 768, LANES), F32),
        in_specs=[VMEM, pl.BlockSpec(memory_space=pl.ANY)],
        out_specs=VMEM,
        scratch_shapes=[pltpu.VMEM((LANES, 768), F32)],
        cost_estimate=cost(1e6, 3e6),
        compiler_params=SMALL,
        name="turn",
    )(table, after)


def tables_kernel(kinds, table_t, after, columns_out, faces_out, edges_out, points_out, picked):
    del after
    species = table_t.shape[0]
    lane = lax.broadcasted_iota(jnp.int32, (1, LANES), 1) // 16

    def choose(values, lane_kind):
        total = jnp.where(lane_kind == 0, values[0], 0.0)
        for q in range(1, species):
            total = jnp.where(lane_kind == q, values[q], total)
        return total.astype(BF16)

    def cell(position, carry):
        a, b, c = position // 4, (position // 2) % 2, position % 2
        lane_kind = corner_kinds(kinds, a + 1, b + 1, c + 1, lane)
        columns_out[position] = choose([table_t[q, 0:CELL] for q in range(species)], lane_kind)
        return carry

    lax.fori_loop(0, 8, cell, 0)
    for axis in range(3):
        for s in range(2):
            near = 8 - 8 * s
            for q in range(species):
                if axis == 0:
                    picked[q, 0:81] = table_t[q, near * 81 : near * 81 + 81]
                elif axis == 1:
                    for x in range(9):
                        picked[q, x * 9 : x * 9 + 9] = table_t[q, x * 81 + near * 9 : x * 81 + near * 9 + 9]
                else:
                    picked[q, 0:81] = table_t[q, pl.ds(near, 81, stride=9)]

            def face(n, carry, axis=axis, s=s):
                spot = [n // 2 + 1, n % 2 + 1]
                spot.insert(axis, 3 * s)
                lane_kind = corner_kinds(kinds, *spot, lane)
                faces_out[axis * 8 + s * 4 + n] = choose([picked[q, 0:81] for q in range(species)], lane_kind)
                return carry

            lax.fori_loop(0, 4, face, 0)
    for axis in range(3):
        for s in range(2):
            for t in range(2):
                first, second = 8 - 8 * s, 8 - 8 * t
                for u in range(2):
                    spot = [3 * s, 3 * t]
                    spot.insert(axis, u + 1)
                    start, stride = ((first * 9 + second, 81), (first * 81 + second, 9), (first * 81 + second * 9, 1))[axis]
                    lane_kind = corner_kinds(kinds, *spot, lane)
                    place = slice(start, start + 9) if stride == 1 else pl.ds(start, 9, stride=stride)
                    edges_out[axis * 8 + s * 4 + t * 2 + u, 0:9] = choose([table_t[q, place] for q in range(species)], lane_kind)
    for n in range(8):
        s, t, w = n // 4, (n // 2) % 2, n % 2
        at = (8 - 8 * s) * 81 + (8 - 8 * t) * 9 + 8 - 8 * w
        lane_kind = corner_kinds(kinds, 3 * s, 3 * t, 3 * w, lane)
        points_out[n, 0:1] = choose([table_t[q, at : at + 1] for q in range(species)], lane_kind)


def make_tables(kinds, table_t, after):
    species = table_t.shape[0]
    return pl.pallas_call(
        tables_kernel,
        out_shape=(
            shape((8, CELL, LANES), BF16),
            shape((24, 81, LANES), BF16),
            shape((24, 9, LANES), BF16),
            shape((8, 1, LANES), BF16),
        ),
        in_specs=[SMEM, VMEM, pl.BlockSpec(memory_space=pl.ANY)],
        out_specs=(VMEM,) * 4,
        scratch_shapes=[pltpu.VMEM((species, 88, LANES), F32)],
        cost_estimate=cost(1e7, 6e6),
        compiler_params=SMALL,
        name="tables",
    )(kinds, table_t, after)


def first_rows_kernel(psi, rows_out, wide, narrow):
    wide[...] = psi[...].reshape(4096, LANES).astype(F32)
    rows = wide[pl.ds(0, 256, stride=16), :]
    narrow[...] = jnp.zeros_like(narrow)
    for x in range(16):
        narrow[x * SIDE : x * SIDE + 16, :] = rows[x * 16 : x * 16 + 16]
    rows_out[...] = narrow[...]


def first_rows(psi):
    return pl.pallas_call(
        first_rows_kernel,
        out_shape=shape((FACE, LANES), F32),
        in_specs=[VMEM],
        out_specs=VMEM,
        scratch_shapes=[pltpu.VMEM((4096, LANES), F32), pltpu.VMEM((FACE, LANES), F32)],
        cost_estimate=cost(1e6, 1.2e6),
        compiler_params=SMALL,
        name="first_rows",
    )(psi)


def first_y_kernel(psi_y, from_x, out):
    out[0:256, :] = psi_y[...].reshape(256, LANES)
    out[256:272, :] = from_x[0:16, :]


def first_y(psi, from_x):
    return pl.pallas_call(
        first_y_kernel,
        grid=(1,),
        out_shape=shape((272, LANES), BF16),
        in_specs=[
            pl.BlockSpec((16, 1, 16, LANES), lambda i: (0, 0, 0, 0)),
            pl.BlockSpec((256, LANES), lambda i: (0, 0)),
        ],
        out_specs=pl.BlockSpec((272, LANES), lambda i: (0, 0)),
        cost_estimate=cost(1e5, 2e5),
        compiler_params=SMALL,
        name="first_y",
    )(psi, from_x)


def first_z_kernel(rows, from_x, from_y, out, wide_x, wide_y, face):
    wide_x[...] = from_x[...].astype(F32)
    wide_y[...] = from_y[...].astype(F32)
    face[...] = rows[...]
    face[16 * SIDE : 16 * SIDE + 16, :] = wide_x[pl.ds(0, 16, stride=16), :]
    face[pl.ds(16, SIDE, stride=SIDE), :] = wide_y[pl.ds(0, SIDE, stride=16), :]
    out[...] = face[...].astype(BF16)


def first_z(rows, from_x, from_y):
    return pl.pallas_call(
        first_z_kernel,
        out_shape=shape((FACE, LANES), BF16),
        in_specs=[VMEM] * 3,
        out_specs=VMEM,
        scratch_shapes=[
            pltpu.VMEM((256, LANES), F32),
            pltpu.VMEM((272, LANES), F32),
            pltpu.VMEM((FACE, LANES), F32),
        ],
        cost_estimate=cost(1e5, 4e5),
        compiler_params=SMALL,
        name="first_z",
    )(rows, from_x, from_y)


def begin_kernel(psi, from_x, from_y, from_z, field_out, field, wide):
    field[...] = jnp.zeros_like(field)

    def slab(x, carry):
        for y in range(16):
            start = pl.multiple_of(x * SLAB + y * ZPAD, 8)
            field[pl.ds(start, 16), :] = psi[x, y].astype(F32)
        return carry

    lax.fori_loop(0, 16, slab, 0)
    for y in range(16):
        at = 16 * SLAB + y * ZPAD
        field[at : at + 16, :] = from_x[y * 16 : y * 16 + 16, :].astype(F32)
    for x in range(SIDE):
        at = x * SLAB + 16 * ZPAD
        field[at : at + 16, :] = from_y[x * 16 : x * 16 + 16, :].astype(F32)
    wide[...] = from_z[...].astype(F32)
    field[pl.ds(16, PLANE, stride=ZPAD), :] = wide[0:PLANE, :]

    def chunk(n, carry):
        spot = pl.ds(pl.multiple_of(n * CHUNK, 16), CHUNK)
        field_out[spot, :] = field[spot, :].astype(BF16)
        return carry

    lax.fori_loop(0, ROWS // CHUNK, chunk, 0)


def begin(psi, from_x, from_y, from_z):
    return pl.pallas_call(
        begin_kernel,
        out_shape=shape((ROWS, LANES), BF16),
        in_specs=[VMEM] * 4,
        out_specs=VMEM,
        scratch_shapes=[pltpu.VMEM((ROWS, LANES), F32), pltpu.VMEM((FACE, LANES), F32)],
        cost_estimate=cost(1e7, 4e6),
        compiler_params=LARGE,
        name="begin",
    )(psi, from_x, from_y, from_z)


HAM_ROWS = 128


def by_cell_kernel(source, after, out, wide):
    del after
    def piece(n, carry):
        spot = pl.ds(pl.multiple_of(n * 16, 16), 16)
        for start in range(0, CELL, LANES):
            width = min(LANES, CELL - start)
            block = wide.at[start : start + LANES]
            block[:, 0:width] = source[spot, :, start : start + width].astype(F32).reshape(128, width)
            for c in range(8):
                found = block[pl.ds(c, 16, stride=8), :]
                out[c, spot, start : start + width] = found[:, 0:width].astype(BF16)
        return carry

    lax.fori_loop(0, HAM_ROWS // 16, piece, 0)


def by_cell(ham, after):
    return pl.pallas_call(
        by_cell_kernel,
        grid=(pl.cdiv(CELL, HAM_ROWS),),
        out_shape=shape((8, CELL, CELL), BF16),
        in_specs=[pl.BlockSpec((HAM_ROWS, 8, CELL), lambda n: (n, 0, 0)), pl.BlockSpec(memory_space=pl.ANY)],
        out_specs=pl.BlockSpec((8, HAM_ROWS, CELL), lambda n: (0, n, 0)),
        scratch_shapes=[pltpu.VMEM((768, LANES), F32)],
        cost_estimate=cost(1e7, 1.8e7),
        compiler_params=LARGE,
        name="by_cell",
    )(pltpu.with_memory_space_constraint(jnp.transpose(ham, (1, 0, 2)), pltpu.HBM), after)


MESSAGE_Y = FACE + 288
MESSAGE_Z = FACE + 480
MESSAGE_X = FACE + 800


def send(odd, low, high, first, second, rows):
    first[rows, :] = jnp.where(odd, low, high).astype(BF16)
    second[rows, :] = jnp.where(odd, high, low).astype(BF16)


def receive(odd, first, second, rows):
    one, two = first[rows, :].astype(F32), second[rows, :].astype(F32)
    return jnp.where(odd, one, two), jnp.where(odd, two, one)


def apply_kernel(odd, now, ham, rows, mix, terms, send_one, send_two, zface, xface, weights, field, cell32, total, yface):
    def chunk(n, carry):
        spot = pl.ds(pl.multiple_of(n * CHUNK, 16), CHUNK)
        field[spot, :] = now[spot, :].astype(F32)
        return carry

    lax.fori_loop(0, ROWS // CHUNK, chunk, 0)
    for ref in (total, xface, yface, zface):
        ref[...] = jnp.zeros_like(ref)

    def cell(position, carry):
        a, b, c = position // 4, (position // 2) % 2, position % 2
        base = cell_base(a, b, c)
        for x in range(9):
            for y in range(9):
                at = (x * 9 + y) * 9
                cell32[at : at + 9, :] = field[pl.ds(line_start(base, x, y), 9), :]
        values = cell32[0:CELL, :].astype(BF16)
        part = jnp.dot(rows[position], values, preferred_element_type=F32)
        for o in range(8):
            i, j, k = o // 4, (o // 2) % 2, o % 2
            vertex = (a + i) * 9 + (b + j) * 3 + c + k
            total[pl.ds(pl.multiple_of(vertex * 16, 16), 16), :] += part[o * 16 : (o + 1) * 16]
        result = jnp.dot(ham[position], values, preferred_element_type=F32)
        terms[position] = result
        cell32[0:CELL, :] = result
        target = xface.at[pl.ds(pl.multiple_of(a * FACE + b * 136 + c * 8, 8), 152)]
        source = cell32.at[pl.ds(pl.multiple_of(a * 648, 8), 88)]
        for y in range(9):
            target[y * SIDE : y * SIDE + 9, :] += source[y * 9 : y * 9 + 9, :]
        target = yface.at[pl.ds(pl.multiple_of(b * FACE + a * 136 + c * 8, 8), 152)]
        source = cell32.at[pl.ds(pl.multiple_of(b * 72, 8), 664)]
        for x in range(9):
            target[x * SIDE : x * SIDE + 9, :] += source[x * 81 : x * 81 + 9, :]
        target = zface.at[pl.ds(pl.multiple_of(c * FACE + a * 136 + b * 8, 8), 152)]
        source = cell32.at[pl.ds(pl.multiple_of(c * 8, 8), 728)]
        for x in range(9):
            target[x * SIDE : x * SIDE + 9, :] += source[pl.ds(x * 81, 9, stride=9), :]
        return carry

    lax.fori_loop(0, 8, cell, 0)
    turn = odd[1] == 1
    for g in range(4):
        spot = slice(g * 128, g * 128 + 128)
        total[spot, :] = jnp.dot(mix[g], total[spot, :], precision=HIGHEST, preferred_element_type=F32)
    weights[...] = total[0:432, :]
    send(turn, yface[0:FACE, :], yface[FACE : 2 * FACE, :], send_one, send_two, slice(0, FACE))
    for p in range(2):
        for x in range(3):
            at = FACE + (p * 3 + x) * 48
            down = total[x * 144 + p * 48 : x * 144 + p * 48 + 48, :]
            up = total[x * 144 + (p + 1) * 48 : x * 144 + (p + 1) * 48 + 48, :]
            send(turn, down, up, send_one, send_two, slice(at, at + 48))


def apply_cells(odd, now, ham, rows, mix):
    faces = shape((2 * FACE, LANES), F32)
    message = shape((MESSAGE_Y, LANES), BF16)
    return pl.pallas_call(
        apply_kernel,
        out_shape=(shape((8, CELL, LANES), F32), message, message, faces, faces, shape((432, LANES), F32)),
        in_specs=[SMEM] + [VMEM] * 4,
        out_specs=(VMEM,) * 6,
        scratch_shapes=[
            pltpu.VMEM((ROWS, LANES), F32),
            pltpu.VMEM((736, LANES), F32),
            pltpu.VMEM((512, LANES), F32),
            pltpu.VMEM((2 * FACE, LANES), F32),
        ],
        cost_estimate=cost(1.3e9, 1.6e7),
        compiler_params=LARGE,
        name="apply_cells",
    )(odd, now, ham, rows, mix)


def assemble_kernel(first, terms, now, *refs):
    before = None if first else refs[0]
    field = refs[-1]
    scale = 1.0 if first else 2.0

    def chunk(n, carry):
        spot = pl.ds(pl.multiple_of(n * CHUNK, 16), CHUNK)
        value = -scale * now[spot, :].astype(F32)
        if before is not None:
            value = value - before[spot, :].astype(F32)
        field[spot, :] = value
        return carry

    lax.fori_loop(0, ROWS // CHUNK, chunk, 0)

    def cell(position, carry):
        a, b, c = position // 4, (position // 2) % 2, position % 2
        base = cell_base(a, b, c)
        for x in range(9):
            for y in range(9):
                at = (x * 9 + y) * 9
                field[pl.ds(line_start(base, x, y), 9), :] += scale * terms[position, at : at + 9, :]
        return carry

    lax.fori_loop(0, 8, cell, 0)


def assemble(terms, now, before):
    args = [terms, now] + ([] if before is None else [before])
    return pl.pallas_call(
        functools.partial(assemble_kernel, before is None),
        out_shape=shape((ROWS, LANES), F32),
        in_specs=[VMEM] * len(args),
        out_specs=VMEM,
        cost_estimate=cost(1e7, 1.2e7),
        compiler_params=SMALL,
        name="assemble",
    )(*args)


def after_y_kernel(odd, one, two, zface, xface, weights, send_one, send_two, xface_out, weights_out, low, high, face_low, face_high):
    low[...], high[...] = receive(odd[1] == 1, one, two, slice(0, FACE))
    turn = odd[2] == 1
    last = 16 * SIDE
    for face, start, column in ((face_low, 0, 0), (face_high, FACE, 16)):
        face[...] = zface[start : start + FACE, :]
        face[pl.ds(0, SIDE, stride=SIDE), :] += low[pl.ds(column, SIDE, stride=SIDE), :]
        face[pl.ds(16, SIDE, stride=SIDE), :] += high[pl.ds(column, SIDE, stride=SIDE), :]
    send(turn, face_low[...], face_high[...], send_one, send_two, slice(0, FACE))
    xface_out[...] = xface[...]
    for start, row in ((0, 0), (FACE, last)):
        xface_out[start : start + SIDE, :] += low[row : row + SIDE, :]
        xface_out[start + last : start + last + SIDE, :] += high[row : row + SIDE, :]
    for x in range(3):
        weights_out[x * 240 + 48 : x * 240 + 192, :] = weights[x * 144 : x * 144 + 144, :]
        for p in range(2):
            at = FACE + (p * 3 + x) * 48
            below, above = receive(odd[1] == 1, one, two, slice(at, at + 48))
            if p == 0:
                weights_out[x * 240 : x * 240 + 48, :] = below
                weights_out[x * 240 + 144 : x * 240 + 192, :] += above
            else:
                weights_out[x * 240 + 48 : x * 240 + 96, :] += below
                weights_out[x * 240 + 192 : x * 240 + 240, :] = above
    for p in range(2):
        for n in range(15):
            at = FACE + (p * 15 + n) * 16
            down = weights_out[n * 48 + p * 16 : n * 48 + p * 16 + 16, :]
            up = weights_out[n * 48 + p * 16 + 16 : n * 48 + p * 16 + 32, :]
            send(turn, down, up, send_one, send_two, slice(at, at + 16))


def after_y(odd, one, two, zface, xface, weights):
    message = shape((MESSAGE_Z, LANES), BF16)
    return pl.pallas_call(
        after_y_kernel,
        out_shape=(message, message, shape((2 * FACE, LANES), F32), shape((720, LANES), F32)),
        in_specs=[SMEM] + [VMEM] * 5,
        out_specs=(VMEM,) * 4,
        scratch_shapes=[pltpu.VMEM((FACE, LANES), F32)] * 4,
        cost_estimate=cost(1e5, 2e6),
        compiler_params=SMALL,
        name="after_y",
    )(odd, one, two, zface, xface, weights)


def after_z_kernel(odd, one, two, xface, weights, send_one, send_two, weights_out, low, high, face_low, face_high):
    low[...], high[...] = receive(odd[2] == 1, one, two, slice(0, FACE))
    turn = odd[0] == 1
    for face, start, row in ((face_low, 0, 0), (face_high, FACE, 16 * SIDE)):
        face[...] = xface[start : start + FACE, :]
        face[pl.ds(0, SIDE, stride=SIDE), :] += low[row : row + SIDE, :]
        face[pl.ds(16, SIDE, stride=SIDE), :] += high[row : row + SIDE, :]
    send(turn, face_low[...], face_high[...], send_one, send_two, slice(0, FACE))
    for n in range(15):
        weights_out[n * 80 + 16 : n * 80 + 64, :] = weights[n * 48 : n * 48 + 48, :]
        for p in range(2):
            at = FACE + (p * 15 + n) * 16
            below, above = receive(odd[2] == 1, one, two, slice(at, at + 16))
            if p == 0:
                weights_out[n * 80 : n * 80 + 16, :] = below
                weights_out[n * 80 + 48 : n * 80 + 64, :] += above
            else:
                weights_out[n * 80 + 16 : n * 80 + 32, :] += below
                weights_out[n * 80 + 64 : n * 80 + 80, :] = above
    for p in range(2):
        at = FACE + p * 400
        down, up = weights_out[p * 400 : p * 400 + 400, :], weights_out[p * 400 + 400 : p * 400 + 800, :]
        send(turn, down, up, send_one, send_two, slice(at, at + 400))


def after_z(odd, one, two, xface, weights):
    message = shape((MESSAGE_X, LANES), BF16)
    return pl.pallas_call(
        after_z_kernel,
        out_shape=(message, message, shape((1200, LANES), F32)),
        in_specs=[SMEM] + [VMEM] * 4,
        out_specs=(VMEM,) * 3,
        scratch_shapes=[pltpu.VMEM((FACE, LANES), F32)] * 4,
        cost_estimate=cost(1e5, 2e6),
        compiler_params=SMALL,
        name="after_z",
    )(odd, one, two, xface, weights)


def corner_weights(weights, a, b, c):
    pieces = []
    for o in range(8):
        i, j, k = o // 4, (o // 2) % 2, o % 2
        vertex = ((a + i) * 5 + b + j) * 5 + c + k
        pieces.append(weights[pl.ds(pl.multiple_of(vertex * 16, 16), 16), :])
    return jnp.concatenate(pieces, axis=0)


def advance_kernel(first, last, odd, start_field, y1, y2, z1, z2, x1, x2, w75, columns, faces, edges, points, out, *refs):
    del start_field
    parts = refs[: len(refs) - 6]
    field, cell32, weights, xs, ys, zs = refs[len(refs) - 6 :]
    scale = 1.0 if first else 2.0
    for ref, one, two, axis in ((xs, x1, x2, 0), (ys, y1, y2, 1), (zs, z1, z2, 2)):
        low, high = receive(odd[axis] == 1, one, two, slice(0, FACE))
        ref[0:FACE, :] = low
        ref[FACE : 2 * FACE, :] = high
    for p in range(2):
        at = FACE + p * 400
        below, above = receive(odd[0] == 1, x1, x2, slice(at, at + 400))
        if p == 0:
            weights[0:400, :] = below.astype(BF16)
            weights[1200:1600, :] = (w75[800:1200, :] + above).astype(BF16)
        else:
            weights[400:800, :] = (w75[0:400, :] + below).astype(BF16)
            weights[1600:2000, :] = above.astype(BF16)
    weights[800:1200, :] = w75[400:800, :].astype(BF16)

    def cell(position, carry):
        a, b, c = position // 4, (position // 2) % 2, position % 2
        corner = corner_weights(weights, a + 1, b + 1, c + 1)
        cell32[0:CELL, :] = scale * jnp.dot(columns[position], corner, preferred_element_type=F32)
        base = cell_base(a, b, c)
        for x in range(9):
            for y in range(9):
                at = (x * 9 + y) * 9
                field[pl.ds(line_start(base, x, y), 9), :] += cell32[at : at + 9, :]
        return carry

    lax.fori_loop(0, 8, cell, 0)

    for axis, ref in enumerate((xs, ys, zs)):

        def face(s, carry, axis=axis, ref=ref):
            for n in range(4):
                spot = [n // 2 + 1, n % 2 + 1]
                spot.insert(axis, 3 * s)
                cell32[n * 88 : n * 88 + 81, :] = jnp.dot(
                    faces[axis * 8 + s * 4 + n], corner_weights(weights, *spot), preferred_element_type=F32
                )
            for n in range(4):
                view = ref.at[pl.ds(pl.multiple_of(s * FACE + (n // 2) * 136 + (n % 2) * 8, 8), 152)]
                for row in range(9):
                    at = n * 88 + row * 9
                    view[row * SIDE : row * SIDE + 9, :] += cell32[at : at + 9, :]
            return carry

        lax.fori_loop(0, 2, face, 0)

    for axis in range(3):

        def edge(s, carry, axis=axis):
            terms = []
            for n in range(4):
                spot = [3 * s, 3 * (n // 2)]
                spot.insert(axis, n % 2 + 1)
                terms.append(
                    jnp.dot(edges[axis * 8 + s * 4 + n], corner_weights(weights, *spot), preferred_element_type=F32)
                )
            for n, term in enumerate(terms):
                t, u = n // 2, n % 2
                if axis == 2:
                    view = xs.at[pl.ds(pl.multiple_of(s * FACE + t * 272 + u * 8, 8), 16)]
                    view[0:9, :] += term
                else:
                    ref = xs if axis == 1 else ys
                    view = ref.at[pl.ds(pl.multiple_of(s * FACE + u * 136 + t * 16, 8), 152)]
                    view[pl.ds(0, 9, stride=SIDE), :] += term
            return carry

        lax.fori_loop(0, 2, edge, 0)

    def point(s, carry):
        terms = []
        for n in range(4):
            corner = corner_weights(weights, 3 * s, 3 * (n // 2), 3 * (n % 2))
            terms.append(jnp.dot(points[s * 4 + n], corner, preferred_element_type=F32))
        for n, term in enumerate(terms):
            view = xs.at[pl.ds(pl.multiple_of(s * FACE + (n // 2) * 272 + (n % 2) * 16, 8), 8)]
            view[0:1, :] += term
        return carry

    lax.fori_loop(0, 2, point, 0)

    for s in range(2):
        for y in range(SIDE):
            at = s * 16 * SLAB + y * ZPAD
            field[at : at + SIDE, :] += scale * xs[s * FACE + y * SIDE : s * FACE + (y + 1) * SIDE, :]
        for x in range(SIDE):
            at = s * 16 * ZPAD + x * SLAB
            field[at : at + SIDE, :] += scale * ys[s * FACE + x * SIDE : s * FACE + (x + 1) * SIDE, :]
        field[pl.ds(s * 16, PLANE, stride=ZPAD), :] += scale * zs[s * FACE : s * FACE + PLANE, :]

    if last:

        def slab(x, carry):
            for y in range(16):
                start = pl.multiple_of(x * SLAB + y * ZPAD, 8)
                out[x, y] = field[pl.ds(start, 16), :].astype(BF16)
            return carry

        lax.fori_loop(0, 16, slab, 0)
        for offset, part in enumerate(parts):
            quarter = (odd[3] + offset) % 4
            part[...] = out[pl.ds(quarter * 4, 4)].reshape(1024, LANES)
    else:

        def chunk(n, carry):
            spot = pl.ds(pl.multiple_of(n * CHUNK, 16), CHUNK)
            out[spot, :] = field[spot, :].astype(BF16)
            return carry

        lax.fori_loop(0, ROWS // CHUNK, chunk, 0)


def advance(odd, field, messages, w75, tables, first, last):
    args = [odd, field, *messages, w75, *tables]
    if last:
        outs = [shape((16, 16, 16, LANES), BF16)] + [shape((1024, LANES), BF16)] * 4
    else:
        outs = [shape((ROWS, LANES), BF16)]
    outs.append(shape((ROWS, LANES), F32))
    return pl.pallas_call(
        functools.partial(advance_kernel, first, last),
        out_shape=tuple(outs),
        in_specs=[SMEM] + [VMEM] * (len(args) - 1),
        out_specs=(VMEM,) * len(outs),
        input_output_aliases={1: len(outs) - 1},
        scratch_shapes=[pltpu.VMEM((736, LANES), F32), pltpu.VMEM((2000, LANES), BF16)]
        + [pltpu.VMEM((2 * FACE, LANES), F32)] * 3,
        cost_estimate=cost(3e8, 1.2e7),
        compiler_params=LARGE,
        name="advance",
    )(*args)[:-1]


def gram_kernel(x0, x1, x2, x3, own, m1, m2, m3):
    blocks = [x0[...], x1[...], x2[...], x3[...]]
    for row, left in enumerate(blocks):
        turned = left.T
        for column, out in ((0, own), (3, m1), (2, m2), (1, m3)):
            part = jnp.dot(turned, blocks[column], preferred_element_type=F32)
            out[row * 128 : row * 128 + 128, :] = part.astype(out.dtype)


def gram(blocks):
    return pl.pallas_call(
        gram_kernel,
        out_shape=(shape((512, LANES), F32),) + (shape((512, LANES), BF16),) * 3,
        in_specs=[VMEM] * 4,
        out_specs=(VMEM,) * 4,
        cost_estimate=cost(6e8, 2e6),
        compiler_params=LARGE,
        name="gram",
    )(*blocks)


def collect_kernel(band, own, m1, m2, m3, out):
    for row in range(4):
        total = own[row * 128 : row * 128 + 128, :]
        for offset, ref in ((1, m1), (2, m2), (3, m3)):
            source = (row - offset) % 4
            total = total + ref[source * 128 : source * 128 + 128, :].astype(F32)
        place = (band[0] + 4 - row) % 4
        out[pl.ds(place * 16, 16)] = total.reshape(16, 8, LANES).astype(BF16)


def collect(band, own, received):
    return pl.pallas_call(
        collect_kernel,
        out_shape=shape((64, 8, LANES), BF16),
        in_specs=[SMEM] + [VMEM] * 4,
        out_specs=VMEM,
        cost_estimate=cost(1e6, 1e6),
        compiler_params=SMALL,
        name="collect",
    )(band, own, *received)


def local(psi, cell_ham, proj_table, coupling, atom_kind):
    devices = lax.axis_size("cells")
    side = cube_root(devices)
    offsets = (1, side, side * side)
    block = lax.axis_index("cells")
    band = lax.axis_index("bands")
    odd = jnp.stack([(block // offset) % 2 for offset in offsets] + [band]).astype(jnp.int32)

    def upward(x, axis):
        return shifted(x, "cells", offsets[axis])

    def downward(x, axis):
        return shifted(x, "cells", -offsets[axis])

    def swap(messages, axis):
        offset = offsets[axis]
        arrived = []
        for start, message in enumerate(messages):
            pairs = []
            for i in range(devices):
                forward = (i // offset) % 2 == start
                pairs.append((i, (i + offset) % devices if forward else (i - offset) % devices))
            arrived.append(lax.ppermute(message, "cells", pairs))
        return arrived

    from_x = downward(psi[0].reshape(256, LANES), 0)
    kinds = atom_kind
    for axis in range(3):
        below = upward(lax.slice_in_dim(kinds, 1, 2, axis=axis), axis)
        above = downward(kinds, axis)
        kinds = jnp.concatenate([below, kinds, above], axis=axis)
    table = proj_table.reshape(4, 128, CELL)
    kinds = kinds.reshape(125)
    rows, mix = first_tables(kinds, table, coupling)
    z_rows = first_rows(psi)
    from_y = downward(first_y(psi, from_x), 1)
    from_z = downward(first_z(z_rows, from_x, from_y), 2)

    ham = by_cell(cell_ham, kinds)

    def step(now, before, last, tables):
        terms, one, two, zface, xface, weights = apply_cells(odd, now, ham, rows, mix)
        ys = swap((one, two), 1)
        if tables is None:
            tables = make_tables(kinds, turn(table, weights), weights)
        field = assemble(terms, now, before)
        one, two, xface, weights = after_y(odd, *ys, zface, xface, weights)
        zs = swap((one, two), 2)
        one, two, weights = after_z(odd, *zs, xface, weights)
        xs = swap((one, two), 0)
        return tables, advance(odd, field, (*ys, *zs, *xs), weights, tables, before is None, last)

    y0 = begin(psi, from_x, from_y, from_z)
    tables, (y1,) = step(y0, None, False, None)
    tables, (y2,) = step(y1, y0, False, tables)
    tables, (filtered, *blocks) = step(y2, y1, True, tables)

    blocks = [block if n == 0 else shifted(block, "bands", n) for n, block in enumerate(blocks)]
    own, *messages = gram(blocks)
    messages = [shifted(message, "bands", n + 1) for n, message in enumerate(messages)]
    terms = collect(band.astype(jnp.int32).reshape(1), own, messages)
    terms = lax.all_to_all(terms, "cells", 0, 0)
    inverse_count = 1.0 / (4096 * devices)
    correlation = jnp.sum(terms.astype(F32), axis=0) * inverse_count
    return filtered, correlation


def solution(mesh):
    in_specs = (
        P("cells", None, None, "bands"),
        P("cells", None, None),
        P(),
        P(),
        P("cells", None, None),
    )
    out_specs = (P("cells", None, None, "bands"), P("cells", "bands"))
    return jax.shard_map(local, mesh=mesh, in_specs=in_specs, out_specs=out_specs, check_vma=False)
```

```python
import functools

import jax
import jax.numpy as jnp
from jax import lax
from jax.experimental import pallas as pl
from jax.experimental.pallas import tpu as pltpu
from jax.sharding import PartitionSpec as P


F32 = jnp.float32
BF16 = jnp.bfloat16
HIGHEST = lax.Precision.HIGHEST

SIDE = 17
ZPAD = 24
SLAB = SIDE * ZPAD
ROWS = 6944
CHUNK = 496
FACE = 304
PLANE = SIDE * SIDE
CELL = 729
LANES = 128


def shifted(x, axis, by):
    devices = lax.axis_size(axis)
    return lax.ppermute(x, axis, [(i, (i + by) % devices) for i in range(devices)])


def cube_root(amount):
    result = 1
    while (result + 1) ** 3 <= amount:
        result = result + 1
    return result


def cost(flops, nbytes):
    return pl.CostEstimate(flops=int(flops), bytes_accessed=int(nbytes), transcendentals=0)


def shape(dims, dtype):
    return jax.ShapeDtypeStruct(dims, dtype)


VMEM = pl.BlockSpec(memory_space=pltpu.VMEM)
LARGE = pltpu.CompilerParams(vmem_limit_bytes=10 * 2**20)
SMALL = pltpu.CompilerParams(vmem_limit_bytes=6 * 2**20)
SMEM = pl.BlockSpec(memory_space=pltpu.SMEM)


def cell_base(a, b, c):
    return a * (8 * SLAB) + b * (8 * ZPAD) + c * 8


def line_start(base, x, y):
    return pl.multiple_of(base + (x * SLAB + y * ZPAD), 8)


def kind_row(kinds, a, b, c):
    return kinds[(a * 5 + b) * 5 + c][0:1, :]


def corner_kinds(kinds, a, b, c, lane):
    found = jnp.full((1, LANES), -1.0, F32)
    for o in range(8):
        i, j, k = o // 4, (o // 2) % 2, o % 2
        found = jnp.where(lane == o, kind_row(kinds, a + i, b + j, c + k), found)
    return found


def first_tables_kernel(from_z, up_z, s50, table, coupling, kinds, rows_out, mix_out, wide, table32):
    for n in range(25):
        kinds[n * 5] = jnp.broadcast_to(up_z[n : n + 1, :], (8, LANES))
        for k in range(2):
            at = n * 2 + k
            kinds[n * 5 + 1 + k] = jnp.broadcast_to(s50[at : at + 1, :], (8, LANES))
    above = from_z[FACE : FACE + 64, :].astype(F32)
    for n in range(50):
        kinds[(n // 2) * 5 + 3 + n % 2] = jnp.broadcast_to(above[n : n + 1, :], (8, LANES))
    species = coupling.shape[0]
    lane_wide = lax.broadcasted_iota(jnp.int32, (16, LANES), 1) // 16
    for q in range(species):
        table32[q] = table[q].astype(F32)

    def cell(position, carry):
        a, b, c = position // 4, (position // 2) % 2, position % 2
        for o in range(8):
            i, j, k = o // 4, (o // 2) % 2, o % 2
            kind = kind_row(kinds, a + i + 1, b + j + 1, c + k + 1)[:, 0:1]
            block = jnp.zeros((16, CELL), F32)
            for q in range(species):
                block = jnp.where(kind == q, table32[q, o * 16 : (o + 1) * 16, :], block)
            rows_out[position, o * 16 : (o + 1) * 16, :] = block.astype(BF16)
        return carry

    lax.fori_loop(0, 8, cell, 0)
    mix_out[...] = jnp.zeros_like(mix_out)
    along = lax.broadcasted_iota(jnp.int32, (16, LANES), 1) % 16
    repeat = jnp.where(along == lax.broadcasted_iota(jnp.int32, (16, LANES), 0), 1.0, 0.0).astype(F32)
    for q in range(species):
        wide[q] = jnp.dot(coupling[q], repeat, precision=HIGHEST, preferred_element_type=F32)

    def vertex(v, carry):
        kind = kind_row(kinds, v // 9 + 1, (v // 3) % 3 + 1, v % 3 + 1)
        block = jnp.zeros((16, LANES), F32)
        for q in range(species):
            block = jnp.where(kind == q, wide[q], block)
        block = jnp.where(lane_wide == v % 8, block, 0.0)
        mix_out[v // 8, pl.ds(pl.multiple_of((v % 8) * 16, 16), 16), :] = block
        return carry

    lax.fori_loop(0, 27, vertex, 0)


def first_tables(from_z, up_z, s50, table, coupling):
    species = coupling.shape[0]
    return pl.pallas_call(
        first_tables_kernel,
        out_shape=(shape((125, 8, LANES), F32), shape((8, 128, CELL), BF16), shape((4, LANES, LANES), F32)),
        in_specs=[VMEM] * 5,
        out_specs=(VMEM,) * 3,
        scratch_shapes=[pltpu.VMEM((species, 16, LANES), F32), pltpu.VMEM((species, 128, CELL), F32)],
        cost_estimate=cost(1e6, 3e6),
        compiler_params=SMALL,
        name="first_tables",
    )(from_z, up_z, s50, table, coupling)


def turn_kernel(table, after, out, wide):
    del after
    wide[...] = jnp.zeros_like(wide)
    for q in range(out.shape[0]):
        wide[:, 0:CELL] = table[q].astype(F32)
        out[q] = wide[...].T


def turn(table, after):
    return pl.pallas_call(
        turn_kernel,
        out_shape=shape((table.shape[0], 768, LANES), F32),
        in_specs=[VMEM, pl.BlockSpec(memory_space=pl.ANY)],
        out_specs=VMEM,
        scratch_shapes=[pltpu.VMEM((LANES, 768), F32)],
        cost_estimate=cost(1e6, 3e6),
        compiler_params=SMALL,
        name="turn",
    )(table, after)


def tables_kernel(kinds, table_t, after, columns_out, faces_out, edges_out, points_out, picked):
    del after
    species = table_t.shape[0]
    lane = lax.broadcasted_iota(jnp.int32, (1, LANES), 1) // 16

    def choose(values, lane_kind):
        total = jnp.where(lane_kind == 0, values[0], 0.0)
        for q in range(1, species):
            total = jnp.where(lane_kind == q, values[q], total)
        return total.astype(BF16)

    def cell(position, carry):
        a, b, c = position // 4, (position // 2) % 2, position % 2
        lane_kind = corner_kinds(kinds, a + 1, b + 1, c + 1, lane)
        columns_out[position] = choose([table_t[q, 0:CELL] for q in range(species)], lane_kind)
        return carry

    lax.fori_loop(0, 8, cell, 0)
    for axis in range(3):
        for s in range(2):
            near = 8 - 8 * s
            for q in range(species):
                if axis == 0:
                    picked[q, 0:81] = table_t[q, near * 81 : near * 81 + 81]
                elif axis == 1:
                    for x in range(9):
                        picked[q, x * 9 : x * 9 + 9] = table_t[q, x * 81 + near * 9 : x * 81 + near * 9 + 9]
                else:
                    picked[q, 0:81] = table_t[q, pl.ds(near, 81, stride=9)]

            def face(n, carry, axis=axis, s=s):
                spot = [n // 2 + 1, n % 2 + 1]
                spot.insert(axis, 3 * s)
                lane_kind = corner_kinds(kinds, *spot, lane)
                faces_out[axis * 8 + s * 4 + n] = choose([picked[q, 0:81] for q in range(species)], lane_kind)
                return carry

            lax.fori_loop(0, 4, face, 0)
    for axis in range(3):
        for s in range(2):
            for t in range(2):
                first, second = 8 - 8 * s, 8 - 8 * t
                for u in range(2):
                    spot = [3 * s, 3 * t]
                    spot.insert(axis, u + 1)
                    start, stride = ((first * 9 + second, 81), (first * 81 + second, 9), (first * 81 + second * 9, 1))[axis]
                    lane_kind = corner_kinds(kinds, *spot, lane)
                    place = slice(start, start + 9) if stride == 1 else pl.ds(start, 9, stride=stride)
                    edges_out[axis * 8 + s * 4 + t * 2 + u, 0:9] = choose([table_t[q, place] for q in range(species)], lane_kind)
    for n in range(8):
        s, t, w = n // 4, (n // 2) % 2, n % 2
        at = (8 - 8 * s) * 81 + (8 - 8 * t) * 9 + 8 - 8 * w
        lane_kind = corner_kinds(kinds, 3 * s, 3 * t, 3 * w, lane)
        points_out[n, 0:1] = choose([table_t[q, at : at + 1] for q in range(species)], lane_kind)


def make_tables(kinds, table_t, after):
    species = table_t.shape[0]
    return pl.pallas_call(
        tables_kernel,
        out_shape=(
            shape((8, CELL, LANES), BF16),
            shape((24, 81, LANES), BF16),
            shape((24, 9, LANES), BF16),
            shape((8, 1, LANES), BF16),
        ),
        in_specs=[VMEM, VMEM, pl.BlockSpec(memory_space=pl.ANY)],
        out_specs=(VMEM,) * 4,
        scratch_shapes=[pltpu.VMEM((species, 88, LANES), F32)],
        cost_estimate=cost(1e7, 6e6),
        compiler_params=SMALL,
        name="tables",
    )(kinds, table_t, after)


def first_x_kernel(psi, own, message, up):
    message[0:256, :] = psi[...].reshape(256, LANES)
    species = [jnp.full((1, LANES), own[n].astype(F32), F32) for n in range(8)]
    blank = jnp.zeros((8, LANES), F32)
    message[256:272, :] = jnp.concatenate(species + [blank], axis=0).astype(BF16)
    up[...] = jnp.concatenate(species[4:] + [blank[0:4]], axis=0)


def first_x(psi, own):
    return pl.pallas_call(
        first_x_kernel,
        grid=(1,),
        out_shape=(shape((272, LANES), BF16), shape((8, LANES), F32)),
        in_specs=[pl.BlockSpec((1, 16, 16, LANES), lambda n: (0, 0, 0, 0)), SMEM],
        out_specs=(pl.BlockSpec((272, LANES), lambda n: (0, 0)), pl.BlockSpec((8, LANES), lambda n: (0, 0))),
        cost_estimate=cost(1e5, 2e5),
        compiler_params=SMALL,
        name="first_x",
    )(pltpu.with_memory_space_constraint(psi, pltpu.HBM), own)


def first_rows_kernel(psi, rows_y, rows_z, wide, narrow):
    for x in range(16):
        rows_y[x * 16 : x * 16 + 16, :] = psi[x, 0]
    wide[...] = psi[...].reshape(4096, LANES).astype(F32)
    rows = wide[pl.ds(0, 256, stride=16), :]
    narrow[...] = jnp.zeros_like(narrow)
    for x in range(16):
        narrow[x * SIDE : x * SIDE + 16, :] = rows[x * 16 : x * 16 + 16]
    rows_z[...] = narrow[...]


def first_rows(psi):
    return pl.pallas_call(
        first_rows_kernel,
        out_shape=(shape((256, LANES), BF16), shape((FACE, LANES), F32)),
        in_specs=[VMEM],
        out_specs=(VMEM, VMEM),
        scratch_shapes=[pltpu.VMEM((4096, LANES), F32), pltpu.VMEM((FACE, LANES), F32)],
        cost_estimate=cost(1e6, 1.2e6),
        compiler_params=SMALL,
        name="first_rows",
    )(psi)


def first_y_kernel(rows_y, from_x, up_x, own, message, up, s20):
    message[0:256, :] = rows_y[...]
    message[256:272, :] = from_x[0:16, :]
    s20[0:4, :] = up_x[0:4, :]
    for n in range(8):
        s20[4 + n : 5 + n, :] = jnp.full((1, LANES), own[n].astype(F32), F32)
    s20[12:20, :] = from_x[256:272, :].astype(F32)[0:8]
    s20[20:32, :] = jnp.zeros((12, LANES), F32)
    message[272:304, :] = s20[...].astype(BF16)
    for x in range(5):
        up[x * 2 : x * 2 + 2, :] = s20[x * 4 + 2 : x * 4 + 4, :]
    up[10:16, :] = jnp.zeros((6, LANES), F32)


def first_y(rows_y, from_x, up_x, own):
    return pl.pallas_call(
        first_y_kernel,
        out_shape=(shape((304, LANES), BF16), shape((16, LANES), F32), shape((32, LANES), F32)),
        in_specs=[VMEM, VMEM, VMEM, SMEM],
        out_specs=(VMEM,) * 3,
        cost_estimate=cost(1e5, 2e5),
        compiler_params=SMALL,
        name="first_y",
    )(rows_y, from_x, up_x, own)


def first_z_kernel(rows, from_x, from_y, up_y, s20, message, up, s50, wide_x, wide_y, face):
    wide_x[...] = from_x[0:256, :].astype(F32)
    wide_y[...] = from_y[...].astype(F32)
    face[...] = rows[...]
    face[16 * SIDE : 16 * SIDE + 16, :] = wide_x[pl.ds(0, 16, stride=16), :]
    face[pl.ds(16, SIDE, stride=SIDE), :] = wide_y[pl.ds(0, SIDE, stride=16), :]
    message[0:FACE, :] = face[...].astype(BF16)
    for x in range(5):
        s50[x * 10 : x * 10 + 2, :] = up_y[x * 2 : x * 2 + 2, :]
        s50[x * 10 + 2 : x * 10 + 6, :] = s20[x * 4 : x * 4 + 4, :]
        s50[x * 10 + 6 : x * 10 + 10, :] = wide_y[272 + x * 4 : 272 + x * 4 + 4, :]
    s50[50:64, :] = jnp.zeros((14, LANES), F32)
    message[FACE : FACE + 64, :] = s50[...].astype(BF16)
    up[0:25, :] = s50[pl.ds(1, 25, stride=2), :]
    up[25:32, :] = jnp.zeros((7, LANES), F32)


def first_z(rows, from_x, from_y, up_y, s20):
    return pl.pallas_call(
        first_z_kernel,
        out_shape=(shape((FACE + 64, LANES), BF16), shape((32, LANES), F32), shape((64, LANES), F32)),
        in_specs=[VMEM] * 5,
        out_specs=(VMEM,) * 3,
        scratch_shapes=[
            pltpu.VMEM((256, LANES), F32),
            pltpu.VMEM((304, LANES), F32),
            pltpu.VMEM((FACE, LANES), F32),
        ],
        cost_estimate=cost(1e5, 4e5),
        compiler_params=SMALL,
        name="first_z",
    )(rows, from_x, from_y, up_y, s20)


def begin_kernel(psi, from_x, from_y, from_z, field_out, field, wide):
    field[...] = jnp.zeros_like(field)

    def slab(x, carry):
        for y in range(16):
            start = pl.multiple_of(x * SLAB + y * ZPAD, 8)
            field[pl.ds(start, 16), :] = psi[x, y].astype(F32)
        return carry

    lax.fori_loop(0, 16, slab, 0)
    for y in range(16):
        at = 16 * SLAB + y * ZPAD
        field[at : at + 16, :] = from_x[y * 16 : y * 16 + 16, :].astype(F32)
    for x in range(SIDE):
        at = x * SLAB + 16 * ZPAD
        field[at : at + 16, :] = from_y[x * 16 : x * 16 + 16, :].astype(F32)
    wide[...] = from_z[0:FACE, :].astype(F32)
    field[pl.ds(16, PLANE, stride=ZPAD), :] = wide[0:PLANE, :]

    def chunk(n, carry):
        spot = pl.ds(pl.multiple_of(n * CHUNK, 16), CHUNK)
        field_out[spot, :] = field[spot, :].astype(BF16)
        return carry

    lax.fori_loop(0, ROWS // CHUNK, chunk, 0)


def begin(psi, from_x, from_y, from_z):
    return pl.pallas_call(
        begin_kernel,
        out_shape=shape((ROWS, LANES), BF16),
        in_specs=[VMEM] * 4,
        out_specs=VMEM,
        scratch_shapes=[pltpu.VMEM((ROWS, LANES), F32), pltpu.VMEM((FACE, LANES), F32)],
        cost_estimate=cost(1e7, 4e6),
        compiler_params=LARGE,
        name="begin",
    )(psi, from_x, from_y, from_z)


HAM_ROWS = 128


def by_cell_kernel(source, out, wide):
    def piece(n, carry):
        for half in range(2):
            spot = pl.ds(pl.multiple_of(n * 32 + half * 16, 16), 16)
            for start in range(0, CELL, LANES):
                width = min(LANES, CELL - start)
                block = wide.at[half, start : start + LANES]
                block[:, 0:width] = source[spot, :, start : start + width].astype(F32).reshape(128, width)
        for half in range(2):
            spot = pl.ds(pl.multiple_of(n * 32 + half * 16, 16), 16)
            for start in range(0, CELL, LANES):
                width = min(LANES, CELL - start)
                block = wide.at[half, start : start + LANES]
                for c in range(8):
                    found = block[pl.ds(c, 16, stride=8), :]
                    out[c, spot, start : start + width] = found[:, 0:width].astype(BF16)
        return carry

    lax.fori_loop(0, HAM_ROWS // 32, piece, 0)


def by_cell(ham):
    return pl.pallas_call(
        by_cell_kernel,
        grid=(pl.cdiv(CELL, HAM_ROWS),),
        out_shape=shape((8, CELL, CELL), BF16),
        in_specs=[pl.BlockSpec((HAM_ROWS, 8, CELL), lambda n: (n, 0, 0))],
        out_specs=pl.BlockSpec((8, HAM_ROWS, CELL), lambda n: (0, n, 0)),
        scratch_shapes=[pltpu.VMEM((2, 768, LANES), F32)],
        cost_estimate=cost(1e7, 1.8e7),
        compiler_params=LARGE,
        name="by_cell",
    )(pltpu.with_memory_space_constraint(jnp.transpose(ham, (1, 0, 2)), pltpu.HBM))


MESSAGE_Y = FACE + 288
MESSAGE_Z = FACE + 480
MESSAGE_X = FACE + 800


def send(odd, low, high, first, second, rows):
    first[rows, :] = jnp.where(odd, low, high).astype(BF16)
    second[rows, :] = jnp.where(odd, high, low).astype(BF16)


def receive(odd, first, second, rows):
    one, two = first[rows, :].astype(F32), second[rows, :].astype(F32)
    return jnp.where(odd, one, two), jnp.where(odd, two, one)


def apply_kernel(odd, now, ham, rows, mix, terms, send_one, send_two, zface, xface, weights, field, cell32, total, yface):
    def chunk(n, carry):
        spot = pl.ds(pl.multiple_of(n * CHUNK, 16), CHUNK)
        field[spot, :] = now[spot, :].astype(F32)
        return carry

    lax.fori_loop(0, ROWS // CHUNK, chunk, 0)
    for ref in (total, xface, yface, zface):
        ref[...] = jnp.zeros_like(ref)

    def cell(position, carry):
        a, b, c = position // 4, (position // 2) % 2, position % 2
        base = cell_base(a, b, c)
        for x in range(9):
            for y in range(9):
                at = (x * 9 + y) * 9
                cell32[at : at + 9, :] = field[pl.ds(line_start(base, x, y), 9), :]
        values = cell32[0:CELL, :].astype(BF16)
        part = jnp.dot(rows[position], values, preferred_element_type=F32)
        for o in range(8):
            i, j, k = o // 4, (o // 2) % 2, o % 2
            vertex = (a + i) * 9 + (b + j) * 3 + c + k
            total[pl.ds(pl.multiple_of(vertex * 16, 16), 16), :] += part[o * 16 : (o + 1) * 16]
        result = jnp.dot(ham[position], values, preferred_element_type=F32)
        terms[position] = result
        cell32[0:CELL, :] = result
        target = xface.at[pl.ds(pl.multiple_of(a * FACE + b * 136 + c * 8, 8), 152)]
        source = cell32.at[pl.ds(pl.multiple_of(a * 648, 8), 88)]
        for y in range(9):
            target[y * SIDE : y * SIDE + 9, :] += source[y * 9 : y * 9 + 9, :]
        target = yface.at[pl.ds(pl.multiple_of(b * FACE + a * 136 + c * 8, 8), 152)]
        source = cell32.at[pl.ds(pl.multiple_of(b * 72, 8), 664)]
        for x in range(9):
            target[x * SIDE : x * SIDE + 9, :] += source[x * 81 : x * 81 + 9, :]
        target = zface.at[pl.ds(pl.multiple_of(c * FACE + a * 136 + b * 8, 8), 152)]
        source = cell32.at[pl.ds(pl.multiple_of(c * 8, 8), 728)]
        for x in range(9):
            target[x * SIDE : x * SIDE + 9, :] += source[pl.ds(x * 81, 9, stride=9), :]
        return carry

    lax.fori_loop(0, 8, cell, 0)
    turn = odd[1] == 1
    for g in range(4):
        spot = slice(g * 128, g * 128 + 128)
        total[spot, :] = jnp.dot(mix[g], total[spot, :], precision=HIGHEST, preferred_element_type=F32)
    weights[...] = total[0:432, :]
    send(turn, yface[0:FACE, :], yface[FACE : 2 * FACE, :], send_one, send_two, slice(0, FACE))
    for p in range(2):
        for x in range(3):
            at = FACE + (p * 3 + x) * 48
            down = total[x * 144 + p * 48 : x * 144 + p * 48 + 48, :]
            up = total[x * 144 + (p + 1) * 48 : x * 144 + (p + 1) * 48 + 48, :]
            send(turn, down, up, send_one, send_two, slice(at, at + 48))


def apply_cells(odd, now, ham, rows, mix):
    faces = shape((2 * FACE, LANES), F32)
    message = shape((MESSAGE_Y, LANES), BF16)
    return pl.pallas_call(
        apply_kernel,
        out_shape=(shape((8, CELL, LANES), F32), message, message, faces, faces, shape((432, LANES), F32)),
        in_specs=[SMEM] + [VMEM] * 4,
        out_specs=(VMEM,) * 6,
        scratch_shapes=[
            pltpu.VMEM((ROWS, LANES), F32),
            pltpu.VMEM((736, LANES), F32),
            pltpu.VMEM((512, LANES), F32),
            pltpu.VMEM((2 * FACE, LANES), F32),
        ],
        cost_estimate=cost(1.3e9, 1.6e7),
        compiler_params=LARGE,
        name="apply_cells",
    )(odd, now, ham, rows, mix)


def assemble_kernel(first, terms, now, *refs):
    before = None if first else refs[0]
    field = refs[-1]
    scale = 1.0 if first else 2.0

    def chunk(n, carry):
        spot = pl.ds(pl.multiple_of(n * CHUNK, 16), CHUNK)
        value = -scale * now[spot, :].astype(F32)
        if before is not None:
            value = value - before[spot, :].astype(F32)
        field[spot, :] = value
        return carry

    lax.fori_loop(0, ROWS // CHUNK, chunk, 0)

    def cell(position, carry):
        a, b, c = position // 4, (position // 2) % 2, position % 2
        base = cell_base(a, b, c)
        for x in range(9):
            for y in range(9):
                at = (x * 9 + y) * 9
                field[pl.ds(line_start(base, x, y), 9), :] += scale * terms[position, at : at + 9, :]
        return carry

    lax.fori_loop(0, 8, cell, 0)


def assemble(terms, now, before):
    args = [terms, now] + ([] if before is None else [before])
    return pl.pallas_call(
        functools.partial(assemble_kernel, before is None),
        out_shape=shape((ROWS, LANES), F32),
        in_specs=[VMEM] * len(args),
        out_specs=VMEM,
        cost_estimate=cost(1e7, 1.2e7),
        compiler_params=SMALL,
        name="assemble",
    )(*args)


def after_y_kernel(odd, one, two, zface, xface, weights, send_one, send_two, xface_out, weights_out, low, high, face_low, face_high):
    low[...], high[...] = receive(odd[1] == 1, one, two, slice(0, FACE))
    turn = odd[2] == 1
    last = 16 * SIDE
    for face, start, column in ((face_low, 0, 0), (face_high, FACE, 16)):
        face[...] = zface[start : start + FACE, :]
        face[pl.ds(0, SIDE, stride=SIDE), :] += low[pl.ds(column, SIDE, stride=SIDE), :]
        face[pl.ds(16, SIDE, stride=SIDE), :] += high[pl.ds(column, SIDE, stride=SIDE), :]
    send(turn, face_low[...], face_high[...], send_one, send_two, slice(0, FACE))
    xface_out[...] = xface[...]
    for start, row in ((0, 0), (FACE, last)):
        xface_out[start : start + SIDE, :] += low[row : row + SIDE, :]
        xface_out[start + last : start + last + SIDE, :] += high[row : row + SIDE, :]
    for x in range(3):
        weights_out[x * 240 + 48 : x * 240 + 192, :] = weights[x * 144 : x * 144 + 144, :]
        for p in range(2):
            at = FACE + (p * 3 + x) * 48
            below, above = receive(odd[1] == 1, one, two, slice(at, at + 48))
            if p == 0:
                weights_out[x * 240 : x * 240 + 48, :] = below
                weights_out[x * 240 + 144 : x * 240 + 192, :] += above
            else:
                weights_out[x * 240 + 48 : x * 240 + 96, :] += below
                weights_out[x * 240 + 192 : x * 240 + 240, :] = above
    for p in range(2):
        for n in range(15):
            at = FACE + (p * 15 + n) * 16
            down = weights_out[n * 48 + p * 16 : n * 48 + p * 16 + 16, :]
            up = weights_out[n * 48 + p * 16 + 16 : n * 48 + p * 16 + 32, :]
            send(turn, down, up, send_one, send_two, slice(at, at + 16))


def after_y(odd, one, two, zface, xface, weights):
    message = shape((MESSAGE_Z, LANES), BF16)
    return pl.pallas_call(
        after_y_kernel,
        out_shape=(message, message, shape((2 * FACE, LANES), F32), shape((720, LANES), F32)),
        in_specs=[SMEM] + [VMEM] * 5,
        out_specs=(VMEM,) * 4,
        scratch_shapes=[pltpu.VMEM((FACE, LANES), F32)] * 4,
        cost_estimate=cost(1e5, 2e6),
        compiler_params=SMALL,
        name="after_y",
    )(odd, one, two, zface, xface, weights)


def after_z_kernel(odd, one, two, xface, weights, send_one, send_two, weights_out, low, high, face_low, face_high):
    low[...], high[...] = receive(odd[2] == 1, one, two, slice(0, FACE))
    turn = odd[0] == 1
    for face, start, row in ((face_low, 0, 0), (face_high, FACE, 16 * SIDE)):
        face[...] = xface[start : start + FACE, :]
        face[pl.ds(0, SIDE, stride=SIDE), :] += low[row : row + SIDE, :]
        face[pl.ds(16, SIDE, stride=SIDE), :] += high[row : row + SIDE, :]
    send(turn, face_low[...], face_high[...], send_one, send_two, slice(0, FACE))
    for n in range(15):
        weights_out[n * 80 + 16 : n * 80 + 64, :] = weights[n * 48 : n * 48 + 48, :]
        for p in range(2):
            at = FACE + (p * 15 + n) * 16
            below, above = receive(odd[2] == 1, one, two, slice(at, at + 16))
            if p == 0:
                weights_out[n * 80 : n * 80 + 16, :] = below
                weights_out[n * 80 + 48 : n * 80 + 64, :] += above
            else:
                weights_out[n * 80 + 16 : n * 80 + 32, :] += below
                weights_out[n * 80 + 64 : n * 80 + 80, :] = above
    for p in range(2):
        at = FACE + p * 400
        down, up = weights_out[p * 400 : p * 400 + 400, :], weights_out[p * 400 + 400 : p * 400 + 800, :]
        send(turn, down, up, send_one, send_two, slice(at, at + 400))


def after_z(odd, one, two, xface, weights):
    message = shape((MESSAGE_X, LANES), BF16)
    return pl.pallas_call(
        after_z_kernel,
        out_shape=(message, message, shape((1200, LANES), F32)),
        in_specs=[SMEM] + [VMEM] * 4,
        out_specs=(VMEM,) * 3,
        scratch_shapes=[pltpu.VMEM((FACE, LANES), F32)] * 4,
        cost_estimate=cost(1e5, 2e6),
        compiler_params=SMALL,
        name="after_z",
    )(odd, one, two, xface, weights)


def corner_weights(weights, a, b, c):
    pieces = []
    for o in range(8):
        i, j, k = o // 4, (o // 2) % 2, o % 2
        vertex = ((a + i) * 5 + b + j) * 5 + c + k
        pieces.append(weights[pl.ds(pl.multiple_of(vertex * 16, 16), 16), :])
    return jnp.concatenate(pieces, axis=0)


def advance_kernel(first, last, odd, start_field, y1, y2, z1, z2, x1, x2, w75, columns, faces, edges, points, out, *refs):
    del start_field
    parts = refs[: len(refs) - 6]
    field, cell32, weights, xs, ys, zs = refs[len(refs) - 6 :]
    scale = 1.0 if first else 2.0
    for ref, one, two, axis in ((xs, x1, x2, 0), (ys, y1, y2, 1), (zs, z1, z2, 2)):
        low, high = receive(odd[axis] == 1, one, two, slice(0, FACE))
        ref[0:FACE, :] = low
        ref[FACE : 2 * FACE, :] = high
    for p in range(2):
        at = FACE + p * 400
        below, above = receive(odd[0] == 1, x1, x2, slice(at, at + 400))
        if p == 0:
            weights[0:400, :] = below.astype(BF16)
            weights[1200:1600, :] = (w75[800:1200, :] + above).astype(BF16)
        else:
            weights[400:800, :] = (w75[0:400, :] + below).astype(BF16)
            weights[1600:2000, :] = above.astype(BF16)
    weights[800:1200, :] = w75[400:800, :].astype(BF16)

    def cell(position, carry):
        a, b, c = position // 4, (position // 2) % 2, position % 2
        corner = corner_weights(weights, a + 1, b + 1, c + 1)
        cell32[0:CELL, :] = scale * jnp.dot(columns[position], corner, preferred_element_type=F32)
        base = cell_base(a, b, c)
        for x in range(9):
            for y in range(9):
                at = (x * 9 + y) * 9
                field[pl.ds(line_start(base, x, y), 9), :] += cell32[at : at + 9, :]
        return carry

    lax.fori_loop(0, 8, cell, 0)

    for axis, ref in enumerate((xs, ys, zs)):

        def face(s, carry, axis=axis, ref=ref):
            for n in range(4):
                spot = [n // 2 + 1, n % 2 + 1]
                spot.insert(axis, 3 * s)
                cell32[n * 88 : n * 88 + 81, :] = jnp.dot(
                    faces[axis * 8 + s * 4 + n], corner_weights(weights, *spot), preferred_element_type=F32
                )
            for n in range(4):
                view = ref.at[pl.ds(pl.multiple_of(s * FACE + (n // 2) * 136 + (n % 2) * 8, 8), 152)]
                for row in range(9):
                    at = n * 88 + row * 9
                    view[row * SIDE : row * SIDE + 9, :] += cell32[at : at + 9, :]
            return carry

        lax.fori_loop(0, 2, face, 0)

    for axis in range(3):

        def edge(s, carry, axis=axis):
            terms = []
            for n in range(4):
                spot = [3 * s, 3 * (n // 2)]
                spot.insert(axis, n % 2 + 1)
                terms.append(
                    jnp.dot(edges[axis * 8 + s * 4 + n], corner_weights(weights, *spot), preferred_element_type=F32)
                )
            for n, term in enumerate(terms):
                t, u = n // 2, n % 2
                if axis == 2:
                    view = xs.at[pl.ds(pl.multiple_of(s * FACE + t * 272 + u * 8, 8), 16)]
                    view[0:9, :] += term
                else:
                    ref = xs if axis == 1 else ys
                    view = ref.at[pl.ds(pl.multiple_of(s * FACE + u * 136 + t * 16, 8), 152)]
                    view[pl.ds(0, 9, stride=SIDE), :] += term
            return carry

        lax.fori_loop(0, 2, edge, 0)

    def point(s, carry):
        terms = []
        for n in range(4):
            corner = corner_weights(weights, 3 * s, 3 * (n // 2), 3 * (n % 2))
            terms.append(jnp.dot(points[s * 4 + n], corner, preferred_element_type=F32))
        for n, term in enumerate(terms):
            view = xs.at[pl.ds(pl.multiple_of(s * FACE + (n // 2) * 272 + (n % 2) * 16, 8), 8)]
            view[0:1, :] += term
        return carry

    lax.fori_loop(0, 2, point, 0)

    for s in range(2):
        for y in range(SIDE):
            at = s * 16 * SLAB + y * ZPAD
            field[at : at + SIDE, :] += scale * xs[s * FACE + y * SIDE : s * FACE + (y + 1) * SIDE, :]
        for x in range(SIDE):
            at = s * 16 * ZPAD + x * SLAB
            field[at : at + SIDE, :] += scale * ys[s * FACE + x * SIDE : s * FACE + (x + 1) * SIDE, :]
        field[pl.ds(s * 16, PLANE, stride=ZPAD), :] += scale * zs[s * FACE : s * FACE + PLANE, :]

    if last:

        def slab(x, carry):
            for y in range(16):
                start = pl.multiple_of(x * SLAB + y * ZPAD, 8)
                out[x, y] = field[pl.ds(start, 16), :].astype(BF16)
            return carry

        lax.fori_loop(0, 16, slab, 0)
        for offset, part in enumerate(parts):
            quarter = (odd[3] + offset) % 4
            part[...] = out[pl.ds(quarter * 4, 4)].reshape(1024, LANES)
    else:

        def chunk(n, carry):
            spot = pl.ds(pl.multiple_of(n * CHUNK, 16), CHUNK)
            out[spot, :] = field[spot, :].astype(BF16)
            return carry

        lax.fori_loop(0, ROWS // CHUNK, chunk, 0)


def advance(odd, field, messages, w75, tables, first, last):
    args = [odd, field, *messages, w75, *tables]
    if last:
        outs = [shape((16, 16, 16, LANES), BF16)] + [shape((1024, LANES), BF16)] * 4
    else:
        outs = [shape((ROWS, LANES), BF16)]
    outs.append(shape((ROWS, LANES), F32))
    return pl.pallas_call(
        functools.partial(advance_kernel, first, last),
        out_shape=tuple(outs),
        in_specs=[SMEM] + [VMEM] * (len(args) - 1),
        out_specs=(VMEM,) * len(outs),
        input_output_aliases={1: len(outs) - 1},
        scratch_shapes=[pltpu.VMEM((736, LANES), F32), pltpu.VMEM((2000, LANES), BF16)]
        + [pltpu.VMEM((2 * FACE, LANES), F32)] * 3,
        cost_estimate=cost(3e8, 1.2e7),
        compiler_params=LARGE,
        name="advance",
    )(*args)[:-1]


def gram_kernel(x0, x1, x2, x3, own, m1, m2, m3):
    blocks = [x0[...], x1[...], x2[...], x3[...]]
    for row, left in enumerate(blocks):
        turned = left.T
        for column, out in ((0, own), (3, m1), (2, m2), (1, m3)):
            part = jnp.dot(turned, blocks[column], preferred_element_type=F32)
            out[row * 128 : row * 128 + 128, :] = part.astype(out.dtype)


def gram(blocks):
    return pl.pallas_call(
        gram_kernel,
        out_shape=(shape((512, LANES), F32),) + (shape((512, LANES), BF16),) * 3,
        in_specs=[VMEM] * 4,
        out_specs=(VMEM,) * 4,
        cost_estimate=cost(6e8, 2e6),
        compiler_params=LARGE,
        name="gram",
    )(*blocks)


def collect_kernel(band, own, m1, m2, m3, out):
    for row in range(4):
        total = own[row * 128 : row * 128 + 128, :]
        for offset, ref in ((1, m1), (2, m2), (3, m3)):
            source = (row - offset) % 4
            total = total + ref[source * 128 : source * 128 + 128, :].astype(F32)
        place = (band[0] + 4 - row) % 4
        out[pl.ds(place * 16, 16)] = total.reshape(16, 8, LANES).astype(BF16)


def collect(band, own, received):
    return pl.pallas_call(
        collect_kernel,
        out_shape=shape((64, 8, LANES), BF16),
        in_specs=[SMEM] + [VMEM] * 4,
        out_specs=VMEM,
        cost_estimate=cost(1e6, 1e6),
        compiler_params=SMALL,
        name="collect",
    )(band, own, *received)


def local(psi, cell_ham, proj_table, coupling, atom_kind):
    devices = lax.axis_size("cells")
    side = cube_root(devices)
    offsets = (1, side, side * side)
    block = lax.axis_index("cells")
    band = lax.axis_index("bands")
    odd = jnp.stack([(block // offset) % 2 for offset in offsets] + [band]).astype(jnp.int32)

    def upward(x, axis):
        return shifted(x, "cells", offsets[axis])

    def downward(x, axis):
        return shifted(x, "cells", -offsets[axis])

    def swap(messages, axis):
        offset = offsets[axis]
        arrived = []
        for start, message in enumerate(messages):
            pairs = []
            for i in range(devices):
                forward = (i // offset) % 2 == start
                pairs.append((i, (i + offset) % devices if forward else (i - offset) % devices))
            arrived.append(lax.ppermute(message, "cells", pairs))
        return arrived

    own = atom_kind.reshape(8)
    message, up = first_x(psi, own)
    from_x, up_x = downward(message, 0), upward(up, 0)
    rows_y, rows_z = first_rows(psi)
    message, up, s20 = first_y(rows_y, from_x, up_x, own)
    from_y, up_y = downward(message, 1), upward(up, 1)
    message, up, s50 = first_z(rows_z, from_x, from_y, up_y, s20)
    from_z, up_z = downward(message, 2), upward(up, 2)
    ham = by_cell(cell_ham)
    table = proj_table.reshape(4, 128, CELL)
    kinds, rows, mix = first_tables(from_z, up_z, s50, table, coupling)

    def step(now, before, last, tables):
        terms, one, two, zface, xface, weights = apply_cells(odd, now, ham, rows, mix)
        ys = swap((one, two), 1)
        if tables is None:
            tables = make_tables(kinds, turn(table, weights), weights)
        field = assemble(terms, now, before)
        one, two, xface, weights = after_y(odd, *ys, zface, xface, weights)
        zs = swap((one, two), 2)
        one, two, weights = after_z(odd, *zs, xface, weights)
        xs = swap((one, two), 0)
        return tables, advance(odd, field, (*ys, *zs, *xs), weights, tables, before is None, last)

    y0 = begin(psi, from_x, from_y, from_z)
    tables, (y1,) = step(y0, None, False, None)
    tables, (y2,) = step(y1, y0, False, tables)
    tables, (filtered, *blocks) = step(y2, y1, True, tables)

    blocks = [block if n == 0 else shifted(block, "bands", n) for n, block in enumerate(blocks)]
    own, *messages = gram(blocks)
    messages = [shifted(message, "bands", n + 1) for n, message in enumerate(messages)]
    terms = collect(band.astype(jnp.int32).reshape(1), own, messages)
    terms = lax.all_to_all(terms, "cells", 0, 0)
    inverse_count = 1.0 / (4096 * devices)
    correlation = jnp.sum(terms.astype(F32), axis=0) * inverse_count
    return filtered, correlation


def solution(mesh):
    in_specs = (
        P("cells", None, None, "bands"),
        P("cells", None, None),
        P(),
        P(),
        P("cells", None, None),
    )
    out_specs = (P("cells", None, None, "bands"), P("cells", "bands"))
    return jax.shard_map(local, mesh=mesh, in_specs=in_specs, out_specs=out_specs, check_vma=False)
```

```python
import functools

import jax
import jax.numpy as jnp
from jax import lax
from jax.experimental import pallas as pl
from jax.experimental.pallas import tpu as pltpu
from jax.sharding import PartitionSpec as P


F32 = jnp.float32
BF16 = jnp.bfloat16
HIGHEST = lax.Precision.HIGHEST

SIDE = 17
ZPAD = 24
SLAB = SIDE * ZPAD
ROWS = 6944
CHUNK = 496
FACE = 304
PLANE = SIDE * SIDE
CELL = 729
LANES = 128


def shifted(x, axis, by):
    devices = lax.axis_size(axis)
    return lax.ppermute(x, axis, [(i, (i + by) % devices) for i in range(devices)])


def cube_root(amount):
    result = 1
    while (result + 1) ** 3 <= amount:
        result = result + 1
    return result


def cost(flops, nbytes):
    return pl.CostEstimate(flops=int(flops), bytes_accessed=int(nbytes), transcendentals=0)


def shape(dims, dtype):
    return jax.ShapeDtypeStruct(dims, dtype)


VMEM = pl.BlockSpec(memory_space=pltpu.VMEM)
LARGE = pltpu.CompilerParams(vmem_limit_bytes=10 * 2**20)
SMALL = pltpu.CompilerParams(vmem_limit_bytes=6 * 2**20)
SMEM = pl.BlockSpec(memory_space=pltpu.SMEM)


def cell_base(a, b, c):
    return a * (8 * SLAB) + b * (8 * ZPAD) + c * 8


def line_start(base, x, y):
    return pl.multiple_of(base + (x * SLAB + y * ZPAD), 8)


def kind_row(kinds, a, b, c):
    return kinds[(a * 5 + b) * 5 + c][0:1, :]


def corner_kinds(kinds, a, b, c, lane):
    found = jnp.full((1, LANES), -1.0, F32)
    for o in range(8):
        i, j, k = o // 4, (o // 2) % 2, o % 2
        found = jnp.where(lane == o, kind_row(kinds, a + i, b + j, c + k), found)
    return found


def first_tables_kernel(from_z, up_z, s50, table, coupling, kinds, rows_out, mix_out, wide, table32):
    for n in range(25):
        kinds[n * 5] = jnp.broadcast_to(up_z[n : n + 1, :], (8, LANES))
        for k in range(2):
            at = n * 2 + k
            kinds[n * 5 + 1 + k] = jnp.broadcast_to(s50[at : at + 1, :], (8, LANES))
    above = from_z[FACE : FACE + 64, :].astype(F32)
    for n in range(50):
        kinds[(n // 2) * 5 + 3 + n % 2] = jnp.broadcast_to(above[n : n + 1, :], (8, LANES))
    species = coupling.shape[0]
    lane_wide = lax.broadcasted_iota(jnp.int32, (16, LANES), 1) // 16
    for q in range(species):
        table32[q] = table[q].astype(F32)

    def cell(position, carry):
        a, b, c = position // 4, (position // 2) % 2, position % 2
        for o in range(8):
            i, j, k = o // 4, (o // 2) % 2, o % 2
            kind = kind_row(kinds, a + i + 1, b + j + 1, c + k + 1)[:, 0:1]
            block = jnp.zeros((16, CELL), F32)
            for q in range(species):
                block = jnp.where(kind == q, table32[q, o * 16 : (o + 1) * 16, :], block)
            rows_out[position, o * 16 : (o + 1) * 16, :] = block.astype(BF16)
        return carry

    lax.fori_loop(0, 8, cell, 0)
    mix_out[...] = jnp.zeros_like(mix_out)
    along = lax.broadcasted_iota(jnp.int32, (16, LANES), 1) % 16
    repeat = jnp.where(along == lax.broadcasted_iota(jnp.int32, (16, LANES), 0), 1.0, 0.0).astype(F32)
    for q in range(species):
        wide[q] = jnp.dot(coupling[q], repeat, precision=HIGHEST, preferred_element_type=F32)

    def vertex(v, carry):
        kind = kind_row(kinds, v // 9 + 1, (v // 3) % 3 + 1, v % 3 + 1)
        block = jnp.zeros((16, LANES), F32)
        for q in range(species):
            block = jnp.where(kind == q, wide[q], block)
        block = jnp.where(lane_wide == v % 8, block, 0.0)
        mix_out[v // 8, pl.ds(pl.multiple_of((v % 8) * 16, 16), 16), :] = block
        return carry

    lax.fori_loop(0, 27, vertex, 0)


def first_tables(from_z, up_z, s50, table, coupling):
    species = coupling.shape[0]
    return pl.pallas_call(
        first_tables_kernel,
        out_shape=(shape((125, 8, LANES), F32), shape((8, 128, CELL), BF16), shape((4, LANES, LANES), F32)),
        in_specs=[VMEM] * 5,
        out_specs=(VMEM,) * 3,
        scratch_shapes=[pltpu.VMEM((species, 16, LANES), F32), pltpu.VMEM((species, 128, CELL), F32)],
        cost_estimate=cost(1e6, 3e6),
        compiler_params=SMALL,
        name="first_tables",
    )(from_z, up_z, s50, table, coupling)


def turn_kernel(table, after, out, wide):
    del after
    wide[...] = jnp.zeros_like(wide)
    for q in range(out.shape[0]):
        wide[:, 0:CELL] = table[q].astype(F32)
        out[q] = wide[...].T


def turn(table, after):
    return pl.pallas_call(
        turn_kernel,
        out_shape=shape((table.shape[0], 768, LANES), F32),
        in_specs=[VMEM, pl.BlockSpec(memory_space=pl.ANY)],
        out_specs=VMEM,
        scratch_shapes=[pltpu.VMEM((LANES, 768), F32)],
        cost_estimate=cost(1e6, 3e6),
        compiler_params=SMALL,
        name="turn",
    )(table, after)


def tables_kernel(kinds, table_t, after, columns_out, faces_out, edges_out, points_out, picked):
    del after
    species = table_t.shape[0]
    lane = lax.broadcasted_iota(jnp.int32, (1, LANES), 1) // 16

    def choose(values, lane_kind):
        total = jnp.where(lane_kind == 0, values[0], 0.0)
        for q in range(1, species):
            total = jnp.where(lane_kind == q, values[q], total)
        return total.astype(BF16)

    def cell(position, carry):
        a, b, c = position // 4, (position // 2) % 2, position % 2
        lane_kind = corner_kinds(kinds, a + 1, b + 1, c + 1, lane)
        columns_out[position] = choose([table_t[q, 0:CELL] for q in range(species)], lane_kind)
        return carry

    lax.fori_loop(0, 8, cell, 0)
    for axis in range(3):
        for s in range(2):
            near = 8 - 8 * s
            for q in range(species):
                if axis == 0:
                    picked[q, 0:81] = table_t[q, near * 81 : near * 81 + 81]
                elif axis == 1:
                    for x in range(9):
                        picked[q, x * 9 : x * 9 + 9] = table_t[q, x * 81 + near * 9 : x * 81 + near * 9 + 9]
                else:
                    picked[q, 0:81] = table_t[q, pl.ds(near, 81, stride=9)]

            def face(n, carry, axis=axis, s=s):
                spot = [n // 2 + 1, n % 2 + 1]
                spot.insert(axis, 3 * s)
                lane_kind = corner_kinds(kinds, *spot, lane)
                faces_out[axis * 8 + s * 4 + n] = choose([picked[q, 0:81] for q in range(species)], lane_kind)
                return carry

            lax.fori_loop(0, 4, face, 0)
    for axis in range(3):
        for s in range(2):
            for t in range(2):
                first, second = 8 - 8 * s, 8 - 8 * t
                for u in range(2):
                    spot = [3 * s, 3 * t]
                    spot.insert(axis, u + 1)
                    start, stride = ((first * 9 + second, 81), (first * 81 + second, 9), (first * 81 + second * 9, 1))[axis]
                    lane_kind = corner_kinds(kinds, *spot, lane)
                    place = slice(start, start + 9) if stride == 1 else pl.ds(start, 9, stride=stride)
                    edges_out[axis * 8 + s * 4 + t * 2 + u, 0:9] = choose([table_t[q, place] for q in range(species)], lane_kind)
    for n in range(8):
        s, t, w = n // 4, (n // 2) % 2, n % 2
        at = (8 - 8 * s) * 81 + (8 - 8 * t) * 9 + 8 - 8 * w
        lane_kind = corner_kinds(kinds, 3 * s, 3 * t, 3 * w, lane)
        points_out[n, 0:1] = choose([table_t[q, at : at + 1] for q in range(species)], lane_kind)


def make_tables(kinds, table_t, after):
    species = table_t.shape[0]
    return pl.pallas_call(
        tables_kernel,
        out_shape=(
            shape((8, CELL, LANES), BF16),
            shape((24, 81, LANES), BF16),
            shape((24, 9, LANES), BF16),
            shape((8, 1, LANES), BF16),
        ),
        in_specs=[VMEM, VMEM, pl.BlockSpec(memory_space=pl.ANY)],
        out_specs=(VMEM,) * 4,
        scratch_shapes=[pltpu.VMEM((species, 88, LANES), F32)],
        cost_estimate=cost(1e7, 6e6),
        compiler_params=SMALL,
        name="tables",
    )(kinds, table_t, after)


def first_x_kernel(psi, own, message, up):
    message[0:256, :] = psi[...].reshape(256, LANES)
    species = [jnp.full((1, LANES), own[n].astype(F32), F32) for n in range(8)]
    blank = jnp.zeros((8, LANES), F32)
    message[256:272, :] = jnp.concatenate(species + [blank], axis=0).astype(BF16)
    up[...] = jnp.concatenate(species[4:] + [blank[0:4]], axis=0)


def first_x(psi, own):
    return pl.pallas_call(
        first_x_kernel,
        grid=(1,),
        out_shape=(shape((272, LANES), BF16), shape((8, LANES), F32)),
        in_specs=[pl.BlockSpec((1, 16, 16, LANES), lambda n: (0, 0, 0, 0)), SMEM],
        out_specs=(pl.BlockSpec((272, LANES), lambda n: (0, 0)), pl.BlockSpec((8, LANES), lambda n: (0, 0))),
        cost_estimate=cost(1e5, 2e5),
        compiler_params=SMALL,
        name="first_x",
    )(pltpu.with_memory_space_constraint(psi, pltpu.HBM), own)


def first_rows_kernel(psi, rows_y, rows_z, wide, narrow):
    for x in range(16):
        rows_y[x * 16 : x * 16 + 16, :] = psi[x, 0]
    wide[...] = psi[...].reshape(4096, LANES).astype(F32)
    rows = wide[pl.ds(0, 256, stride=16), :]
    narrow[...] = jnp.zeros_like(narrow)
    for x in range(16):
        narrow[x * SIDE : x * SIDE + 16, :] = rows[x * 16 : x * 16 + 16]
    rows_z[...] = narrow[...]


def first_rows(psi):
    return pl.pallas_call(
        first_rows_kernel,
        out_shape=(shape((256, LANES), BF16), shape((FACE, LANES), F32)),
        in_specs=[VMEM],
        out_specs=(VMEM, VMEM),
        scratch_shapes=[pltpu.VMEM((4096, LANES), F32), pltpu.VMEM((FACE, LANES), F32)],
        cost_estimate=cost(1e6, 1.2e6),
        compiler_params=SMALL,
        name="first_rows",
    )(psi)


def first_y_kernel(rows_y, from_x, up_x, own, message, up, s20):
    message[0:256, :] = rows_y[...]
    message[256:272, :] = from_x[0:16, :]
    s20[0:4, :] = up_x[0:4, :]
    for n in range(8):
        s20[4 + n : 5 + n, :] = jnp.full((1, LANES), own[n].astype(F32), F32)
    s20[12:20, :] = from_x[256:272, :].astype(F32)[0:8]
    s20[20:32, :] = jnp.zeros((12, LANES), F32)
    message[272:304, :] = s20[...].astype(BF16)
    for x in range(5):
        up[x * 2 : x * 2 + 2, :] = s20[x * 4 + 2 : x * 4 + 4, :]
    up[10:16, :] = jnp.zeros((6, LANES), F32)


def first_y(rows_y, from_x, up_x, own):
    return pl.pallas_call(
        first_y_kernel,
        out_shape=(shape((304, LANES), BF16), shape((16, LANES), F32), shape((32, LANES), F32)),
        in_specs=[VMEM, VMEM, VMEM, SMEM],
        out_specs=(VMEM,) * 3,
        cost_estimate=cost(1e5, 2e5),
        compiler_params=SMALL,
        name="first_y",
    )(rows_y, from_x, up_x, own)


def first_z_kernel(rows, from_x, from_y, up_y, s20, after, message, up, s50, wide_x, wide_y, face):
    del after
    wide_x[...] = from_x[0:256, :].astype(F32)
    wide_y[...] = from_y[...].astype(F32)
    face[...] = rows[...]
    face[16 * SIDE : 16 * SIDE + 16, :] = wide_x[pl.ds(0, 16, stride=16), :]
    face[pl.ds(16, SIDE, stride=SIDE), :] = wide_y[pl.ds(0, SIDE, stride=16), :]
    message[0:FACE, :] = face[...].astype(BF16)
    for x in range(5):
        s50[x * 10 : x * 10 + 2, :] = up_y[x * 2 : x * 2 + 2, :]
        s50[x * 10 + 2 : x * 10 + 6, :] = s20[x * 4 : x * 4 + 4, :]
        s50[x * 10 + 6 : x * 10 + 10, :] = wide_y[272 + x * 4 : 272 + x * 4 + 4, :]
    s50[50:64, :] = jnp.zeros((14, LANES), F32)
    message[FACE : FACE + 64, :] = s50[...].astype(BF16)
    up[0:25, :] = s50[pl.ds(1, 25, stride=2), :]
    up[25:32, :] = jnp.zeros((7, LANES), F32)


def first_z(rows, from_x, from_y, up_y, s20, after):
    return pl.pallas_call(
        first_z_kernel,
        out_shape=(shape((FACE + 64, LANES), BF16), shape((32, LANES), F32), shape((64, LANES), F32)),
        in_specs=[VMEM] * 5 + [pl.BlockSpec(memory_space=pl.ANY)],
        out_specs=(VMEM,) * 3,
        scratch_shapes=[
            pltpu.VMEM((256, LANES), F32),
            pltpu.VMEM((304, LANES), F32),
            pltpu.VMEM((FACE, LANES), F32),
        ],
        cost_estimate=cost(1e5, 4e5),
        compiler_params=SMALL,
        name="first_z",
    )(rows, from_x, from_y, up_y, s20, after)


def begin_kernel(psi, from_x, from_y, from_z, field_out, field, wide):
    field[...] = jnp.zeros_like(field)

    def slab(x, carry):
        for y in range(16):
            start = pl.multiple_of(x * SLAB + y * ZPAD, 8)
            field[pl.ds(start, 16), :] = psi[x, y].astype(F32)
        return carry

    lax.fori_loop(0, 16, slab, 0)
    for y in range(16):
        at = 16 * SLAB + y * ZPAD
        field[at : at + 16, :] = from_x[y * 16 : y * 16 + 16, :].astype(F32)
    for x in range(SIDE):
        at = x * SLAB + 16 * ZPAD
        field[at : at + 16, :] = from_y[x * 16 : x * 16 + 16, :].astype(F32)
    wide[...] = from_z[0:FACE, :].astype(F32)
    field[pl.ds(16, PLANE, stride=ZPAD), :] = wide[0:PLANE, :]

    def chunk(n, carry):
        spot = pl.ds(pl.multiple_of(n * CHUNK, 16), CHUNK)
        field_out[spot, :] = field[spot, :].astype(BF16)
        return carry

    lax.fori_loop(0, ROWS // CHUNK, chunk, 0)


def begin(psi, from_x, from_y, from_z):
    return pl.pallas_call(
        begin_kernel,
        out_shape=shape((ROWS, LANES), BF16),
        in_specs=[VMEM] * 4,
        out_specs=VMEM,
        scratch_shapes=[pltpu.VMEM((ROWS, LANES), F32), pltpu.VMEM((FACE, LANES), F32)],
        cost_estimate=cost(1e7, 4e6),
        compiler_params=LARGE,
        name="begin",
    )(psi, from_x, from_y, from_z)


HAM_ROWS = 128


def by_cell_kernel(source, after, out, token, wide):
    del after
    token[...] = jnp.zeros_like(token)
    def piece(n, carry):
        for half in range(2):
            spot = pl.ds(pl.multiple_of(n * 32 + half * 16, 16), 16)
            for start in range(0, CELL, LANES):
                width = min(LANES, CELL - start)
                block = wide.at[half, start : start + LANES]
                block[:, 0:width] = source[spot, :, start : start + width].astype(F32).reshape(128, width)
        for half in range(2):
            spot = pl.ds(pl.multiple_of(n * 32 + half * 16, 16), 16)
            for start in range(0, CELL, LANES):
                width = min(LANES, CELL - start)
                block = wide.at[half, start : start + LANES]
                for c in range(8):
                    found = block[pl.ds(c, 16, stride=8), :]
                    out[c, spot, start : start + width] = found[:, 0:width].astype(BF16)
        return carry

    lax.fori_loop(0, HAM_ROWS // 32, piece, 0)


def by_cell(ham, after):
    return pl.pallas_call(
        by_cell_kernel,
        grid=(pl.cdiv(CELL, HAM_ROWS),),
        out_shape=(shape((8, CELL, CELL), BF16), shape((8, LANES), F32)),
        in_specs=[pl.BlockSpec((HAM_ROWS, 8, CELL), lambda n: (n, 0, 0)), pl.BlockSpec(memory_space=pl.ANY)],
        out_specs=(
            pl.BlockSpec((8, HAM_ROWS, CELL), lambda n: (0, n, 0)),
            pl.BlockSpec((8, LANES), lambda n: (0, 0)),
        ),
        scratch_shapes=[pltpu.VMEM((2, 768, LANES), F32)],
        cost_estimate=cost(1e7, 1.8e7),
        compiler_params=LARGE,
        name="by_cell",
    )(pltpu.with_memory_space_constraint(jnp.transpose(ham, (1, 0, 2)), pltpu.HBM), after)


MESSAGE_Y = FACE + 288
MESSAGE_Z = FACE + 480
MESSAGE_X = FACE + 800


def send(odd, low, high, first, second, rows):
    first[rows, :] = jnp.where(odd, low, high).astype(BF16)
    second[rows, :] = jnp.where(odd, high, low).astype(BF16)


def receive(odd, first, second, rows):
    one, two = first[rows, :].astype(F32), second[rows, :].astype(F32)
    return jnp.where(odd, one, two), jnp.where(odd, two, one)


def apply_kernel(full, odd, now, ham, rows, mix, terms, send_one, send_two, zface, xface, weights, field, cell32, total, yface):
    def chunk(n, carry):
        spot = pl.ds(pl.multiple_of(n * CHUNK, 16), CHUNK)
        field[spot, :] = now[spot, :].astype(F32)
        return carry

    lax.fori_loop(0, ROWS // CHUNK, chunk, 0)
    for ref in (total, xface, yface, zface):
        ref[...] = jnp.zeros_like(ref)

    def cell(position, carry):
        a, b, c = position // 4, (position // 2) % 2, position % 2
        base = cell_base(a, b, c)
        for x in range(9):
            for y in range(9):
                at = (x * 9 + y) * 9
                cell32[at : at + 9, :] = field[pl.ds(line_start(base, x, y), 9), :]
        values = cell32[0:CELL, :].astype(BF16)
        part = jnp.dot(rows[position], values, preferred_element_type=F32)
        for o in range(8):
            i, j, k = o // 4, (o // 2) % 2, o % 2
            vertex = (a + i) * 9 + (b + j) * 3 + c + k
            total[pl.ds(pl.multiple_of(vertex * 16, 16), 16), :] += part[o * 16 : (o + 1) * 16]
        result = jnp.dot(ham[position], values, preferred_element_type=F32)
        if full:
            terms[position] = result
            cell32[0:CELL, :] = result
            sources = (
                cell32.at[pl.ds(pl.multiple_of(a * 648, 8), 88)],
                cell32.at[pl.ds(pl.multiple_of(b * 72, 8), 664)],
                cell32.at[pl.ds(pl.multiple_of(c * 8, 8), 728)],
            )
        else:
            terms[position] = values
            cell32[0:PICKED, :] = result
            sources = (cell32, cell32, cell32)
        places = (
            xface.at[pl.ds(pl.multiple_of(a * FACE + b * 136 + c * 8, 8), 152)],
            yface.at[pl.ds(pl.multiple_of(b * FACE + a * 136 + c * 8, 8), 152)],
            zface.at[pl.ds(pl.multiple_of(c * FACE + a * 136 + b * 8, 8), 152)],
        )
        for axis in range(3):
            for n in range(9):
                if not full:
                    spot = slice(axis * 81 + n * 9, axis * 81 + n * 9 + 9)
                elif axis == 0:
                    spot = slice(n * 9, n * 9 + 9)
                elif axis == 1:
                    spot = slice(n * 81, n * 81 + 9)
                else:
                    spot = pl.ds(n * 81, 9, stride=9)
                places[axis][n * SIDE : n * SIDE + 9, :] += sources[axis][spot, :]
        return carry

    lax.fori_loop(0, 8, cell, 0)
    turn = odd[1] == 1
    for g in range(4):
        spot = slice(g * 128, g * 128 + 128)
        total[spot, :] = jnp.dot(mix[g], total[spot, :], precision=HIGHEST, preferred_element_type=F32)
    weights[...] = total[0:432, :]
    send(turn, yface[0:FACE, :], yface[FACE : 2 * FACE, :], send_one, send_two, slice(0, FACE))
    for p in range(2):
        for x in range(3):
            at = FACE + (p * 3 + x) * 48
            down = total[x * 144 + p * 48 : x * 144 + p * 48 + 48, :]
            up = total[x * 144 + (p + 1) * 48 : x * 144 + (p + 1) * 48 + 48, :]
            send(turn, down, up, send_one, send_two, slice(at, at + 48))


def apply_cells(full, odd, now, ham, rows, mix):
    faces = shape((2 * FACE, LANES), F32)
    message = shape((MESSAGE_Y, LANES), BF16)
    return pl.pallas_call(
        functools.partial(apply_kernel, full),
        out_shape=(shape((8, CELL, LANES), F32 if full else BF16), message, message, faces, faces, shape((432, LANES), F32)),
        in_specs=[SMEM] + [VMEM] * 4,
        out_specs=(VMEM,) * 6,
        scratch_shapes=[
            pltpu.VMEM((ROWS, LANES), F32),
            pltpu.VMEM((736, LANES), F32),
            pltpu.VMEM((512, LANES), F32),
            pltpu.VMEM((2 * FACE, LANES), F32),
        ],
        cost_estimate=cost(1.3e9 if full else 6e8, 1.6e7),
        compiler_params=LARGE,
        name="apply_cells",
    )(odd, now, ham, rows, mix)


PICKED = 256


def pick_kernel(ham, after, out):
    del after
    row = lax.broadcasted_iota(jnp.int32, (PICKED, 1), 0)
    column = lax.broadcasted_iota(jnp.int32, (PICKED, CELL), 1)

    def cell(position, carry):
        a, b, c = position // 4, (position // 2) % 2, position % 2
        on_y, on_z = row - 81, row - 162
        nine_y, nine_z = lax.shift_right_arithmetic(on_y * 57, 9), lax.shift_right_arithmetic(on_z * 57, 9)
        node = nine_z * 81 + (on_z - nine_z * 9) * 9 + c * 8
        node = jnp.where(row < 162, nine_y * 81 + b * 72 + (on_y - nine_y * 9), node)
        node = jnp.where(row < 81, a * 648 + row, node)
        node = jnp.where(row < 243, node, -1)
        chosen = jnp.where(column == node, 1.0, 0.0).astype(BF16)
        out[position] = jnp.dot(chosen, ham[position], preferred_element_type=F32).astype(BF16)
        return carry

    lax.fori_loop(0, 8, cell, 0)


def pick(ham, after):
    return pl.pallas_call(
        pick_kernel,
        out_shape=shape((8, PICKED, CELL), BF16),
        in_specs=[VMEM, pl.BlockSpec(memory_space=pl.ANY)],
        out_specs=VMEM,
        cost_estimate=cost(2e9, 1.2e7),
        compiler_params=LARGE,
        name="pick",
    )(ham, after)


def local_kernel(ham, values, terms, token):
    token[...] = jnp.zeros_like(token)

    def cell(position, carry):
        terms[position] = jnp.dot(ham[position], values[position], preferred_element_type=F32)
        return carry

    lax.fori_loop(0, 8, cell, 0)


def local_part(ham, values):
    return pl.pallas_call(
        local_kernel,
        out_shape=(shape((8, CELL, LANES), F32), shape((8, LANES), F32)),
        in_specs=[VMEM, VMEM],
        out_specs=(VMEM, VMEM),
        cost_estimate=cost(1.1e9, 1.4e7),
        compiler_params=LARGE,
        name="local_part",
    )(ham, values)


def assemble_kernel(first, terms, now, *refs):
    before = None if first else refs[0]
    field = refs[-1]
    scale = 1.0 if first else 2.0

    def chunk(n, carry):
        spot = pl.ds(pl.multiple_of(n * CHUNK, 16), CHUNK)
        value = -scale * now[spot, :].astype(F32)
        if before is not None:
            value = value - before[spot, :].astype(F32)
        field[spot, :] = value
        return carry

    lax.fori_loop(0, ROWS // CHUNK, chunk, 0)

    def cell(position, carry):
        a, b, c = position // 4, (position // 2) % 2, position % 2
        base = cell_base(a, b, c)
        for x in range(9):
            for y in range(9):
                at = (x * 9 + y) * 9
                field[pl.ds(line_start(base, x, y), 9), :] += scale * terms[position, at : at + 9, :]
        return carry

    lax.fori_loop(0, 8, cell, 0)


def assemble(terms, now, before):
    args = [terms, now] + ([] if before is None else [before])
    return pl.pallas_call(
        functools.partial(assemble_kernel, before is None),
        out_shape=shape((ROWS, LANES), F32),
        in_specs=[VMEM] * len(args),
        out_specs=VMEM,
        cost_estimate=cost(1e7, 1.2e7),
        compiler_params=SMALL,
        name="assemble",
    )(*args)


def after_y_kernel(odd, one, two, zface, xface, weights, after, send_one, send_two, xface_out, weights_out, low, high, face_low, face_high):
    del after
    low[...], high[...] = receive(odd[1] == 1, one, two, slice(0, FACE))
    turn = odd[2] == 1
    last = 16 * SIDE
    for face, start, column in ((face_low, 0, 0), (face_high, FACE, 16)):
        face[...] = zface[start : start + FACE, :]
        face[pl.ds(0, SIDE, stride=SIDE), :] += low[pl.ds(column, SIDE, stride=SIDE), :]
        face[pl.ds(16, SIDE, stride=SIDE), :] += high[pl.ds(column, SIDE, stride=SIDE), :]
    send(turn, face_low[...], face_high[...], send_one, send_two, slice(0, FACE))
    xface_out[...] = xface[...]
    for start, row in ((0, 0), (FACE, last)):
        xface_out[start : start + SIDE, :] += low[row : row + SIDE, :]
        xface_out[start + last : start + last + SIDE, :] += high[row : row + SIDE, :]
    for x in range(3):
        weights_out[x * 240 + 48 : x * 240 + 192, :] = weights[x * 144 : x * 144 + 144, :]
        for p in range(2):
            at = FACE + (p * 3 + x) * 48
            below, above = receive(odd[1] == 1, one, two, slice(at, at + 48))
            if p == 0:
                weights_out[x * 240 : x * 240 + 48, :] = below
                weights_out[x * 240 + 144 : x * 240 + 192, :] += above
            else:
                weights_out[x * 240 + 48 : x * 240 + 96, :] += below
                weights_out[x * 240 + 192 : x * 240 + 240, :] = above
    for p in range(2):
        for n in range(15):
            at = FACE + (p * 15 + n) * 16
            down = weights_out[n * 48 + p * 16 : n * 48 + p * 16 + 16, :]
            up = weights_out[n * 48 + p * 16 + 16 : n * 48 + p * 16 + 32, :]
            send(turn, down, up, send_one, send_two, slice(at, at + 16))


def after_y(odd, one, two, zface, xface, weights, after):
    message = shape((MESSAGE_Z, LANES), BF16)
    return pl.pallas_call(
        after_y_kernel,
        out_shape=(message, message, shape((2 * FACE, LANES), F32), shape((720, LANES), F32)),
        in_specs=[SMEM] + [VMEM] * 5 + [pl.BlockSpec(memory_space=pl.ANY)],
        out_specs=(VMEM,) * 4,
        scratch_shapes=[pltpu.VMEM((FACE, LANES), F32)] * 4,
        cost_estimate=cost(1e5, 2e6),
        compiler_params=SMALL,
        name="after_y",
    )(odd, one, two, zface, xface, weights, after)


def after_z_kernel(odd, one, two, xface, weights, send_one, send_two, weights_out, low, high, face_low, face_high):
    low[...], high[...] = receive(odd[2] == 1, one, two, slice(0, FACE))
    turn = odd[0] == 1
    for face, start, row in ((face_low, 0, 0), (face_high, FACE, 16 * SIDE)):
        face[...] = xface[start : start + FACE, :]
        face[pl.ds(0, SIDE, stride=SIDE), :] += low[row : row + SIDE, :]
        face[pl.ds(16, SIDE, stride=SIDE), :] += high[row : row + SIDE, :]
    send(turn, face_low[...], face_high[...], send_one, send_two, slice(0, FACE))
    for n in range(15):
        weights_out[n * 80 + 16 : n * 80 + 64, :] = weights[n * 48 : n * 48 + 48, :]
        for p in range(2):
            at = FACE + (p * 15 + n) * 16
            below, above = receive(odd[2] == 1, one, two, slice(at, at + 16))
            if p == 0:
                weights_out[n * 80 : n * 80 + 16, :] = below
                weights_out[n * 80 + 48 : n * 80 + 64, :] += above
            else:
                weights_out[n * 80 + 16 : n * 80 + 32, :] += below
                weights_out[n * 80 + 64 : n * 80 + 80, :] = above
    for p in range(2):
        at = FACE + p * 400
        down, up = weights_out[p * 400 : p * 400 + 400, :], weights_out[p * 400 + 400 : p * 400 + 800, :]
        send(turn, down, up, send_one, send_two, slice(at, at + 400))


def after_z(odd, one, two, xface, weights):
    message = shape((MESSAGE_X, LANES), BF16)
    return pl.pallas_call(
        after_z_kernel,
        out_shape=(message, message, shape((1200, LANES), F32)),
        in_specs=[SMEM] + [VMEM] * 4,
        out_specs=(VMEM,) * 3,
        scratch_shapes=[pltpu.VMEM((FACE, LANES), F32)] * 4,
        cost_estimate=cost(1e5, 2e6),
        compiler_params=SMALL,
        name="after_z",
    )(odd, one, two, xface, weights)


def corner_weights(weights, a, b, c):
    pieces = []
    for o in range(8):
        i, j, k = o // 4, (o // 2) % 2, o % 2
        vertex = ((a + i) * 5 + b + j) * 5 + c + k
        pieces.append(weights[pl.ds(pl.multiple_of(vertex * 16, 16), 16), :])
    return jnp.concatenate(pieces, axis=0)


def advance_kernel(first, last, odd, start_field, y1, y2, z1, z2, x1, x2, w75, columns, faces, edges, points, out, *refs):
    del start_field
    parts = refs[: len(refs) - 6]
    field, cell32, weights, xs, ys, zs = refs[len(refs) - 6 :]
    scale = 1.0 if first else 2.0
    for ref, one, two, axis in ((xs, x1, x2, 0), (ys, y1, y2, 1), (zs, z1, z2, 2)):
        low, high = receive(odd[axis] == 1, one, two, slice(0, FACE))
        ref[0:FACE, :] = low
        ref[FACE : 2 * FACE, :] = high
    for p in range(2):
        at = FACE + p * 400
        below, above = receive(odd[0] == 1, x1, x2, slice(at, at + 400))
        if p == 0:
            weights[0:400, :] = below.astype(BF16)
            weights[1200:1600, :] = (w75[800:1200, :] + above).astype(BF16)
        else:
            weights[400:800, :] = (w75[0:400, :] + below).astype(BF16)
            weights[1600:2000, :] = above.astype(BF16)
    weights[800:1200, :] = w75[400:800, :].astype(BF16)

    def cell(position, carry):
        a, b, c = position // 4, (position // 2) % 2, position % 2
        corner = corner_weights(weights, a + 1, b + 1, c + 1)
        cell32[0:CELL, :] = scale * jnp.dot(columns[position], corner, preferred_element_type=F32)
        base = cell_base(a, b, c)
        for x in range(9):
            for y in range(9):
                at = (x * 9 + y) * 9
                field[pl.ds(line_start(base, x, y), 9), :] += cell32[at : at + 9, :]
        return carry

    lax.fori_loop(0, 8, cell, 0)

    for axis, ref in enumerate((xs, ys, zs)):

        def face(s, carry, axis=axis, ref=ref):
            for n in range(4):
                spot = [n // 2 + 1, n % 2 + 1]
                spot.insert(axis, 3 * s)
                cell32[n * 88 : n * 88 + 81, :] = jnp.dot(
                    faces[axis * 8 + s * 4 + n], corner_weights(weights, *spot), preferred_element_type=F32
                )
            for n in range(4):
                view = ref.at[pl.ds(pl.multiple_of(s * FACE + (n // 2) * 136 + (n % 2) * 8, 8), 152)]
                for row in range(9):
                    at = n * 88 + row * 9
                    view[row * SIDE : row * SIDE + 9, :] += cell32[at : at + 9, :]
            return carry

        lax.fori_loop(0, 2, face, 0)

    for axis in range(3):

        def edge(s, carry, axis=axis):
            terms = []
            for n in range(4):
                spot = [3 * s, 3 * (n // 2)]
                spot.insert(axis, n % 2 + 1)
                terms.append(
                    jnp.dot(edges[axis * 8 + s * 4 + n], corner_weights(weights, *spot), preferred_element_type=F32)
                )
            for n, term in enumerate(terms):
                t, u = n // 2, n % 2
                if axis == 2:
                    view = xs.at[pl.ds(pl.multiple_of(s * FACE + t * 272 + u * 8, 8), 16)]
                    view[0:9, :] += term
                else:
                    ref = xs if axis == 1 else ys
                    view = ref.at[pl.ds(pl.multiple_of(s * FACE + u * 136 + t * 16, 8), 152)]
                    view[pl.ds(0, 9, stride=SIDE), :] += term
            return carry

        lax.fori_loop(0, 2, edge, 0)

    def point(s, carry):
        terms = []
        for n in range(4):
            corner = corner_weights(weights, 3 * s, 3 * (n // 2), 3 * (n % 2))
            terms.append(jnp.dot(points[s * 4 + n], corner, preferred_element_type=F32))
        for n, term in enumerate(terms):
            view = xs.at[pl.ds(pl.multiple_of(s * FACE + (n // 2) * 272 + (n % 2) * 16, 8), 8)]
            view[0:1, :] += term
        return carry

    lax.fori_loop(0, 2, point, 0)

    for s in range(2):
        for y in range(SIDE):
            at = s * 16 * SLAB + y * ZPAD
            field[at : at + SIDE, :] += scale * xs[s * FACE + y * SIDE : s * FACE + (y + 1) * SIDE, :]
        for x in range(SIDE):
            at = s * 16 * ZPAD + x * SLAB
            field[at : at + SIDE, :] += scale * ys[s * FACE + x * SIDE : s * FACE + (x + 1) * SIDE, :]
        field[pl.ds(s * 16, PLANE, stride=ZPAD), :] += scale * zs[s * FACE : s * FACE + PLANE, :]

    if last:

        def slab(x, carry):
            for y in range(16):
                start = pl.multiple_of(x * SLAB + y * ZPAD, 8)
                out[x, y] = field[pl.ds(start, 16), :].astype(BF16)
            return carry

        lax.fori_loop(0, 16, slab, 0)
        for offset, part in enumerate(parts):
            quarter = (odd[3] + offset) % 4
            part[...] = out[pl.ds(quarter * 4, 4)].reshape(1024, LANES)
    else:

        def chunk(n, carry):
            spot = pl.ds(pl.multiple_of(n * CHUNK, 16), CHUNK)
            out[spot, :] = field[spot, :].astype(BF16)
            return carry

        lax.fori_loop(0, ROWS // CHUNK, chunk, 0)


def advance(odd, field, messages, w75, tables, first, last):
    args = [odd, field, *messages, w75, *tables]
    if last:
        outs = [shape((16, 16, 16, LANES), BF16)] + [shape((1024, LANES), BF16)] * 4
    else:
        outs = [shape((ROWS, LANES), BF16)]
    outs.append(shape((ROWS, LANES), F32))
    return pl.pallas_call(
        functools.partial(advance_kernel, first, last),
        out_shape=tuple(outs),
        in_specs=[SMEM] + [VMEM] * (len(args) - 1),
        out_specs=(VMEM,) * len(outs),
        input_output_aliases={1: len(outs) - 1},
        scratch_shapes=[pltpu.VMEM((736, LANES), F32), pltpu.VMEM((2000, LANES), BF16)]
        + [pltpu.VMEM((2 * FACE, LANES), F32)] * 3,
        cost_estimate=cost(3e8, 1.2e7),
        compiler_params=LARGE,
        name="advance",
    )(*args)[:-1]


def gram_kernel(x0, x1, x2, x3, own, m1, m2, m3):
    blocks = [x0[...], x1[...], x2[...], x3[...]]
    for row, left in enumerate(blocks):
        turned = left.T
        for column, out in ((0, own), (3, m1), (2, m2), (1, m3)):
            part = jnp.dot(turned, blocks[column], preferred_element_type=F32)
            out[row * 128 : row * 128 + 128, :] = part.astype(out.dtype)


def gram(blocks):
    return pl.pallas_call(
        gram_kernel,
        out_shape=(shape((512, LANES), F32),) + (shape((512, LANES), BF16),) * 3,
        in_specs=[VMEM] * 4,
        out_specs=(VMEM,) * 4,
        cost_estimate=cost(6e8, 2e6),
        compiler_params=LARGE,
        name="gram",
    )(*blocks)


def collect_kernel(band, own, m1, m2, m3, out):
    for row in range(4):
        total = own[row * 128 : row * 128 + 128, :]
        for offset, ref in ((1, m1), (2, m2), (3, m3)):
            source = (row - offset) % 4
            total = total + ref[source * 128 : source * 128 + 128, :].astype(F32)
        place = (band[0] + 4 - row) % 4
        out[pl.ds(place * 16, 16)] = total.reshape(16, 8, LANES).astype(BF16)


def collect(band, own, received):
    return pl.pallas_call(
        collect_kernel,
        out_shape=shape((64, 8, LANES), BF16),
        in_specs=[SMEM] + [VMEM] * 4,
        out_specs=VMEM,
        cost_estimate=cost(1e6, 1e6),
        compiler_params=SMALL,
        name="collect",
    )(band, own, *received)


def local(psi, cell_ham, proj_table, coupling, atom_kind):
    devices = lax.axis_size("cells")
    side = cube_root(devices)
    offsets = (1, side, side * side)
    block = lax.axis_index("cells")
    band = lax.axis_index("bands")
    odd = jnp.stack([(block // offset) % 2 for offset in offsets] + [band]).astype(jnp.int32)

    def upward(x, axis):
        return shifted(x, "cells", offsets[axis])

    def downward(x, axis):
        return shifted(x, "cells", -offsets[axis])

    def swap(messages, axis):
        offset = offsets[axis]
        arrived = []
        for start, message in enumerate(messages):
            pairs = []
            for i in range(devices):
                forward = (i // offset) % 2 == start
                pairs.append((i, (i + offset) % devices if forward else (i - offset) % devices))
            arrived.append(lax.ppermute(message, "cells", pairs))
        return arrived

    own = atom_kind.reshape(8)
    message, up = first_x(psi, own)
    from_x, up_x = downward(message, 0), upward(up, 0)
    rows_y, rows_z = first_rows(psi)
    message, up, s20 = first_y(rows_y, from_x, up_x, own)
    from_y, up_y = downward(message, 1), upward(up, 1)
    ham, token = by_cell(cell_ham, s20)
    message, up, s50 = first_z(rows_z, from_x, from_y, up_y, s20, token)
    from_z, up_z = downward(message, 2), upward(up, 2)
    table = proj_table.reshape(4, 128, CELL)
    kinds, rows, mix = first_tables(from_z, up_z, s50, table, coupling)

    def step(now, before, last, tables):
        first = tables is None
        terms, one, two, zface, xface, weights = apply_cells(
            first, odd, now, ham if first else tables[-1], rows, mix
        )
        ys = swap((one, two), 1)
        if first:
            picked = pick(ham, weights)
            token = picked
            tables = (*make_tables(kinds, turn(table, weights), weights), picked)
        else:
            terms, token = local_part(ham, terms)
        field = assemble(terms, now, before)
        one, two, xface, weights = after_y(odd, *ys, zface, xface, weights, token)
        zs = swap((one, two), 2)
        one, two, weights = after_z(odd, *zs, xface, weights)
        xs = swap((one, two), 0)
        return tables, advance(odd, field, (*ys, *zs, *xs), weights, tables[:4], before is None, last)

    y0 = begin(psi, from_x, from_y, from_z)
    tables, (y1,) = step(y0, None, False, None)
    tables, (y2,) = step(y1, y0, False, tables)
    tables, (filtered, *blocks) = step(y2, y1, True, tables)

    two = shifted(blocks[2], "bands", 2)
    blocks = [blocks[0], shifted(blocks[1], "bands", 1), two, shifted(blocks[3], "bands", 3)]
    own, *messages = gram(blocks)
    messages = [shifted(message, "bands", n + 1) for n, message in enumerate(messages)]
    terms = collect(band.astype(jnp.int32).reshape(1), own, messages)
    terms = lax.all_to_all(terms, "cells", 0, 0)
    inverse_count = 1.0 / (4096 * devices)
    correlation = jnp.sum(terms.astype(F32), axis=0) * inverse_count
    return filtered, correlation


def solution(mesh):
    in_specs = (
        P("cells", None, None, "bands"),
        P("cells", None, None),
        P(),
        P(),
        P("cells", None, None),
    )
    out_specs = (P("cells", None, None, "bands"), P("cells", "bands"))
    return jax.shard_map(local, mesh=mesh, in_specs=in_specs, out_specs=out_specs, check_vma=False)
```

```python
import functools

import jax
import jax.numpy as jnp
from jax import lax
from jax.experimental import pallas as pl
from jax.experimental.pallas import tpu as pltpu
from jax.sharding import PartitionSpec as P


F32 = jnp.float32
BF16 = jnp.bfloat16
HIGHEST = lax.Precision.HIGHEST

SIDE = 17
ZPAD = 24
SLAB = SIDE * ZPAD
ROWS = 6944
CHUNK = 496
FACE = 304
PLANE = SIDE * SIDE
CELL = 729
LANES = 128


def shifted(x, axis, by):
    devices = lax.axis_size(axis)
    return lax.ppermute(x, axis, [(i, (i + by) % devices) for i in range(devices)])


def cube_root(amount):
    result = 1
    while (result + 1) ** 3 <= amount:
        result = result + 1
    return result


def cost(flops, nbytes):
    return pl.CostEstimate(flops=int(flops), bytes_accessed=int(nbytes), transcendentals=0)


def shape(dims, dtype):
    return jax.ShapeDtypeStruct(dims, dtype)


VMEM = pl.BlockSpec(memory_space=pltpu.VMEM)
LARGE = pltpu.CompilerParams(vmem_limit_bytes=10 * 2**20)
SMALL = pltpu.CompilerParams(vmem_limit_bytes=6 * 2**20)
SMEM = pl.BlockSpec(memory_space=pltpu.SMEM)


def cell_base(a, b, c):
    return a * (8 * SLAB) + b * (8 * ZPAD) + c * 8


def line_start(base, x, y):
    return pl.multiple_of(base + (x * SLAB + y * ZPAD), 8)


def kind_row(kinds, a, b, c):
    return kinds[(a * 5 + b) * 5 + c][0:1, :]


def corner_kinds(kinds, a, b, c, lane):
    found = jnp.full((1, LANES), -1.0, F32)
    for o in range(8):
        i, j, k = o // 4, (o // 2) % 2, o % 2
        found = jnp.where(lane == o, kind_row(kinds, a + i, b + j, c + k), found)
    return found


def first_tables_kernel(from_z, up_z, s50, table, coupling, kinds, rows_out, mix_out, wide, chosen):
    for n in range(25):
        kinds[n * 5] = jnp.broadcast_to(up_z[n : n + 1, :], (8, LANES))
        for k in range(2):
            at = n * 2 + k
            kinds[n * 5 + 1 + k] = jnp.broadcast_to(s50[at : at + 1, :], (8, LANES))
    above = from_z[FACE : FACE + 64, :].astype(F32)
    for n in range(50):
        kinds[(n // 2) * 5 + 3 + n % 2] = jnp.broadcast_to(above[n : n + 1, :], (8, LANES))
    species = coupling.shape[0]
    lane_wide = lax.broadcasted_iota(jnp.int32, (16, LANES), 1) // 16
    entry = lax.broadcasted_iota(jnp.int32, (16, species * 128), 1) - lax.broadcasted_iota(
        jnp.int32, (16, species * 128), 0
    )
    entry = entry.astype(F32)

    def cell(position, carry):
        a, b, c = position // 4, (position // 2) % 2, position % 2
        for o in range(8):
            i, j, k = o // 4, (o // 2) % 2, o % 2
            kind = kind_row(kinds, a + i + 1, b + j + 1, c + k + 1)[:, 0:1]
            start = jnp.where(kind >= 0.0, kind * 128.0 + o * 16.0, -1000.0)
            chosen[o * 16 : (o + 1) * 16, :] = jnp.where(entry == start, 1.0, 0.0).astype(BF16)
        rows_out[position] = jnp.dot(chosen[...], table[...], preferred_element_type=F32).astype(BF16)
        return carry

    lax.fori_loop(0, 8, cell, 0)
    mix_out[...] = jnp.zeros_like(mix_out)
    along = lax.broadcasted_iota(jnp.int32, (16, LANES), 1) % 16
    repeat = jnp.where(along == lax.broadcasted_iota(jnp.int32, (16, LANES), 0), 1.0, 0.0).astype(F32)
    for q in range(species):
        wide[q] = jnp.dot(coupling[q], repeat, precision=HIGHEST, preferred_element_type=F32)

    def vertex(v, carry):
        kind = kind_row(kinds, v // 9 + 1, (v // 3) % 3 + 1, v % 3 + 1)
        block = jnp.zeros((16, LANES), F32)
        for q in range(species):
            block = jnp.where(kind == q, wide[q], block)
        block = jnp.where(lane_wide == v % 8, block, 0.0)
        mix_out[v // 8, pl.ds(pl.multiple_of((v % 8) * 16, 16), 16), :] = block
        return carry

    lax.fori_loop(0, 27, vertex, 0)


def first_tables(from_z, up_z, s50, table, coupling):
    species = coupling.shape[0]
    return pl.pallas_call(
        first_tables_kernel,
        out_shape=(shape((125, 8, LANES), F32), shape((8, 128, CELL), BF16), shape((4, LANES, LANES), F32)),
        in_specs=[VMEM] * 5,
        out_specs=(VMEM,) * 3,
        scratch_shapes=[pltpu.VMEM((species, 16, LANES), F32), pltpu.VMEM((128, species * 128), BF16)],
        cost_estimate=cost(1e6, 3e6),
        compiler_params=SMALL,
        name="first_tables",
    )(from_z, up_z, s50, table.reshape(species * 128, CELL), coupling)


def turn_kernel(table, after, out, wide):
    del after
    wide[...] = jnp.zeros_like(wide)
    for q in range(out.shape[0]):
        wide[:, 0:CELL] = table[q].astype(F32)
        out[q] = wide[...].T


def turn(table, after):
    return pl.pallas_call(
        turn_kernel,
        out_shape=shape((table.shape[0], 768, LANES), F32),
        in_specs=[VMEM, pl.BlockSpec(memory_space=pl.ANY)],
        out_specs=VMEM,
        scratch_shapes=[pltpu.VMEM((LANES, 768), F32)],
        cost_estimate=cost(1e6, 3e6),
        compiler_params=SMALL,
        name="turn",
    )(table, after)


def tables_kernel(kinds, table_t, after, columns_out, faces_out, edges_out, points_out, picked):
    del after
    species = table_t.shape[0]
    lane = lax.broadcasted_iota(jnp.int32, (1, LANES), 1) // 16

    def choose(values, lane_kind):
        total = jnp.where(lane_kind == 0, values[0], 0.0)
        for q in range(1, species):
            total = jnp.where(lane_kind == q, values[q], total)
        return total.astype(BF16)

    def cell(position, carry):
        a, b, c = position // 4, (position // 2) % 2, position % 2
        lane_kind = corner_kinds(kinds, a + 1, b + 1, c + 1, lane)
        columns_out[position] = choose([table_t[q, 0:CELL] for q in range(species)], lane_kind)
        return carry

    lax.fori_loop(0, 8, cell, 0)
    for axis in range(3):
        for s in range(2):
            near = 8 - 8 * s
            for q in range(species):
                if axis == 0:
                    picked[q, 0:81] = table_t[q, near * 81 : near * 81 + 81]
                elif axis == 1:
                    for x in range(9):
                        picked[q, x * 9 : x * 9 + 9] = table_t[q, x * 81 + near * 9 : x * 81 + near * 9 + 9]
                else:
                    picked[q, 0:81] = table_t[q, pl.ds(near, 81, stride=9)]

            def face(n, carry, axis=axis, s=s):
                spot = [n // 2 + 1, n % 2 + 1]
                spot.insert(axis, 3 * s)
                lane_kind = corner_kinds(kinds, *spot, lane)
                faces_out[axis * 8 + s * 4 + n] = choose([picked[q, 0:81] for q in range(species)], lane_kind)
                return carry

            lax.fori_loop(0, 4, face, 0)
    for axis in range(3):
        for s in range(2):
            for t in range(2):
                first, second = 8 - 8 * s, 8 - 8 * t
                for u in range(2):
                    spot = [3 * s, 3 * t]
                    spot.insert(axis, u + 1)
                    start, stride = ((first * 9 + second, 81), (first * 81 + second, 9), (first * 81 + second * 9, 1))[axis]
                    lane_kind = corner_kinds(kinds, *spot, lane)
                    place = slice(start, start + 9) if stride == 1 else pl.ds(start, 9, stride=stride)
                    edges_out[axis * 8 + s * 4 + t * 2 + u, 0:9] = choose([table_t[q, place] for q in range(species)], lane_kind)
    for n in range(8):
        s, t, w = n // 4, (n // 2) % 2, n % 2
        at = (8 - 8 * s) * 81 + (8 - 8 * t) * 9 + 8 - 8 * w
        lane_kind = corner_kinds(kinds, 3 * s, 3 * t, 3 * w, lane)
        points_out[n, 0:1] = choose([table_t[q, at : at + 1] for q in range(species)], lane_kind)


def make_tables(kinds, table_t, after):
    species = table_t.shape[0]
    return pl.pallas_call(
        tables_kernel,
        out_shape=(
            shape((8, CELL, LANES), BF16),
            shape((24, 81, LANES), BF16),
            shape((24, 9, LANES), BF16),
            shape((8, 1, LANES), BF16),
        ),
        in_specs=[VMEM, VMEM, pl.BlockSpec(memory_space=pl.ANY)],
        out_specs=(VMEM,) * 4,
        scratch_shapes=[pltpu.VMEM((species, 88, LANES), F32)],
        cost_estimate=cost(1e7, 6e6),
        compiler_params=SMALL,
        name="tables",
    )(kinds, table_t, after)


def first_x_kernel(psi, own, message, up, species_out):
    message[0:256, :] = psi[...].reshape(256, LANES)
    species = [jnp.full((1, LANES), own[n // 4, (n // 2) % 2, n % 2].astype(F32), F32) for n in range(8)]
    blank = jnp.zeros((8, LANES), F32)
    message[256:272, :] = jnp.concatenate(species + [blank], axis=0).astype(BF16)
    up[...] = jnp.concatenate(species[4:] + [blank[0:4]], axis=0)
    species_out[...] = jnp.concatenate(species, axis=0)


def first_x(psi, own):
    return pl.pallas_call(
        first_x_kernel,
        grid=(1,),
        out_shape=(shape((272, LANES), BF16), shape((8, LANES), F32), shape((8, LANES), F32)),
        in_specs=[pl.BlockSpec((1, 16, 16, LANES), lambda n: (0, 0, 0, 0)), SMEM],
        out_specs=(
            pl.BlockSpec((272, LANES), lambda n: (0, 0)),
            pl.BlockSpec((8, LANES), lambda n: (0, 0)),
            pl.BlockSpec((8, LANES), lambda n: (0, 0)),
        ),
        cost_estimate=cost(1e5, 2e5),
        compiler_params=SMALL,
        name="first_x",
    )(pltpu.with_memory_space_constraint(psi, pltpu.HBM), pltpu.with_memory_space_constraint(own, pltpu.HBM))


def first_rows_kernel(psi, rows_y, rows_z, wide, narrow):
    for x in range(16):
        rows_y[x * 16 : x * 16 + 16, :] = psi[x, 0]
    wide[...] = psi[...].reshape(4096, LANES).astype(F32)
    rows = wide[pl.ds(0, 256, stride=16), :]
    narrow[...] = jnp.zeros_like(narrow)
    for x in range(16):
        narrow[x * SIDE : x * SIDE + 16, :] = rows[x * 16 : x * 16 + 16]
    rows_z[...] = narrow[...]


def first_rows(psi):
    return pl.pallas_call(
        first_rows_kernel,
        out_shape=(shape((256, LANES), BF16), shape((FACE, LANES), F32)),
        in_specs=[VMEM],
        out_specs=(VMEM, VMEM),
        scratch_shapes=[pltpu.VMEM((4096, LANES), F32), pltpu.VMEM((FACE, LANES), F32)],
        cost_estimate=cost(1e6, 1.2e6),
        compiler_params=SMALL,
        name="first_rows",
    )(psi)


def first_y_kernel(rows_y, from_x, up_x, own, message, up, s20):
    message[0:256, :] = rows_y[...]
    message[256:272, :] = from_x[0:16, :]
    s20[0:4, :] = up_x[0:4, :]
    s20[4:12, :] = own[...]
    s20[12:20, :] = from_x[256:272, :].astype(F32)[0:8]
    s20[20:32, :] = jnp.zeros((12, LANES), F32)
    message[272:304, :] = s20[...].astype(BF16)
    for x in range(5):
        up[x * 2 : x * 2 + 2, :] = s20[x * 4 + 2 : x * 4 + 4, :]
    up[10:16, :] = jnp.zeros((6, LANES), F32)


def first_y(rows_y, from_x, up_x, own):
    return pl.pallas_call(
        first_y_kernel,
        out_shape=(shape((304, LANES), BF16), shape((16, LANES), F32), shape((32, LANES), F32)),
        in_specs=[VMEM] * 4,
        out_specs=(VMEM,) * 3,
        cost_estimate=cost(1e5, 2e5),
        compiler_params=SMALL,
        name="first_y",
    )(rows_y, from_x, up_x, own)


def first_z_kernel(rows, from_x, from_y, up_y, s20, after, message, up, s50, wide_x, wide_y, face):
    del after
    wide_x[...] = from_x[0:256, :].astype(F32)
    wide_y[...] = from_y[...].astype(F32)
    face[...] = rows[...]
    face[16 * SIDE : 16 * SIDE + 16, :] = wide_x[pl.ds(0, 16, stride=16), :]
    face[pl.ds(16, SIDE, stride=SIDE), :] = wide_y[pl.ds(0, SIDE, stride=16), :]
    message[0:FACE, :] = face[...].astype(BF16)
    for x in range(5):
        s50[x * 10 : x * 10 + 2, :] = up_y[x * 2 : x * 2 + 2, :]
        s50[x * 10 + 2 : x * 10 + 6, :] = s20[x * 4 : x * 4 + 4, :]
        s50[x * 10 + 6 : x * 10 + 10, :] = wide_y[272 + x * 4 : 272 + x * 4 + 4, :]
    s50[50:64, :] = jnp.zeros((14, LANES), F32)
    message[FACE : FACE + 64, :] = s50[...].astype(BF16)
    up[0:25, :] = s50[pl.ds(1, 25, stride=2), :]
    up[25:32, :] = jnp.zeros((7, LANES), F32)


def first_z(rows, from_x, from_y, up_y, s20, after):
    return pl.pallas_call(
        first_z_kernel,
        out_shape=(shape((FACE + 64, LANES), BF16), shape((32, LANES), F32), shape((64, LANES), F32)),
        in_specs=[VMEM] * 5 + [pl.BlockSpec(memory_space=pl.ANY)],
        out_specs=(VMEM,) * 3,
        scratch_shapes=[
            pltpu.VMEM((256, LANES), F32),
            pltpu.VMEM((304, LANES), F32),
            pltpu.VMEM((FACE, LANES), F32),
        ],
        cost_estimate=cost(1e5, 4e5),
        compiler_params=SMALL,
        name="first_z",
    )(rows, from_x, from_y, up_y, s20, after)


def begin_kernel(psi, from_x, from_y, from_z, field_out, field, wide):
    field[...] = jnp.zeros_like(field)

    def slab(x, carry):
        for y in range(16):
            start = pl.multiple_of(x * SLAB + y * ZPAD, 8)
            field[pl.ds(start, 16), :] = psi[x, y].astype(F32)
        return carry

    lax.fori_loop(0, 16, slab, 0)
    for y in range(16):
        at = 16 * SLAB + y * ZPAD
        field[at : at + 16, :] = from_x[y * 16 : y * 16 + 16, :].astype(F32)
    for x in range(SIDE):
        at = x * SLAB + 16 * ZPAD
        field[at : at + 16, :] = from_y[x * 16 : x * 16 + 16, :].astype(F32)
    wide[...] = from_z[0:FACE, :].astype(F32)
    field[pl.ds(16, PLANE, stride=ZPAD), :] = wide[0:PLANE, :]

    def chunk(n, carry):
        spot = pl.ds(pl.multiple_of(n * CHUNK, 16), CHUNK)
        field_out[spot, :] = field[spot, :].astype(BF16)
        return carry

    lax.fori_loop(0, ROWS // CHUNK, chunk, 0)


def begin(psi, from_x, from_y, from_z):
    return pl.pallas_call(
        begin_kernel,
        out_shape=shape((ROWS, LANES), BF16),
        in_specs=[VMEM] * 4,
        out_specs=VMEM,
        scratch_shapes=[pltpu.VMEM((ROWS, LANES), F32), pltpu.VMEM((FACE, LANES), F32)],
        cost_estimate=cost(1e7, 4e6),
        compiler_params=LARGE,
        name="begin",
    )(psi, from_x, from_y, from_z)


HAM_ROWS = 128


def by_cell_kernel(source, after, out, token, wide):
    del after
    token[...] = jnp.zeros_like(token)
    def piece(n, carry):
        for half in range(2):
            spot = pl.ds(pl.multiple_of(n * 32 + half * 16, 16), 16)
            for start in range(0, CELL, LANES):
                width = min(LANES, CELL - start)
                block = wide.at[half, start : start + LANES]
                block[:, 0:width] = source[spot, :, start : start + width].astype(F32).reshape(128, width)
        for half in range(2):
            spot = pl.ds(pl.multiple_of(n * 32 + half * 16, 16), 16)
            for start in range(0, CELL, LANES):
                width = min(LANES, CELL - start)
                block = wide.at[half, start : start + LANES]
                for c in range(8):
                    found = block[pl.ds(c, 16, stride=8), :]
                    out[c, spot, start : start + width] = found[:, 0:width].astype(BF16)
        return carry

    lax.fori_loop(0, HAM_ROWS // 32, piece, 0)


UPPER = 384


def by_cell(ham, first, count, after):
    return pl.pallas_call(
        by_cell_kernel,
        grid=(pl.cdiv(count, HAM_ROWS),),
        out_shape=(shape((8, count, CELL), BF16), shape((8, LANES), F32)),
        in_specs=[
            pl.BlockSpec((HAM_ROWS, 8, CELL), lambda n: (n + first // HAM_ROWS, 0, 0)),
            pl.BlockSpec(memory_space=pl.ANY),
        ],
        out_specs=(
            pl.BlockSpec((8, HAM_ROWS, CELL), lambda n: (0, n, 0)),
            pl.BlockSpec((8, LANES), lambda n: (0, 0)),
        ),
        scratch_shapes=[pltpu.VMEM((2, 768, LANES), F32)],
        cost_estimate=cost(1e7, 9e6),
        compiler_params=LARGE,
        name="by_cell",
    )(pltpu.with_memory_space_constraint(jnp.transpose(ham, (1, 0, 2)), pltpu.HBM), after)


MESSAGE_Y = FACE + 288
MESSAGE_Z = FACE + 480
MESSAGE_X = FACE + 800


def send(odd, low, high, first, second, rows):
    first[rows, :] = jnp.where(odd, low, high).astype(BF16)
    second[rows, :] = jnp.where(odd, high, low).astype(BF16)


def receive(odd, first, second, rows):
    one, two = first[rows, :].astype(F32), second[rows, :].astype(F32)
    return jnp.where(odd, one, two), jnp.where(odd, two, one)


def apply_kernel(full, odd, now, *refs):
    split = len(refs) - 12
    ham, refs = refs[:split], refs[split:]
    rows, mix, terms, send_one, send_two, zface, xface, weights, field, cell32, total, yface = refs
    def chunk(n, carry):
        spot = pl.ds(pl.multiple_of(n * CHUNK, 16), CHUNK)
        field[spot, :] = now[spot, :].astype(F32)
        return carry

    lax.fori_loop(0, ROWS // CHUNK, chunk, 0)
    for ref in (total, xface, yface, zface):
        ref[...] = jnp.zeros_like(ref)

    def cell(position, carry):
        a, b, c = position // 4, (position // 2) % 2, position % 2
        base = cell_base(a, b, c)
        for x in range(9):
            for y in range(9):
                at = (x * 9 + y) * 9
                cell32[at : at + 9, :] = field[pl.ds(line_start(base, x, y), 9), :]
        values = cell32[0:CELL, :].astype(BF16)
        part = jnp.dot(rows[position], values, preferred_element_type=F32)
        for o in range(8):
            i, j, k = o // 4, (o // 2) % 2, o % 2
            vertex = (a + i) * 9 + (b + j) * 3 + c + k
            total[pl.ds(pl.multiple_of(vertex * 16, 16), 16), :] += part[o * 16 : (o + 1) * 16]
        if full:
            for part, spot in zip(ham, (slice(0, UPPER), slice(UPPER, CELL))):
                result = jnp.dot(part[position], values, preferred_element_type=F32)
                terms[position, spot, :] = result
                cell32[spot, :] = result
            sources = (
                cell32.at[pl.ds(pl.multiple_of(a * 648, 8), 88)],
                cell32.at[pl.ds(pl.multiple_of(b * 72, 8), 664)],
                cell32.at[pl.ds(pl.multiple_of(c * 8, 8), 728)],
            )
        else:
            terms[position] = values
            cell32[0:PICKED, :] = jnp.dot(ham[0][position], values, preferred_element_type=F32)
            sources = (cell32, cell32, cell32)
        places = (
            xface.at[pl.ds(pl.multiple_of(a * FACE + b * 136 + c * 8, 8), 152)],
            yface.at[pl.ds(pl.multiple_of(b * FACE + a * 136 + c * 8, 8), 152)],
            zface.at[pl.ds(pl.multiple_of(c * FACE + a * 136 + b * 8, 8), 152)],
        )
        for axis in range(3):
            for n in range(9):
                if not full:
                    spot = slice(axis * 81 + n * 9, axis * 81 + n * 9 + 9)
                elif axis == 0:
                    spot = slice(n * 9, n * 9 + 9)
                elif axis == 1:
                    spot = slice(n * 81, n * 81 + 9)
                else:
                    spot = pl.ds(n * 81, 9, stride=9)
                places[axis][n * SIDE : n * SIDE + 9, :] += sources[axis][spot, :]
        return carry

    lax.fori_loop(0, 8, cell, 0)
    turn = odd[1] == 1
    for g in range(4):
        spot = slice(g * 128, g * 128 + 128)
        total[spot, :] = jnp.dot(mix[g], total[spot, :], precision=HIGHEST, preferred_element_type=F32)
    weights[...] = total[0:432, :]
    send(turn, yface[0:FACE, :], yface[FACE : 2 * FACE, :], send_one, send_two, slice(0, FACE))
    for p in range(2):
        for x in range(3):
            at = FACE + (p * 3 + x) * 48
            down = total[x * 144 + p * 48 : x * 144 + p * 48 + 48, :]
            up = total[x * 144 + (p + 1) * 48 : x * 144 + (p + 1) * 48 + 48, :]
            send(turn, down, up, send_one, send_two, slice(at, at + 48))


def apply_cells(full, odd, now, ham, rows, mix):
    faces = shape((2 * FACE, LANES), F32)
    message = shape((MESSAGE_Y, LANES), BF16)
    return pl.pallas_call(
        functools.partial(apply_kernel, full),
        out_shape=(shape((8, CELL, LANES), F32 if full else BF16), message, message, faces, faces, shape((432, LANES), F32)),
        in_specs=[SMEM] + [VMEM] * (3 + len(ham)),
        out_specs=(VMEM,) * 6,
        scratch_shapes=[
            pltpu.VMEM((ROWS, LANES), F32),
            pltpu.VMEM((736, LANES), F32),
            pltpu.VMEM((512, LANES), F32),
            pltpu.VMEM((2 * FACE, LANES), F32),
        ],
        cost_estimate=cost(1.3e9 if full else 6e8, 1.6e7),
        compiler_params=LARGE,
        name="apply_cells",
    )(odd, now, *ham, rows, mix)


PICKED = 256


def pick_kernel(upper, lower, after, out):
    del after
    row = lax.broadcasted_iota(jnp.int32, (PICKED, 1), 0)
    column = lax.broadcasted_iota(jnp.int32, (PICKED, CELL), 1)

    def cell(position, carry):
        a, b, c = position // 4, (position // 2) % 2, position % 2
        on_y, on_z = row - 81, row - 162
        nine_y, nine_z = lax.shift_right_arithmetic(on_y * 57, 9), lax.shift_right_arithmetic(on_z * 57, 9)
        node = nine_z * 81 + (on_z - nine_z * 9) * 9 + c * 8
        node = jnp.where(row < 162, nine_y * 81 + b * 72 + (on_y - nine_y * 9), node)
        node = jnp.where(row < 81, a * 648 + row, node)
        node = jnp.where(row < 243, node, -1)
        chosen = jnp.where(column == node, 1.0, 0.0).astype(BF16)
        found = jnp.dot(chosen[:, 0:UPPER], upper[position], preferred_element_type=F32)
        found += jnp.dot(chosen[:, UPPER:CELL], lower[position], preferred_element_type=F32)
        out[position] = found.astype(BF16)
        return carry

    lax.fori_loop(0, 8, cell, 0)


def pick(ham, after):
    return pl.pallas_call(
        pick_kernel,
        out_shape=shape((8, PICKED, CELL), BF16),
        in_specs=[VMEM, VMEM, pl.BlockSpec(memory_space=pl.ANY)],
        out_specs=VMEM,
        cost_estimate=cost(2e9, 1.2e7),
        compiler_params=LARGE,
        name="pick",
    )(*ham, after)


def local_kernel(upper, lower, values, terms, token):
    token[...] = jnp.zeros_like(token)

    def cell(position, carry):
        for part, spot in ((upper, slice(0, UPPER)), (lower, slice(UPPER, CELL))):
            terms[position, spot, :] = jnp.dot(part[position], values[position], preferred_element_type=F32)
        return carry

    lax.fori_loop(0, 8, cell, 0)


def local_part(ham, values):
    return pl.pallas_call(
        local_kernel,
        out_shape=(shape((8, CELL, LANES), F32), shape((8, LANES), F32)),
        in_specs=[VMEM] * 3,
        out_specs=(VMEM, VMEM),
        cost_estimate=cost(1.1e9, 1.4e7),
        compiler_params=LARGE,
        name="local_part",
    )(*ham, values)


def assemble_kernel(first, terms, now, *refs):
    before = None if first else refs[0]
    field = refs[-1]
    scale = 1.0 if first else 2.0

    def chunk(n, carry):
        spot = pl.ds(pl.multiple_of(n * CHUNK, 16), CHUNK)
        value = -scale * now[spot, :].astype(F32)
        if before is not None:
            value = value - before[spot, :].astype(F32)
        field[spot, :] = value
        return carry

    lax.fori_loop(0, ROWS // CHUNK, chunk, 0)

    def cell(position, carry):
        a, b, c = position // 4, (position // 2) % 2, position % 2
        base = cell_base(a, b, c)
        for x in range(9):
            for y in range(9):
                at = (x * 9 + y) * 9
                field[pl.ds(line_start(base, x, y), 9), :] += scale * terms[position, at : at + 9, :]
        return carry

    lax.fori_loop(0, 8, cell, 0)


def assemble(terms, now, before):
    args = [terms, now] + ([] if before is None else [before])
    return pl.pallas_call(
        functools.partial(assemble_kernel, before is None),
        out_shape=shape((ROWS, LANES), F32),
        in_specs=[VMEM] * len(args),
        out_specs=VMEM,
        cost_estimate=cost(1e7, 1.2e7),
        compiler_params=SMALL,
        name="assemble",
    )(*args)


def after_y_kernel(odd, one, two, zface, xface, weights, after, send_one, send_two, xface_out, weights_out, low, high, face_low, face_high):
    del after
    low[...], high[...] = receive(odd[1] == 1, one, two, slice(0, FACE))
    turn = odd[2] == 1
    last = 16 * SIDE
    for face, start, column in ((face_low, 0, 0), (face_high, FACE, 16)):
        face[...] = zface[start : start + FACE, :]
        face[pl.ds(0, SIDE, stride=SIDE), :] += low[pl.ds(column, SIDE, stride=SIDE), :]
        face[pl.ds(16, SIDE, stride=SIDE), :] += high[pl.ds(column, SIDE, stride=SIDE), :]
    send(turn, face_low[...], face_high[...], send_one, send_two, slice(0, FACE))
    xface_out[...] = xface[...]
    for start, row in ((0, 0), (FACE, last)):
        xface_out[start : start + SIDE, :] += low[row : row + SIDE, :]
        xface_out[start + last : start + last + SIDE, :] += high[row : row + SIDE, :]
    for x in range(3):
        weights_out[x * 240 + 48 : x * 240 + 192, :] = weights[x * 144 : x * 144 + 144, :]
        for p in range(2):
            at = FACE + (p * 3 + x) * 48
            below, above = receive(odd[1] == 1, one, two, slice(at, at + 48))
            if p == 0:
                weights_out[x * 240 : x * 240 + 48, :] = below
                weights_out[x * 240 + 144 : x * 240 + 192, :] += above
            else:
                weights_out[x * 240 + 48 : x * 240 + 96, :] += below
                weights_out[x * 240 + 192 : x * 240 + 240, :] = above
    for p in range(2):
        for n in range(15):
            at = FACE + (p * 15 + n) * 16
            down = weights_out[n * 48 + p * 16 : n * 48 + p * 16 + 16, :]
            up = weights_out[n * 48 + p * 16 + 16 : n * 48 + p * 16 + 32, :]
            send(turn, down, up, send_one, send_two, slice(at, at + 16))


def after_y(odd, one, two, zface, xface, weights, after):
    message = shape((MESSAGE_Z, LANES), BF16)
    return pl.pallas_call(
        after_y_kernel,
        out_shape=(message, message, shape((2 * FACE, LANES), F32), shape((720, LANES), F32)),
        in_specs=[SMEM] + [VMEM] * 5 + [pl.BlockSpec(memory_space=pl.ANY)],
        out_specs=(VMEM,) * 4,
        scratch_shapes=[pltpu.VMEM((FACE, LANES), F32)] * 4,
        cost_estimate=cost(1e5, 2e6),
        compiler_params=SMALL,
        name="after_y",
    )(odd, one, two, zface, xface, weights, after)


def after_z_kernel(odd, one, two, xface, weights, send_one, send_two, weights_out, low, high, face_low, face_high):
    low[...], high[...] = receive(odd[2] == 1, one, two, slice(0, FACE))
    turn = odd[0] == 1
    for face, start, row in ((face_low, 0, 0), (face_high, FACE, 16 * SIDE)):
        face[...] = xface[start : start + FACE, :]
        face[pl.ds(0, SIDE, stride=SIDE), :] += low[row : row + SIDE, :]
        face[pl.ds(16, SIDE, stride=SIDE), :] += high[row : row + SIDE, :]
    send(turn, face_low[...], face_high[...], send_one, send_two, slice(0, FACE))
    for n in range(15):
        weights_out[n * 80 + 16 : n * 80 + 64, :] = weights[n * 48 : n * 48 + 48, :]
        for p in range(2):
            at = FACE + (p * 15 + n) * 16
            below, above = receive(odd[2] == 1, one, two, slice(at, at + 16))
            if p == 0:
                weights_out[n * 80 : n * 80 + 16, :] = below
                weights_out[n * 80 + 48 : n * 80 + 64, :] += above
            else:
                weights_out[n * 80 + 16 : n * 80 + 32, :] += below
                weights_out[n * 80 + 64 : n * 80 + 80, :] = above
    for p in range(2):
        at = FACE + p * 400
        down, up = weights_out[p * 400 : p * 400 + 400, :], weights_out[p * 400 + 400 : p * 400 + 800, :]
        send(turn, down, up, send_one, send_two, slice(at, at + 400))


def after_z(odd, one, two, xface, weights):
    message = shape((MESSAGE_X, LANES), BF16)
    return pl.pallas_call(
        after_z_kernel,
        out_shape=(message, message, shape((1200, LANES), F32)),
        in_specs=[SMEM] + [VMEM] * 4,
        out_specs=(VMEM,) * 3,
        scratch_shapes=[pltpu.VMEM((FACE, LANES), F32)] * 4,
        cost_estimate=cost(1e5, 2e6),
        compiler_params=SMALL,
        name="after_z",
    )(odd, one, two, xface, weights)


def corner_weights(weights, a, b, c):
    pieces = []
    for o in range(8):
        i, j, k = o // 4, (o // 2) % 2, o % 2
        vertex = ((a + i) * 5 + b + j) * 5 + c + k
        pieces.append(weights[pl.ds(pl.multiple_of(vertex * 16, 16), 16), :])
    return jnp.concatenate(pieces, axis=0)


def advance_kernel(first, last, odd, start_field, y1, y2, z1, z2, x1, x2, w75, columns, faces, edges, points, out, *refs):
    del start_field
    parts = refs[: len(refs) - 6]
    field, cell32, weights, xs, ys, zs = refs[len(refs) - 6 :]
    scale = 1.0 if first else 2.0
    for ref, one, two, axis in ((xs, x1, x2, 0), (ys, y1, y2, 1), (zs, z1, z2, 2)):
        low, high = receive(odd[axis] == 1, one, two, slice(0, FACE))
        ref[0:FACE, :] = low
        ref[FACE : 2 * FACE, :] = high
    for p in range(2):
        at = FACE + p * 400
        below, above = receive(odd[0] == 1, x1, x2, slice(at, at + 400))
        if p == 0:
            weights[0:400, :] = below.astype(BF16)
            weights[1200:1600, :] = (w75[800:1200, :] + above).astype(BF16)
        else:
            weights[400:800, :] = (w75[0:400, :] + below).astype(BF16)
            weights[1600:2000, :] = above.astype(BF16)
    weights[800:1200, :] = w75[400:800, :].astype(BF16)

    def cell(position, carry):
        a, b, c = position // 4, (position // 2) % 2, position % 2
        corner = corner_weights(weights, a + 1, b + 1, c + 1)
        cell32[0:CELL, :] = scale * jnp.dot(columns[position], corner, preferred_element_type=F32)
        base = cell_base(a, b, c)
        for x in range(9):
            for y in range(9):
                at = (x * 9 + y) * 9
                field[pl.ds(line_start(base, x, y), 9), :] += cell32[at : at + 9, :]
        return carry

    lax.fori_loop(0, 8, cell, 0)

    for axis, ref in enumerate((xs, ys, zs)):

        def face(s, carry, axis=axis, ref=ref):
            for n in range(4):
                spot = [n // 2 + 1, n % 2 + 1]
                spot.insert(axis, 3 * s)
                cell32[n * 88 : n * 88 + 81, :] = jnp.dot(
                    faces[axis * 8 + s * 4 + n], corner_weights(weights, *spot), preferred_element_type=F32
                )
            for n in range(4):
                view = ref.at[pl.ds(pl.multiple_of(s * FACE + (n // 2) * 136 + (n % 2) * 8, 8), 152)]
                for row in range(9):
                    at = n * 88 + row * 9
                    view[row * SIDE : row * SIDE + 9, :] += cell32[at : at + 9, :]
            return carry

        lax.fori_loop(0, 2, face, 0)

    for axis in range(3):

        def edge(s, carry, axis=axis):
            terms = []
            for n in range(4):
                spot = [3 * s, 3 * (n // 2)]
                spot.insert(axis, n % 2 + 1)
                terms.append(
                    jnp.dot(edges[axis * 8 + s * 4 + n], corner_weights(weights, *spot), preferred_element_type=F32)
                )
            for n, term in enumerate(terms):
                t, u = n // 2, n % 2
                if axis == 2:
                    view = xs.at[pl.ds(pl.multiple_of(s * FACE + t * 272 + u * 8, 8), 16)]
                    view[0:9, :] += term
                else:
                    ref = xs if axis == 1 else ys
                    view = ref.at[pl.ds(pl.multiple_of(s * FACE + u * 136 + t * 16, 8), 152)]
                    view[pl.ds(0, 9, stride=SIDE), :] += term
            return carry

        lax.fori_loop(0, 2, edge, 0)

    def point(s, carry):
        terms = []
        for n in range(4):
            corner = corner_weights(weights, 3 * s, 3 * (n // 2), 3 * (n % 2))
            terms.append(jnp.dot(points[s * 4 + n], corner, preferred_element_type=F32))
        for n, term in enumerate(terms):
            view = xs.at[pl.ds(pl.multiple_of(s * FACE + (n // 2) * 272 + (n % 2) * 16, 8), 8)]
            view[0:1, :] += term
        return carry

    lax.fori_loop(0, 2, point, 0)

    for s in range(2):
        for y in range(SIDE):
            at = s * 16 * SLAB + y * ZPAD
            field[at : at + SIDE, :] += scale * xs[s * FACE + y * SIDE : s * FACE + (y + 1) * SIDE, :]
        for x in range(SIDE):
            at = s * 16 * ZPAD + x * SLAB
            field[at : at + SIDE, :] += scale * ys[s * FACE + x * SIDE : s * FACE + (x + 1) * SIDE, :]
        field[pl.ds(s * 16, PLANE, stride=ZPAD), :] += scale * zs[s * FACE : s * FACE + PLANE, :]

    if last:

        def slab(x, carry):
            for y in range(16):
                start = pl.multiple_of(x * SLAB + y * ZPAD, 8)
                out[x, y] = field[pl.ds(start, 16), :].astype(BF16)
            return carry

        lax.fori_loop(0, 16, slab, 0)
        for offset, part in enumerate(parts):
            quarter = (odd[3] + offset) % 4
            part[...] = out[pl.ds(quarter * 4, 4)].reshape(1024, LANES)
    else:

        def chunk(n, carry):
            spot = pl.ds(pl.multiple_of(n * CHUNK, 16), CHUNK)
            out[spot, :] = field[spot, :].astype(BF16)
            return carry

        lax.fori_loop(0, ROWS // CHUNK, chunk, 0)


def advance(odd, field, messages, w75, tables, first, last):
    args = [odd, field, *messages, w75, *tables]
    if last:
        outs = [shape((16, 16, 16, LANES), BF16)] + [shape((1024, LANES), BF16)] * 4
    else:
        outs = [shape((ROWS, LANES), BF16)]
    outs.append(shape((ROWS, LANES), F32))
    return pl.pallas_call(
        functools.partial(advance_kernel, first, last),
        out_shape=tuple(outs),
        in_specs=[SMEM] + [VMEM] * (len(args) - 1),
        out_specs=(VMEM,) * len(outs),
        input_output_aliases={1: len(outs) - 1},
        scratch_shapes=[pltpu.VMEM((736, LANES), F32), pltpu.VMEM((2000, LANES), BF16)]
        + [pltpu.VMEM((2 * FACE, LANES), F32)] * 3,
        cost_estimate=cost(3e8, 1.2e7),
        compiler_params=LARGE,
        name="advance",
    )(*args)[:-1]


def gram_kernel(x0, x1, x2, x3, own, m1, m2, m3):
    blocks = [x0[...], x1[...], x2[...], x3[...]]
    for row, left in enumerate(blocks):
        turned = left.T
        for column, out in ((0, own), (3, m1), (2, m2), (1, m3)):
            part = jnp.dot(turned, blocks[column], preferred_element_type=F32)
            out[row * 128 : row * 128 + 128, :] = part.astype(out.dtype)


def gram(blocks):
    return pl.pallas_call(
        gram_kernel,
        out_shape=(shape((512, LANES), F32),) + (shape((512, LANES), BF16),) * 3,
        in_specs=[VMEM] * 4,
        out_specs=(VMEM,) * 4,
        cost_estimate=cost(6e8, 2e6),
        compiler_params=LARGE,
        name="gram",
    )(*blocks)


def collect_kernel(band, own, m1, m2, m3, out):
    for row in range(4):
        total = own[row * 128 : row * 128 + 128, :]
        for offset, ref in ((1, m1), (2, m2), (3, m3)):
            source = (row - offset) % 4
            total = total + ref[source * 128 : source * 128 + 128, :].astype(F32)
        place = (band[0] + 4 - row) % 4
        out[pl.ds(place * 16, 16)] = total.reshape(16, 8, LANES).astype(BF16)


def collect(band, own, received):
    return pl.pallas_call(
        collect_kernel,
        out_shape=shape((64, 8, LANES), BF16),
        in_specs=[SMEM] + [VMEM] * 4,
        out_specs=VMEM,
        cost_estimate=cost(1e6, 1e6),
        compiler_params=SMALL,
        name="collect",
    )(band, own, *received)


def total_kernel(scale, terms, out):
    out[...] = jnp.sum(terms[...].astype(F32), axis=0) * scale


def total(terms, scale):
    return pl.pallas_call(
        functools.partial(total_kernel, scale),
        out_shape=shape(terms.shape[1:], F32),
        in_specs=[VMEM],
        out_specs=VMEM,
        cost_estimate=cost(1e5, 2e5),
        compiler_params=SMALL,
        name="total",
    )(terms)


def local(psi, cell_ham, proj_table, coupling, atom_kind):
    devices = lax.axis_size("cells")
    side = cube_root(devices)
    offsets = (1, side, side * side)
    block = lax.axis_index("cells")
    band = lax.axis_index("bands")
    odd = jnp.stack([(block // offset) % 2 for offset in offsets] + [band]).astype(jnp.int32)

    def upward(x, axis):
        return shifted(x, "cells", offsets[axis])

    def downward(x, axis):
        return shifted(x, "cells", -offsets[axis])

    def swap(messages, axis):
        offset = offsets[axis]
        arrived = []
        for start, message in enumerate(messages):
            pairs = []
            for i in range(devices):
                forward = (i // offset) % 2 == start
                pairs.append((i, (i + offset) % devices if forward else (i - offset) % devices))
            arrived.append(lax.ppermute(message, "cells", pairs))
        return arrived

    message, up, own = first_x(psi, atom_kind)
    from_x, up_x = downward(message, 0), upward(up, 0)
    rows_y, rows_z = first_rows(psi)
    message, up, s20 = first_y(rows_y, from_x, up_x, own)
    from_y, up_y = downward(message, 1), upward(up, 1)
    upper, token = by_cell(cell_ham, 0, UPPER, s20)
    message, up, s50 = first_z(rows_z, from_x, from_y, up_y, s20, token)
    from_z, up_z = downward(message, 2), upward(up, 2)
    lower, _ = by_cell(cell_ham, UPPER, CELL - UPPER, s50)
    ham = (upper, lower)
    table = proj_table.reshape(4, 128, CELL)
    kinds, rows, mix = first_tables(from_z, up_z, s50, table, coupling)

    def step(now, before, last, tables):
        first = tables is None
        terms, one, two, zface, xface, weights = apply_cells(
            first, odd, now, ham if first else (tables[-1],), rows, mix
        )
        ys = swap((one, two), 1)
        if first:
            picked = pick(ham, weights)
            token = picked
            tables = (*make_tables(kinds, turn(table, weights), weights), picked)
        else:
            terms, token = local_part(ham, terms)
        field = assemble(terms, now, before)
        one, two, xface, weights = after_y(odd, *ys, zface, xface, weights, token)
        zs = swap((one, two), 2)
        one, two, weights = after_z(odd, *zs, xface, weights)
        xs = swap((one, two), 0)
        return tables, advance(odd, field, (*ys, *zs, *xs), weights, tables[:4], before is None, last)

    y0 = begin(psi, from_x, from_y, from_z)
    tables, (y1,) = step(y0, None, False, None)
    tables, (y2,) = step(y1, y0, False, tables)
    tables, (filtered, *blocks) = step(y2, y1, True, tables)

    two = shifted(blocks[2], "bands", 2)
    blocks = [blocks[0], shifted(blocks[1], "bands", 1), two, shifted(blocks[3], "bands", 3)]
    own, *messages = gram(blocks)
    messages = [shifted(message, "bands", n + 1) for n, message in enumerate(messages)]
    terms = collect(band.astype(jnp.int32).reshape(1), own, messages)
    terms = lax.all_to_all(terms, "cells", 0, 0)
    inverse_count = 1.0 / (4096 * devices)
    correlation = total(terms, inverse_count)
    return filtered, correlation


def solution(mesh):
    in_specs = (
        P("cells", None, None, "bands"),
        P("cells", None, None),
        P(),
        P(),
        P("cells", None, None),
    )
    out_specs = (P("cells", None, None, "bands"), P("cells", "bands"))
    return jax.shard_map(local, mesh=mesh, in_specs=in_specs, out_specs=out_specs, check_vma=False)
```

```python
import functools

import jax
import jax.numpy as jnp
from jax import lax
from jax.experimental import pallas as pl
from jax.experimental.pallas import tpu as pltpu
from jax.sharding import PartitionSpec as P


F32 = jnp.float32
BF16 = jnp.bfloat16
HIGHEST = lax.Precision.HIGHEST

SIDE = 17
ZPAD = 24
SLAB = SIDE * ZPAD
ROWS = 6944
CHUNK = 496
FACE = 304
PLANE = SIDE * SIDE
CELL = 729
LANES = 128


def shifted(x, axis, by):
    devices = lax.axis_size(axis)
    return lax.ppermute(x, axis, [(i, (i + by) % devices) for i in range(devices)])


def cube_root(amount):
    result = 1
    while (result + 1) ** 3 <= amount:
        result = result + 1
    return result


def cost(flops, nbytes):
    return pl.CostEstimate(flops=int(flops), bytes_accessed=int(nbytes), transcendentals=0)


def shape(dims, dtype):
    return jax.ShapeDtypeStruct(dims, dtype)


VMEM = pl.BlockSpec(memory_space=pltpu.VMEM)
LARGE = pltpu.CompilerParams(vmem_limit_bytes=10 * 2**20)
SMALL = pltpu.CompilerParams(vmem_limit_bytes=6 * 2**20)
SMEM = pl.BlockSpec(memory_space=pltpu.SMEM)


def cell_base(a, b, c):
    return a * (8 * SLAB) + b * (8 * ZPAD) + c * 8


def line_start(base, x, y):
    return pl.multiple_of(base + (x * SLAB + y * ZPAD), 8)


def kind_row(kinds, a, b, c):
    return kinds[(a * 5 + b) * 5 + c][0:1, :]


def corner_kinds(kinds, a, b, c, lane):
    found = jnp.full((1, LANES), -1.0, F32)
    for o in range(8):
        i, j, k = o // 4, (o // 2) % 2, o % 2
        found = jnp.where(lane == o, kind_row(kinds, a + i, b + j, c + k), found)
    return found


def first_tables_kernel(from_z, up_z, s50, table, coupling, kinds, rows_out, mix_out, wide, table32):
    for n in range(25):
        kinds[n * 5] = jnp.broadcast_to(up_z[n : n + 1, :], (8, LANES))
        for k in range(2):
            at = n * 2 + k
            kinds[n * 5 + 1 + k] = jnp.broadcast_to(s50[at : at + 1, :], (8, LANES))
    above = from_z[FACE : FACE + 64, :].astype(F32)
    for n in range(50):
        kinds[(n // 2) * 5 + 3 + n % 2] = jnp.broadcast_to(above[n : n + 1, :], (8, LANES))
    species = coupling.shape[0]
    lane_wide = lax.broadcasted_iota(jnp.int32, (16, LANES), 1) // 16
    for q in range(species):
        table32[q] = table[q].astype(F32)

    def cell(position, carry):
        a, b, c = position // 4, (position // 2) % 2, position % 2
        for o in range(8):
            i, j, k = o // 4, (o // 2) % 2, o % 2
            kind = kind_row(kinds, a + i + 1, b + j + 1, c + k + 1)[:, 0:1]
            block = jnp.zeros((16, CELL), F32)
            for q in range(species):
                block = jnp.where(kind == q, table32[q, o * 16 : (o + 1) * 16, :], block)
            rows_out[position, o * 16 : (o + 1) * 16, :] = block.astype(BF16)
        return carry

    lax.fori_loop(0, 8, cell, 0)
    mix_out[...] = jnp.zeros_like(mix_out)
    along = lax.broadcasted_iota(jnp.int32, (16, LANES), 1) % 16
    repeat = jnp.where(along == lax.broadcasted_iota(jnp.int32, (16, LANES), 0), 1.0, 0.0).astype(F32)
    for q in range(species):
        wide[q] = jnp.dot(coupling[q], repeat, precision=HIGHEST, preferred_element_type=F32)

    def vertex(v, carry):
        kind = kind_row(kinds, v // 9 + 1, (v // 3) % 3 + 1, v % 3 + 1)
        block = jnp.zeros((16, LANES), F32)
        for q in range(species):
            block = jnp.where(kind == q, wide[q], block)
        block = jnp.where(lane_wide == v % 8, block, 0.0)
        mix_out[v // 8, pl.ds(pl.multiple_of((v % 8) * 16, 16), 16), :] = block
        return carry

    lax.fori_loop(0, 27, vertex, 0)


def first_tables(from_z, up_z, s50, table, coupling):
    species = coupling.shape[0]
    return pl.pallas_call(
        first_tables_kernel,
        out_shape=(shape((125, 8, LANES), F32), shape((8, 128, CELL), BF16), shape((4, LANES, LANES), F32)),
        in_specs=[VMEM] * 5,
        out_specs=(VMEM,) * 3,
        scratch_shapes=[pltpu.VMEM((species, 16, LANES), F32), pltpu.VMEM((species, 128, CELL), F32)],
        cost_estimate=cost(1e6, 3e6),
        compiler_params=SMALL,
        name="first_tables",
    )(from_z, up_z, s50, table, coupling)


def turn_kernel(table, after, out, wide):
    del after
    wide[...] = jnp.zeros_like(wide)
    for q in range(out.shape[0]):
        wide[:, 0:CELL] = table[q].astype(F32)
        out[q] = wide[...].T


def turn(table, after):
    return pl.pallas_call(
        turn_kernel,
        out_shape=shape((table.shape[0], 768, LANES), F32),
        in_specs=[VMEM, pl.BlockSpec(memory_space=pl.ANY)],
        out_specs=VMEM,
        scratch_shapes=[pltpu.VMEM((LANES, 768), F32)],
        cost_estimate=cost(1e6, 3e6),
        compiler_params=SMALL,
        name="turn",
    )(table, after)


def tables_kernel(kinds, table_t, after, columns_out, faces_out, edges_out, points_out, picked):
    del after
    species = table_t.shape[0]
    lane = lax.broadcasted_iota(jnp.int32, (1, LANES), 1) // 16

    def choose(values, lane_kind):
        total = jnp.where(lane_kind == 0, values[0], 0.0)
        for q in range(1, species):
            total = jnp.where(lane_kind == q, values[q], total)
        return total.astype(BF16)

    def cell(position, carry):
        a, b, c = position // 4, (position // 2) % 2, position % 2
        lane_kind = corner_kinds(kinds, a + 1, b + 1, c + 1, lane)
        columns_out[position] = choose([table_t[q, 0:CELL] for q in range(species)], lane_kind)
        return carry

    lax.fori_loop(0, 8, cell, 0)
    for axis in range(3):
        for s in range(2):
            near = 8 - 8 * s
            for q in range(species):
                if axis == 0:
                    picked[q, 0:81] = table_t[q, near * 81 : near * 81 + 81]
                elif axis == 1:
                    for x in range(9):
                        picked[q, x * 9 : x * 9 + 9] = table_t[q, x * 81 + near * 9 : x * 81 + near * 9 + 9]
                else:
                    picked[q, 0:81] = table_t[q, pl.ds(near, 81, stride=9)]

            def face(n, carry, axis=axis, s=s):
                spot = [n // 2 + 1, n % 2 + 1]
                spot.insert(axis, 3 * s)
                lane_kind = corner_kinds(kinds, *spot, lane)
                faces_out[axis * 8 + s * 4 + n] = choose([picked[q, 0:81] for q in range(species)], lane_kind)
                return carry

            lax.fori_loop(0, 4, face, 0)
    for axis in range(3):
        for s in range(2):
            for t in range(2):
                first, second = 8 - 8 * s, 8 - 8 * t
                for u in range(2):
                    spot = [3 * s, 3 * t]
                    spot.insert(axis, u + 1)
                    start, stride = ((first * 9 + second, 81), (first * 81 + second, 9), (first * 81 + second * 9, 1))[axis]
                    lane_kind = corner_kinds(kinds, *spot, lane)
                    place = slice(start, start + 9) if stride == 1 else pl.ds(start, 9, stride=stride)
                    edges_out[axis * 8 + s * 4 + t * 2 + u, 0:9] = choose([table_t[q, place] for q in range(species)], lane_kind)
    for n in range(8):
        s, t, w = n // 4, (n // 2) % 2, n % 2
        at = (8 - 8 * s) * 81 + (8 - 8 * t) * 9 + 8 - 8 * w
        lane_kind = corner_kinds(kinds, 3 * s, 3 * t, 3 * w, lane)
        points_out[n, 0:1] = choose([table_t[q, at : at + 1] for q in range(species)], lane_kind)


def make_tables(kinds, table_t, after):
    species = table_t.shape[0]
    return pl.pallas_call(
        tables_kernel,
        out_shape=(
            shape((8, CELL, LANES), BF16),
            shape((24, 81, LANES), BF16),
            shape((24, 9, LANES), BF16),
            shape((8, 1, LANES), BF16),
        ),
        in_specs=[VMEM, VMEM, pl.BlockSpec(memory_space=pl.ANY)],
        out_specs=(VMEM,) * 4,
        scratch_shapes=[pltpu.VMEM((species, 88, LANES), F32)],
        cost_estimate=cost(1e7, 6e6),
        compiler_params=SMALL,
        name="tables",
    )(kinds, table_t, after)


def first_x_kernel(psi, own, message, up, species_out):
    message[0:256, :] = psi[...].reshape(256, LANES)
    species = [jnp.full((1, LANES), own[n // 4, (n // 2) % 2, n % 2].astype(F32), F32) for n in range(8)]
    blank = jnp.zeros((8, LANES), F32)
    message[256:272, :] = jnp.concatenate(species + [blank], axis=0).astype(BF16)
    up[...] = jnp.concatenate(species[4:] + [blank[0:4]], axis=0)
    species_out[...] = jnp.concatenate(species, axis=0)


def first_x(psi, own):
    return pl.pallas_call(
        first_x_kernel,
        grid=(1,),
        out_shape=(shape((272, LANES), BF16), shape((8, LANES), F32), shape((8, LANES), F32)),
        in_specs=[pl.BlockSpec((1, 16, 16, LANES), lambda n: (0, 0, 0, 0)), SMEM],
        out_specs=(
            pl.BlockSpec((272, LANES), lambda n: (0, 0)),
            pl.BlockSpec((8, LANES), lambda n: (0, 0)),
            pl.BlockSpec((8, LANES), lambda n: (0, 0)),
        ),
        cost_estimate=cost(1e5, 2e5),
        compiler_params=SMALL,
        name="first_x",
    )(pltpu.with_memory_space_constraint(psi, pltpu.HBM), pltpu.with_memory_space_constraint(own, pltpu.HBM))


def first_rows_kernel(psi, rows_y, rows_z, wide, narrow):
    for x in range(16):
        rows_y[x * 16 : x * 16 + 16, :] = psi[x, 0]
    wide[...] = psi[...].reshape(4096, LANES).astype(F32)
    rows = wide[pl.ds(0, 256, stride=16), :]
    narrow[...] = jnp.zeros_like(narrow)
    for x in range(16):
        narrow[x * SIDE : x * SIDE + 16, :] = rows[x * 16 : x * 16 + 16]
    rows_z[...] = narrow[...]


def first_rows(psi):
    return pl.pallas_call(
        first_rows_kernel,
        out_shape=(shape((256, LANES), BF16), shape((FACE, LANES), F32)),
        in_specs=[VMEM],
        out_specs=(VMEM, VMEM),
        scratch_shapes=[pltpu.VMEM((4096, LANES), F32), pltpu.VMEM((FACE, LANES), F32)],
        cost_estimate=cost(1e6, 1.2e6),
        compiler_params=SMALL,
        name="first_rows",
    )(psi)


def first_y_kernel(rows_y, from_x, up_x, own, message, up, s20):
    message[0:256, :] = rows_y[...]
    message[256:272, :] = from_x[0:16, :]
    s20[0:4, :] = up_x[0:4, :]
    s20[4:12, :] = own[...]
    s20[12:20, :] = from_x[256:272, :].astype(F32)[0:8]
    s20[20:32, :] = jnp.zeros((12, LANES), F32)
    message[272:304, :] = s20[...].astype(BF16)
    for x in range(5):
        up[x * 2 : x * 2 + 2, :] = s20[x * 4 + 2 : x * 4 + 4, :]
    up[10:16, :] = jnp.zeros((6, LANES), F32)


def first_y(rows_y, from_x, up_x, own):
    return pl.pallas_call(
        first_y_kernel,
        out_shape=(shape((304, LANES), BF16), shape((16, LANES), F32), shape((32, LANES), F32)),
        in_specs=[VMEM] * 4,
        out_specs=(VMEM,) * 3,
        cost_estimate=cost(1e5, 2e5),
        compiler_params=SMALL,
        name="first_y",
    )(rows_y, from_x, up_x, own)


def first_z_kernel(rows, from_x, from_y, up_y, s20, after, message, up, s50, wide_x, wide_y, face):
    del after
    wide_x[...] = from_x[0:256, :].astype(F32)
    wide_y[...] = from_y[...].astype(F32)
    face[...] = rows[...]
    face[16 * SIDE : 16 * SIDE + 16, :] = wide_x[pl.ds(0, 16, stride=16), :]
    face[pl.ds(16, SIDE, stride=SIDE), :] = wide_y[pl.ds(0, SIDE, stride=16), :]
    message[0:FACE, :] = face[...].astype(BF16)
    for x in range(5):
        s50[x * 10 : x * 10 + 2, :] = up_y[x * 2 : x * 2 + 2, :]
        s50[x * 10 + 2 : x * 10 + 6, :] = s20[x * 4 : x * 4 + 4, :]
        s50[x * 10 + 6 : x * 10 + 10, :] = wide_y[272 + x * 4 : 272 + x * 4 + 4, :]
    s50[50:64, :] = jnp.zeros((14, LANES), F32)
    message[FACE : FACE + 64, :] = s50[...].astype(BF16)
    up[0:25, :] = s50[pl.ds(1, 25, stride=2), :]
    up[25:32, :] = jnp.zeros((7, LANES), F32)


def first_z(rows, from_x, from_y, up_y, s20, after):
    return pl.pallas_call(
        first_z_kernel,
        out_shape=(shape((FACE + 64, LANES), BF16), shape((32, LANES), F32), shape((64, LANES), F32)),
        in_specs=[VMEM] * 5 + [pl.BlockSpec(memory_space=pl.ANY)],
        out_specs=(VMEM,) * 3,
        scratch_shapes=[
            pltpu.VMEM((256, LANES), F32),
            pltpu.VMEM((304, LANES), F32),
            pltpu.VMEM((FACE, LANES), F32),
        ],
        cost_estimate=cost(1e5, 4e5),
        compiler_params=SMALL,
        name="first_z",
    )(rows, from_x, from_y, up_y, s20, after)


def begin_kernel(psi, from_x, from_y, from_z, field_out, field, wide):
    field[...] = jnp.zeros_like(field)

    def slab(x, carry):
        for y in range(16):
            start = pl.multiple_of(x * SLAB + y * ZPAD, 8)
            field[pl.ds(start, 16), :] = psi[x, y].astype(F32)
        return carry

    lax.fori_loop(0, 16, slab, 0)
    for y in range(16):
        at = 16 * SLAB + y * ZPAD
        field[at : at + 16, :] = from_x[y * 16 : y * 16 + 16, :].astype(F32)
    for x in range(SIDE):
        at = x * SLAB + 16 * ZPAD
        field[at : at + 16, :] = from_y[x * 16 : x * 16 + 16, :].astype(F32)
    wide[...] = from_z[0:FACE, :].astype(F32)
    field[pl.ds(16, PLANE, stride=ZPAD), :] = wide[0:PLANE, :]

    def chunk(n, carry):
        spot = pl.ds(pl.multiple_of(n * CHUNK, 16), CHUNK)
        field_out[spot, :] = field[spot, :].astype(BF16)
        return carry

    lax.fori_loop(0, ROWS // CHUNK, chunk, 0)


def begin(psi, from_x, from_y, from_z):
    return pl.pallas_call(
        begin_kernel,
        out_shape=shape((ROWS, LANES), BF16),
        in_specs=[VMEM] * 4,
        out_specs=VMEM,
        scratch_shapes=[pltpu.VMEM((ROWS, LANES), F32), pltpu.VMEM((FACE, LANES), F32)],
        cost_estimate=cost(1e7, 4e6),
        compiler_params=LARGE,
        name="begin",
    )(psi, from_x, from_y, from_z)


HAM_ROWS = 128


def by_cell_kernel(source, after, out, token, wide):
    del after
    token[...] = jnp.zeros_like(token)
    def piece(n, carry):
        for half in range(2):
            spot = pl.ds(pl.multiple_of(n * 32 + half * 16, 16), 16)
            for start in range(0, CELL, LANES):
                width = min(LANES, CELL - start)
                block = wide.at[half, start : start + LANES]
                block[:, 0:width] = source[spot, :, start : start + width].astype(F32).reshape(128, width)
        for half in range(2):
            spot = pl.ds(pl.multiple_of(n * 32 + half * 16, 16), 16)
            for start in range(0, CELL, LANES):
                width = min(LANES, CELL - start)
                block = wide.at[half, start : start + LANES]
                for c in range(8):
                    found = block[pl.ds(c, 16, stride=8), :]
                    out[c, spot, start : start + width] = found[:, 0:width].astype(BF16)
        return carry

    lax.fori_loop(0, HAM_ROWS // 32, piece, 0)


UPPER = 384


def by_cell(ham, first, count, after):
    return pl.pallas_call(
        by_cell_kernel,
        grid=(pl.cdiv(count, HAM_ROWS),),
        out_shape=(shape((8, count, CELL), BF16), shape((8, LANES), F32)),
        in_specs=[
            pl.BlockSpec((HAM_ROWS, 8, CELL), lambda n: (n + first // HAM_ROWS, 0, 0)),
            pl.BlockSpec(memory_space=pl.ANY),
        ],
        out_specs=(
            pl.BlockSpec((8, HAM_ROWS, CELL), lambda n: (0, n, 0)),
            pl.BlockSpec((8, LANES), lambda n: (0, 0)),
        ),
        scratch_shapes=[pltpu.VMEM((2, 768, LANES), F32)],
        cost_estimate=cost(1e7, 9e6),
        compiler_params=LARGE,
        name="by_cell",
    )(pltpu.with_memory_space_constraint(jnp.transpose(ham, (1, 0, 2)), pltpu.HBM), after)


MESSAGE_Y = FACE + 288
MESSAGE_Z = FACE + 480
MESSAGE_X = FACE + 800


def send(odd, low, high, first, second, rows):
    first[rows, :] = jnp.where(odd, low, high).astype(BF16)
    second[rows, :] = jnp.where(odd, high, low).astype(BF16)


def receive(odd, first, second, rows):
    one, two = first[rows, :].astype(F32), second[rows, :].astype(F32)
    return jnp.where(odd, one, two), jnp.where(odd, two, one)


def apply_kernel(full, odd, now, *refs):
    split = len(refs) - 12
    ham, refs = refs[:split], refs[split:]
    rows, mix, terms, send_one, send_two, zface, xface, weights, field, cell32, total, yface = refs
    def chunk(n, carry):
        spot = pl.ds(pl.multiple_of(n * CHUNK, 16), CHUNK)
        field[spot, :] = now[spot, :].astype(F32)
        return carry

    lax.fori_loop(0, ROWS // CHUNK, chunk, 0)
    for ref in (total, xface, yface, zface):
        ref[...] = jnp.zeros_like(ref)

    def pair(n, carry):
        staged = [cell32.at[0:736], cell32.at[736:1472]]
        loaded = []
        for h, stage in enumerate(staged):
            base = cell_base(n // 2, n % 2, h)
            for x in range(9):
                for y in range(9):
                    at = (x * 9 + y) * 9
                    stage[at : at + 9, :] = field[pl.ds(line_start(base, x, y), 9), :]
            loaded.append(stage[0:CELL, :].astype(BF16))
        for h, (stage, values) in enumerate(zip(staged, loaded)):
            position, a, b, c = n * 2 + h, n // 2, n % 2, h
            part = jnp.dot(rows[position], values, preferred_element_type=F32)
            for o in range(8):
                i, j, k = o // 4, (o // 2) % 2, o % 2
                vertex = (a + i) * 9 + (b + j) * 3 + c + k
                total[pl.ds(pl.multiple_of(vertex * 16, 16), 16), :] += part[o * 16 : (o + 1) * 16]
            if full:
                for block, spot in zip(ham, (slice(0, UPPER), slice(UPPER, CELL))):
                    result = jnp.dot(block[position], values, preferred_element_type=F32)
                    terms[position, spot, :] = result
                    stage[spot, :] = result
            else:
                terms[position] = values
                stage[0:PICKED, :] = jnp.dot(ham[0][position], values, preferred_element_type=F32)
        for h, stage in enumerate(staged):
            a, b, c = n // 2, n % 2, h
            sources = (stage, stage, stage)
            if full:
                sources = (
                    stage.at[pl.ds(pl.multiple_of(a * 648, 8), 88)],
                    stage.at[pl.ds(pl.multiple_of(b * 72, 8), 664)],
                    stage.at[c * 8 : c * 8 + 728],
                )
            places = (
                xface.at[pl.ds(pl.multiple_of(a * FACE + b * 136 + c * 8, 8), 152)],
                yface.at[pl.ds(pl.multiple_of(b * FACE + a * 136 + c * 8, 8), 152)],
                zface.at[pl.ds(pl.multiple_of(c * FACE + a * 136 + b * 8, 8), 152)],
            )
            for axis in range(3):
                for line in range(9):
                    if not full:
                        spot = slice(axis * 81 + line * 9, axis * 81 + line * 9 + 9)
                    elif axis == 0:
                        spot = slice(line * 9, line * 9 + 9)
                    elif axis == 1:
                        spot = slice(line * 81, line * 81 + 9)
                    else:
                        spot = pl.ds(line * 81, 9, stride=9)
                    places[axis][line * SIDE : line * SIDE + 9, :] += sources[axis][spot, :]
        return carry

    lax.fori_loop(0, 4, pair, 0)
    turn = odd[1] == 1
    for g in range(4):
        spot = slice(g * 128, g * 128 + 128)
        total[spot, :] = jnp.dot(mix[g], total[spot, :], precision=HIGHEST, preferred_element_type=F32)
    weights[...] = total[0:432, :]
    send(turn, yface[0:FACE, :], yface[FACE : 2 * FACE, :], send_one, send_two, slice(0, FACE))
    for p in range(2):
        for x in range(3):
            at = FACE + (p * 3 + x) * 48
            down = total[x * 144 + p * 48 : x * 144 + p * 48 + 48, :]
            up = total[x * 144 + (p + 1) * 48 : x * 144 + (p + 1) * 48 + 48, :]
            send(turn, down, up, send_one, send_two, slice(at, at + 48))


def apply_cells(full, odd, now, ham, rows, mix):
    faces = shape((2 * FACE, LANES), F32)
    message = shape((MESSAGE_Y, LANES), BF16)
    return pl.pallas_call(
        functools.partial(apply_kernel, full),
        out_shape=(shape((8, CELL, LANES), F32 if full else BF16), message, message, faces, faces, shape((432, LANES), F32)),
        in_specs=[SMEM] + [VMEM] * (3 + len(ham)),
        out_specs=(VMEM,) * 6,
        scratch_shapes=[
            pltpu.VMEM((ROWS, LANES), F32),
            pltpu.VMEM((1472, LANES), F32),
            pltpu.VMEM((512, LANES), F32),
            pltpu.VMEM((2 * FACE, LANES), F32),
        ],
        cost_estimate=cost(1.3e9 if full else 6e8, 1.6e7),
        compiler_params=LARGE,
        name="apply_cells",
    )(odd, now, *ham, rows, mix)


PICKED = 256


def pick_kernel(upper, lower, after, out):
    del after
    row = lax.broadcasted_iota(jnp.int32, (PICKED, 1), 0)
    column = lax.broadcasted_iota(jnp.int32, (PICKED, CELL), 1)

    def cell(position, carry):
        a, b, c = position // 4, (position // 2) % 2, position % 2
        on_y, on_z = row - 81, row - 162
        nine_y, nine_z = lax.shift_right_arithmetic(on_y * 57, 9), lax.shift_right_arithmetic(on_z * 57, 9)
        node = nine_z * 81 + (on_z - nine_z * 9) * 9 + c * 8
        node = jnp.where(row < 162, nine_y * 81 + b * 72 + (on_y - nine_y * 9), node)
        node = jnp.where(row < 81, a * 648 + row, node)
        node = jnp.where(row < 243, node, -1)
        chosen = jnp.where(column == node, 1.0, 0.0).astype(BF16)
        found = jnp.dot(chosen[:, 0:UPPER], upper[position], preferred_element_type=F32)
        found += jnp.dot(chosen[:, UPPER:CELL], lower[position], preferred_element_type=F32)
        out[position] = found.astype(BF16)
        return carry

    lax.fori_loop(0, 8, cell, 0)


def pick(ham, after):
    return pl.pallas_call(
        pick_kernel,
        out_shape=shape((8, PICKED, CELL), BF16),
        in_specs=[VMEM, VMEM, pl.BlockSpec(memory_space=pl.ANY)],
        out_specs=VMEM,
        cost_estimate=cost(2e9, 1.2e7),
        compiler_params=LARGE,
        name="pick",
    )(*ham, after)


def local_kernel(upper, lower, values, terms, token):
    token[...] = jnp.zeros_like(token)

    def cell(position, carry):
        for part, spot in ((upper, slice(0, UPPER)), (lower, slice(UPPER, CELL))):
            terms[position, spot, :] = jnp.dot(part[position], values[position], preferred_element_type=F32)
        return carry

    lax.fori_loop(0, 8, cell, 0)


def local_part(ham, values):
    return pl.pallas_call(
        local_kernel,
        out_shape=(shape((8, CELL, LANES), F32), shape((8, LANES), F32)),
        in_specs=[VMEM] * 3,
        out_specs=(VMEM, VMEM),
        cost_estimate=cost(1.1e9, 1.4e7),
        compiler_params=LARGE,
        name="local_part",
    )(*ham, values)


def assemble_kernel(first, terms, now, *refs):
    before = None if first else refs[0]
    field = refs[-1]
    scale = 1.0 if first else 2.0

    def chunk(n, carry):
        spot = pl.ds(pl.multiple_of(n * CHUNK, 16), CHUNK)
        value = -scale * now[spot, :].astype(F32)
        if before is not None:
            value = value - before[spot, :].astype(F32)
        field[spot, :] = value
        return carry

    lax.fori_loop(0, ROWS // CHUNK, chunk, 0)

    def cell(position, carry):
        a, b, c = position // 4, (position // 2) % 2, position % 2
        base = cell_base(a, b, c)
        for x in range(9):
            for y in range(9):
                at = (x * 9 + y) * 9
                field[pl.ds(line_start(base, x, y), 9), :] += scale * terms[position, at : at + 9, :]
        return carry

    lax.fori_loop(0, 8, cell, 0)


def assemble(terms, now, before):
    args = [terms, now] + ([] if before is None else [before])
    return pl.pallas_call(
        functools.partial(assemble_kernel, before is None),
        out_shape=shape((ROWS, LANES), F32),
        in_specs=[VMEM] * len(args),
        out_specs=VMEM,
        cost_estimate=cost(1e7, 1.2e7),
        compiler_params=SMALL,
        name="assemble",
    )(*args)


def after_y_kernel(odd, one, two, zface, xface, weights, after, send_one, send_two, xface_out, weights_out, low, high, face_low, face_high):
    del after
    low[...], high[...] = receive(odd[1] == 1, one, two, slice(0, FACE))
    turn = odd[2] == 1
    last = 16 * SIDE
    for face, start, column in ((face_low, 0, 0), (face_high, FACE, 16)):
        face[...] = zface[start : start + FACE, :]
        face[pl.ds(0, SIDE, stride=SIDE), :] += low[pl.ds(column, SIDE, stride=SIDE), :]
        face[pl.ds(16, SIDE, stride=SIDE), :] += high[pl.ds(column, SIDE, stride=SIDE), :]
    send(turn, face_low[...], face_high[...], send_one, send_two, slice(0, FACE))
    xface_out[...] = xface[...]
    for start, row in ((0, 0), (FACE, last)):
        xface_out[start : start + SIDE, :] += low[row : row + SIDE, :]
        xface_out[start + last : start + last + SIDE, :] += high[row : row + SIDE, :]
    for x in range(3):
        weights_out[x * 240 + 48 : x * 240 + 192, :] = weights[x * 144 : x * 144 + 144, :]
        for p in range(2):
            at = FACE + (p * 3 + x) * 48
            below, above = receive(odd[1] == 1, one, two, slice(at, at + 48))
            if p == 0:
                weights_out[x * 240 : x * 240 + 48, :] = below
                weights_out[x * 240 + 144 : x * 240 + 192, :] += above
            else:
                weights_out[x * 240 + 48 : x * 240 + 96, :] += below
                weights_out[x * 240 + 192 : x * 240 + 240, :] = above
    for p in range(2):
        for n in range(15):
            at = FACE + (p * 15 + n) * 16
            down = weights_out[n * 48 + p * 16 : n * 48 + p * 16 + 16, :]
            up = weights_out[n * 48 + p * 16 + 16 : n * 48 + p * 16 + 32, :]
            send(turn, down, up, send_one, send_two, slice(at, at + 16))


def after_y(odd, one, two, zface, xface, weights, after):
    message = shape((MESSAGE_Z, LANES), BF16)
    return pl.pallas_call(
        after_y_kernel,
        out_shape=(message, message, shape((2 * FACE, LANES), F32), shape((720, LANES), F32)),
        in_specs=[SMEM] + [VMEM] * 5 + [pl.BlockSpec(memory_space=pl.ANY)],
        out_specs=(VMEM,) * 4,
        scratch_shapes=[pltpu.VMEM((FACE, LANES), F32)] * 4,
        cost_estimate=cost(1e5, 2e6),
        compiler_params=SMALL,
        name="after_y",
    )(odd, one, two, zface, xface, weights, after)


def after_z_kernel(odd, one, two, xface, weights, send_one, send_two, weights_out, low, high, face_low, face_high):
    low[...], high[...] = receive(odd[2] == 1, one, two, slice(0, FACE))
    turn = odd[0] == 1
    for face, start, row in ((face_low, 0, 0), (face_high, FACE, 16 * SIDE)):
        face[...] = xface[start : start + FACE, :]
        face[pl.ds(0, SIDE, stride=SIDE), :] += low[row : row + SIDE, :]
        face[pl.ds(16, SIDE, stride=SIDE), :] += high[row : row + SIDE, :]
    send(turn, face_low[...], face_high[...], send_one, send_two, slice(0, FACE))
    for n in range(15):
        weights_out[n * 80 + 16 : n * 80 + 64, :] = weights[n * 48 : n * 48 + 48, :]
        for p in range(2):
            at = FACE + (p * 15 + n) * 16
            below, above = receive(odd[2] == 1, one, two, slice(at, at + 16))
            if p == 0:
                weights_out[n * 80 : n * 80 + 16, :] = below
                weights_out[n * 80 + 48 : n * 80 + 64, :] += above
            else:
                weights_out[n * 80 + 16 : n * 80 + 32, :] += below
                weights_out[n * 80 + 64 : n * 80 + 80, :] = above
    for p in range(2):
        at = FACE + p * 400
        down, up = weights_out[p * 400 : p * 400 + 400, :], weights_out[p * 400 + 400 : p * 400 + 800, :]
        send(turn, down, up, send_one, send_two, slice(at, at + 400))


def after_z(odd, one, two, xface, weights):
    message = shape((MESSAGE_X, LANES), BF16)
    return pl.pallas_call(
        after_z_kernel,
        out_shape=(message, message, shape((1200, LANES), F32)),
        in_specs=[SMEM] + [VMEM] * 4,
        out_specs=(VMEM,) * 3,
        scratch_shapes=[pltpu.VMEM((FACE, LANES), F32)] * 4,
        cost_estimate=cost(1e5, 2e6),
        compiler_params=SMALL,
        name="after_z",
    )(odd, one, two, xface, weights)


def corner_weights(weights, a, b, c):
    pieces = []
    for o in range(8):
        i, j, k = o // 4, (o // 2) % 2, o % 2
        vertex = ((a + i) * 5 + b + j) * 5 + c + k
        pieces.append(weights[pl.ds(pl.multiple_of(vertex * 16, 16), 16), :])
    return jnp.concatenate(pieces, axis=0)


def advance_kernel(first, last, odd, start_field, y1, y2, z1, z2, x1, x2, w75, columns, faces, edges, points, out, *refs):
    del start_field
    parts = refs[: len(refs) - 6]
    field, cell32, weights, xs, ys, zs = refs[len(refs) - 6 :]
    scale = 1.0 if first else 2.0
    for ref, one, two, axis in ((xs, x1, x2, 0), (ys, y1, y2, 1), (zs, z1, z2, 2)):
        low, high = receive(odd[axis] == 1, one, two, slice(0, FACE))
        ref[0:FACE, :] = low
        ref[FACE : 2 * FACE, :] = high
    for p in range(2):
        at = FACE + p * 400
        below, above = receive(odd[0] == 1, x1, x2, slice(at, at + 400))
        if p == 0:
            weights[0:400, :] = below.astype(BF16)
            weights[1200:1600, :] = (w75[800:1200, :] + above).astype(BF16)
        else:
            weights[400:800, :] = (w75[0:400, :] + below).astype(BF16)
            weights[1600:2000, :] = above.astype(BF16)
    weights[800:1200, :] = w75[400:800, :].astype(BF16)

    def pair(n, carry):
        for h in range(2):
            corner = corner_weights(weights, n // 2 + 1, n % 2 + 1, h + 1)
            term = jnp.dot(columns[n * 2 + h], corner, preferred_element_type=F32)
            cell32[h * 736 : h * 736 + CELL, :] = scale * term
        for h in range(2):
            base = cell_base(n // 2, n % 2, h)
            for x in range(9):
                for y in range(9):
                    at = h * 736 + (x * 9 + y) * 9
                    field[pl.ds(line_start(base, x, y), 9), :] += cell32[at : at + 9, :]
        return carry

    lax.fori_loop(0, 4, pair, 0)

    for axis, ref in enumerate((xs, ys, zs)):

        def face(s, carry, axis=axis, ref=ref):
            for n in range(4):
                spot = [n // 2 + 1, n % 2 + 1]
                spot.insert(axis, 3 * s)
                cell32[n * 88 : n * 88 + 81, :] = jnp.dot(
                    faces[axis * 8 + s * 4 + n], corner_weights(weights, *spot), preferred_element_type=F32
                )
            for n in range(4):
                view = ref.at[pl.ds(pl.multiple_of(s * FACE + (n // 2) * 136 + (n % 2) * 8, 8), 152)]
                for row in range(9):
                    at = n * 88 + row * 9
                    view[row * SIDE : row * SIDE + 9, :] += cell32[at : at + 9, :]
            return carry

        lax.fori_loop(0, 2, face, 0)

    for axis in range(3):

        def edge(s, carry, axis=axis):
            terms = []
            for n in range(4):
                spot = [3 * s, 3 * (n // 2)]
                spot.insert(axis, n % 2 + 1)
                terms.append(
                    jnp.dot(edges[axis * 8 + s * 4 + n], corner_weights(weights, *spot), preferred_element_type=F32)
                )
            for n, term in enumerate(terms):
                t, u = n // 2, n % 2
                if axis == 2:
                    view = xs.at[pl.ds(pl.multiple_of(s * FACE + t * 272 + u * 8, 8), 16)]
                    view[0:9, :] += term
                else:
                    ref = xs if axis == 1 else ys
                    view = ref.at[pl.ds(pl.multiple_of(s * FACE + u * 136 + t * 16, 8), 152)]
                    view[pl.ds(0, 9, stride=SIDE), :] += term
            return carry

        lax.fori_loop(0, 2, edge, 0)

    def point(s, carry):
        terms = []
        for n in range(4):
            corner = corner_weights(weights, 3 * s, 3 * (n // 2), 3 * (n % 2))
            terms.append(jnp.dot(points[s * 4 + n], corner, preferred_element_type=F32))
        for n, term in enumerate(terms):
            view = xs.at[pl.ds(pl.multiple_of(s * FACE + (n // 2) * 272 + (n % 2) * 16, 8), 8)]
            view[0:1, :] += term
        return carry

    lax.fori_loop(0, 2, point, 0)

    for s in range(2):
        for y in range(SIDE):
            at = s * 16 * SLAB + y * ZPAD
            field[at : at + SIDE, :] += scale * xs[s * FACE + y * SIDE : s * FACE + (y + 1) * SIDE, :]
        for x in range(SIDE):
            at = s * 16 * ZPAD + x * SLAB
            field[at : at + SIDE, :] += scale * ys[s * FACE + x * SIDE : s * FACE + (x + 1) * SIDE, :]
        field[pl.ds(s * 16, PLANE, stride=ZPAD), :] += scale * zs[s * FACE : s * FACE + PLANE, :]

    if last:

        def slab(x, carry):
            for y in range(16):
                start = pl.multiple_of(x * SLAB + y * ZPAD, 8)
                out[x, y] = field[pl.ds(start, 16), :].astype(BF16)
            return carry

        lax.fori_loop(0, 16, slab, 0)
        for offset, part in enumerate(parts):
            quarter = (odd[3] + offset) % 4
            part[...] = out[pl.ds(quarter * 4, 4)].reshape(1024, LANES)
    else:

        def chunk(n, carry):
            spot = pl.ds(pl.multiple_of(n * CHUNK, 16), CHUNK)
            out[spot, :] = field[spot, :].astype(BF16)
            return carry

        lax.fori_loop(0, ROWS // CHUNK, chunk, 0)


def advance(odd, field, messages, w75, tables, first, last):
    args = [odd, field, *messages, w75, *tables]
    if last:
        outs = [shape((16, 16, 16, LANES), BF16)] + [shape((1024, LANES), BF16)] * 4
    else:
        outs = [shape((ROWS, LANES), BF16)]
    outs.append(shape((ROWS, LANES), F32))
    return pl.pallas_call(
        functools.partial(advance_kernel, first, last),
        out_shape=tuple(outs),
        in_specs=[SMEM] + [VMEM] * (len(args) - 1),
        out_specs=(VMEM,) * len(outs),
        input_output_aliases={1: len(outs) - 1},
        scratch_shapes=[pltpu.VMEM((1472, LANES), F32), pltpu.VMEM((2000, LANES), BF16)]
        + [pltpu.VMEM((2 * FACE, LANES), F32)] * 3,
        cost_estimate=cost(3e8, 1.2e7),
        compiler_params=LARGE,
        name="advance",
    )(*args)[:-1]


def gram_kernel(x0, x1, x2, x3, own, m1, m2, m3):
    blocks = [x0[...], x1[...], x2[...], x3[...]]
    for row, left in enumerate(blocks):
        turned = left.T
        for column, out in ((0, own), (3, m1), (2, m2), (1, m3)):
            part = jnp.dot(turned, blocks[column], preferred_element_type=F32)
            out[row * 128 : row * 128 + 128, :] = part.astype(out.dtype)


def gram(blocks):
    return pl.pallas_call(
        gram_kernel,
        out_shape=(shape((512, LANES), F32),) + (shape((512, LANES), BF16),) * 3,
        in_specs=[VMEM] * 4,
        out_specs=(VMEM,) * 4,
        cost_estimate=cost(6e8, 2e6),
        compiler_params=LARGE,
        name="gram",
    )(*blocks)


def collect_kernel(band, own, m1, m2, m3, out):
    for row in range(4):
        total = own[row * 128 : row * 128 + 128, :]
        for offset, ref in ((1, m1), (2, m2), (3, m3)):
            source = (row - offset) % 4
            total = total + ref[source * 128 : source * 128 + 128, :].astype(F32)
        place = (band[0] + 4 - row) % 4
        out[pl.ds(place * 16, 16)] = total.reshape(16, 8, LANES).astype(BF16)


def collect(band, own, received):
    return pl.pallas_call(
        collect_kernel,
        out_shape=shape((64, 8, LANES), BF16),
        in_specs=[SMEM] + [VMEM] * 4,
        out_specs=VMEM,
        cost_estimate=cost(1e6, 1e6),
        compiler_params=SMALL,
        name="collect",
    )(band, own, *received)


def total_kernel(scale, terms, out):
    out[...] = jnp.sum(terms[...].astype(F32), axis=0) * scale


def total(terms, scale):
    return pl.pallas_call(
        functools.partial(total_kernel, scale),
        out_shape=shape(terms.shape[1:], F32),
        in_specs=[VMEM],
        out_specs=VMEM,
        cost_estimate=cost(1e5, 2e5),
        compiler_params=SMALL,
        name="total",
    )(terms)


def local(psi, cell_ham, proj_table, coupling, atom_kind):
    devices = lax.axis_size("cells")
    side = cube_root(devices)
    offsets = (1, side, side * side)
    block = lax.axis_index("cells")
    band = lax.axis_index("bands")
    odd = jnp.stack([(block // offset) % 2 for offset in offsets] + [band]).astype(jnp.int32)

    def upward(x, axis):
        return shifted(x, "cells", offsets[axis])

    def downward(x, axis):
        return shifted(x, "cells", -offsets[axis])

    def swap(messages, axis):
        offset = offsets[axis]
        arrived = []
        for start, message in enumerate(messages):
            pairs = []
            for i in range(devices):
                forward = (i // offset) % 2 == start
                pairs.append((i, (i + offset) % devices if forward else (i - offset) % devices))
            arrived.append(lax.ppermute(message, "cells", pairs))
        return arrived

    message, up, own = first_x(psi, atom_kind)
    from_x, up_x = downward(message, 0), upward(up, 0)
    rows_y, rows_z = first_rows(psi)
    message, up, s20 = first_y(rows_y, from_x, up_x, own)
    from_y, up_y = downward(message, 1), upward(up, 1)
    upper, token = by_cell(cell_ham, 0, UPPER, s20)
    message, up, s50 = first_z(rows_z, from_x, from_y, up_y, s20, token)
    from_z, up_z = downward(message, 2), upward(up, 2)
    lower, _ = by_cell(cell_ham, UPPER, CELL - UPPER, s50)
    ham = (upper, lower)
    table = proj_table.reshape(4, 128, CELL)
    kinds, rows, mix = first_tables(from_z, up_z, s50, table, coupling)

    def step(now, before, last, tables):
        first = tables is None
        terms, one, two, zface, xface, weights = apply_cells(
            first, odd, now, ham if first else (tables[-1],), rows, mix
        )
        ys = swap((one, two), 1)
        if first:
            picked = pick(ham, weights)
            token = picked
            tables = (*make_tables(kinds, turn(table, weights), weights), picked)
        else:
            terms, token = local_part(ham, terms)
        field = assemble(terms, now, before)
        one, two, xface, weights = after_y(odd, *ys, zface, xface, weights, token)
        zs = swap((one, two), 2)
        one, two, weights = after_z(odd, *zs, xface, weights)
        xs = swap((one, two), 0)
        return tables, advance(odd, field, (*ys, *zs, *xs), weights, tables[:4], before is None, last)

    y0 = begin(psi, from_x, from_y, from_z)
    tables, (y1,) = step(y0, None, False, None)
    tables, (y2,) = step(y1, y0, False, tables)
    tables, (filtered, *blocks) = step(y2, y1, True, tables)

    two = shifted(blocks[2], "bands", 2)
    blocks = [blocks[0], shifted(blocks[1], "bands", 1), two, shifted(blocks[3], "bands", 3)]
    own, *messages = gram(blocks)
    messages = [shifted(message, "bands", n + 1) for n, message in enumerate(messages)]
    terms = collect(band.astype(jnp.int32).reshape(1), own, messages)
    terms = lax.all_to_all(terms, "cells", 0, 0)
    inverse_count = 1.0 / (4096 * devices)
    correlation = total(terms, inverse_count)
    return filtered, correlation


def solution(mesh):
    in_specs = (
        P("cells", None, None, "bands"),
        P("cells", None, None),
        P(),
        P(),
        P("cells", None, None),
    )
    out_specs = (P("cells", None, None, "bands"), P("cells", "bands"))
    return jax.shard_map(local, mesh=mesh, in_specs=in_specs, out_specs=out_specs, check_vma=False)
```

```python
import functools

import jax
import jax.numpy as jnp
from jax import lax
from jax.experimental import pallas as pl
from jax.experimental.pallas import tpu as pltpu
from jax.sharding import PartitionSpec as P


F32 = jnp.float32
BF16 = jnp.bfloat16
HIGHEST = lax.Precision.HIGHEST

SIDE = 17
ZPAD = 24
SLAB = SIDE * ZPAD
ROWS = 6944
CHUNK = 496
FACE = 304
PLANE = SIDE * SIDE
CELL = 729
LANES = 128


def shifted(x, axis, by):
    devices = lax.axis_size(axis)
    return lax.ppermute(x, axis, [(i, (i + by) % devices) for i in range(devices)])


def cube_root(amount):
    result = 1
    while (result + 1) ** 3 <= amount:
        result = result + 1
    return result


def cost(flops, nbytes):
    return pl.CostEstimate(flops=int(flops), bytes_accessed=int(nbytes), transcendentals=0)


def shape(dims, dtype):
    return jax.ShapeDtypeStruct(dims, dtype)


VMEM = pl.BlockSpec(memory_space=pltpu.VMEM)
LARGE = pltpu.CompilerParams(vmem_limit_bytes=10 * 2**20)
SMALL = pltpu.CompilerParams(vmem_limit_bytes=6 * 2**20)
SMEM = pl.BlockSpec(memory_space=pltpu.SMEM)


def cell_base(a, b, c):
    return a * (8 * SLAB) + b * (8 * ZPAD) + c * 8


def line_start(base, x, y):
    return pl.multiple_of(base + (x * SLAB + y * ZPAD), 8)


def kind_row(kinds, a, b, c):
    return kinds[(a * 5 + b) * 5 + c][0:1, :]


def corner_kinds(kinds, a, b, c, lane):
    found = jnp.full((1, LANES), -1.0, F32)
    for o in range(8):
        i, j, k = o // 4, (o // 2) % 2, o % 2
        found = jnp.where(lane == o, kind_row(kinds, a + i, b + j, c + k), found)
    return found


def first_tables_kernel(from_z, up_z, s50, table, coupling, kinds, rows_out, mix_out, wide, table32):
    for n in range(25):
        kinds[n * 5] = jnp.broadcast_to(up_z[n : n + 1, :], (8, LANES))
        for k in range(2):
            at = n * 2 + k
            kinds[n * 5 + 1 + k] = jnp.broadcast_to(s50[at : at + 1, :], (8, LANES))
    above = from_z[FACE : FACE + 64, :].astype(F32)
    for n in range(50):
        kinds[(n // 2) * 5 + 3 + n % 2] = jnp.broadcast_to(above[n : n + 1, :], (8, LANES))
    species = coupling.shape[0]
    lane_wide = lax.broadcasted_iota(jnp.int32, (16, LANES), 1) // 16
    for q in range(species):
        table32[q] = table[q].astype(F32)

    def cell(position, carry):
        a, b, c = position // 4, (position // 2) % 2, position % 2
        for o in range(8):
            i, j, k = o // 4, (o // 2) % 2, o % 2
            kind = kind_row(kinds, a + i + 1, b + j + 1, c + k + 1)[:, 0:1]
            block = jnp.zeros((16, CELL), F32)
            for q in range(species):
                block = jnp.where(kind == q, table32[q, o * 16 : (o + 1) * 16, :], block)
            rows_out[position, o * 16 : (o + 1) * 16, :] = block.astype(BF16)
        return carry

    lax.fori_loop(0, 8, cell, 0)
    mix_out[...] = jnp.zeros_like(mix_out)
    along = lax.broadcasted_iota(jnp.int32, (16, LANES), 1) % 16
    repeat = jnp.where(along == lax.broadcasted_iota(jnp.int32, (16, LANES), 0), 1.0, 0.0).astype(F32)
    for q in range(species):
        wide[q] = jnp.dot(coupling[q], repeat, precision=HIGHEST, preferred_element_type=F32)

    def vertex(v, carry):
        kind = kind_row(kinds, v // 9 + 1, (v // 3) % 3 + 1, v % 3 + 1)
        block = jnp.zeros((16, LANES), F32)
        for q in range(species):
            block = jnp.where(kind == q, wide[q], block)
        block = jnp.where(lane_wide == v % 8, block, 0.0)
        mix_out[v // 8, pl.ds(pl.multiple_of((v % 8) * 16, 16), 16), :] = block
        return carry

    lax.fori_loop(0, 27, vertex, 0)


def first_tables(from_z, up_z, s50, table, coupling):
    species = coupling.shape[0]
    return pl.pallas_call(
        first_tables_kernel,
        out_shape=(shape((125, 8, LANES), F32), shape((8, 128, CELL), BF16), shape((4, LANES, LANES), F32)),
        in_specs=[VMEM] * 5,
        out_specs=(VMEM,) * 3,
        scratch_shapes=[pltpu.VMEM((species, 16, LANES), F32), pltpu.VMEM((species, 128, CELL), F32)],
        cost_estimate=cost(1e6, 3e6),
        compiler_params=SMALL,
        name="first_tables",
    )(from_z, up_z, s50, table, coupling)


def turn_kernel(table, after, out, wide):
    del after
    wide[...] = jnp.zeros_like(wide)
    for q in range(out.shape[0]):
        wide[:, 0:CELL] = table[q].astype(F32)
        out[q] = wide[...].T


def turn(table, after):
    return pl.pallas_call(
        turn_kernel,
        out_shape=shape((table.shape[0], 768, LANES), F32),
        in_specs=[VMEM, pl.BlockSpec(memory_space=pl.ANY)],
        out_specs=VMEM,
        scratch_shapes=[pltpu.VMEM((LANES, 768), F32)],
        cost_estimate=cost(1e6, 3e6),
        compiler_params=SMALL,
        name="turn",
    )(table, after)


def tables_kernel(kinds, table_t, after, columns_out, faces_out, edges_out, points_out, picked):
    del after
    species = table_t.shape[0]
    lane = lax.broadcasted_iota(jnp.int32, (1, LANES), 1) // 16

    def choose(values, lane_kind):
        total = jnp.where(lane_kind == 0, values[0], 0.0)
        for q in range(1, species):
            total = jnp.where(lane_kind == q, values[q], total)
        return total.astype(BF16)

    def cell(position, carry):
        a, b, c = position // 4, (position // 2) % 2, position % 2
        lane_kind = corner_kinds(kinds, a + 1, b + 1, c + 1, lane)
        columns_out[position] = choose([table_t[q, 0:CELL] for q in range(species)], lane_kind)
        return carry

    lax.fori_loop(0, 8, cell, 0)
    for axis in range(3):
        for s in range(2):
            near = 8 - 8 * s
            for q in range(species):
                if axis == 0:
                    picked[q, 0:81] = table_t[q, near * 81 : near * 81 + 81]
                elif axis == 1:
                    for x in range(9):
                        picked[q, x * 9 : x * 9 + 9] = table_t[q, x * 81 + near * 9 : x * 81 + near * 9 + 9]
                else:
                    picked[q, 0:81] = table_t[q, pl.ds(near, 81, stride=9)]

            def face(n, carry, axis=axis, s=s):
                spot = [n // 2 + 1, n % 2 + 1]
                spot.insert(axis, 3 * s)
                lane_kind = corner_kinds(kinds, *spot, lane)
                faces_out[axis * 8 + s * 4 + n] = choose([picked[q, 0:81] for q in range(species)], lane_kind)
                return carry

            lax.fori_loop(0, 4, face, 0)
    for axis in range(3):
        for s in range(2):
            for t in range(2):
                first, second = 8 - 8 * s, 8 - 8 * t
                for u in range(2):
                    spot = [3 * s, 3 * t]
                    spot.insert(axis, u + 1)
                    start, stride = ((first * 9 + second, 81), (first * 81 + second, 9), (first * 81 + second * 9, 1))[axis]
                    lane_kind = corner_kinds(kinds, *spot, lane)
                    place = slice(start, start + 9) if stride == 1 else pl.ds(start, 9, stride=stride)
                    edges_out[axis * 8 + s * 4 + t * 2 + u, 0:9] = choose([table_t[q, place] for q in range(species)], lane_kind)
    for n in range(8):
        s, t, w = n // 4, (n // 2) % 2, n % 2
        at = (8 - 8 * s) * 81 + (8 - 8 * t) * 9 + 8 - 8 * w
        lane_kind = corner_kinds(kinds, 3 * s, 3 * t, 3 * w, lane)
        points_out[n, 0:1] = choose([table_t[q, at : at + 1] for q in range(species)], lane_kind)


def make_tables(kinds, table_t, after):
    species = table_t.shape[0]
    return pl.pallas_call(
        tables_kernel,
        out_shape=(
            shape((8, CELL, LANES), BF16),
            shape((24, 81, LANES), BF16),
            shape((24, 9, LANES), BF16),
            shape((8, 1, LANES), BF16),
        ),
        in_specs=[VMEM, VMEM, pl.BlockSpec(memory_space=pl.ANY)],
        out_specs=(VMEM,) * 4,
        scratch_shapes=[pltpu.VMEM((species, 88, LANES), F32)],
        cost_estimate=cost(1e7, 6e6),
        compiler_params=SMALL,
        name="tables",
    )(kinds, table_t, after)


def first_x_kernel(psi, own, message, up, species_out):
    message[0:256, :] = psi[...].reshape(256, LANES)
    species = [jnp.full((1, LANES), own[n // 4, (n // 2) % 2, n % 2].astype(F32), F32) for n in range(8)]
    blank = jnp.zeros((8, LANES), F32)
    message[256:272, :] = jnp.concatenate(species + [blank], axis=0).astype(BF16)
    up[...] = jnp.concatenate(species[4:] + [blank[0:4]], axis=0)
    species_out[...] = jnp.concatenate(species, axis=0)


def first_x(psi, own):
    return pl.pallas_call(
        first_x_kernel,
        grid=(1,),
        out_shape=(shape((272, LANES), BF16), shape((8, LANES), F32), shape((8, LANES), F32)),
        in_specs=[pl.BlockSpec((1, 16, 16, LANES), lambda n: (0, 0, 0, 0)), SMEM],
        out_specs=(
            pl.BlockSpec((272, LANES), lambda n: (0, 0)),
            pl.BlockSpec((8, LANES), lambda n: (0, 0)),
            pl.BlockSpec((8, LANES), lambda n: (0, 0)),
        ),
        cost_estimate=cost(1e5, 2e5),
        compiler_params=SMALL,
        name="first_x",
    )(pltpu.with_memory_space_constraint(psi, pltpu.HBM), pltpu.with_memory_space_constraint(own, pltpu.HBM))


def first_rows_kernel(psi, rows_y, rows_z, wide, narrow):
    for x in range(16):
        rows_y[x * 16 : x * 16 + 16, :] = psi[x, 0]
    wide[...] = psi[...].reshape(4096, LANES).astype(F32)
    rows = wide[pl.ds(0, 256, stride=16), :]
    narrow[...] = jnp.zeros_like(narrow)
    for x in range(16):
        narrow[x * SIDE : x * SIDE + 16, :] = rows[x * 16 : x * 16 + 16]
    rows_z[...] = narrow[...]


def first_rows(psi):
    return pl.pallas_call(
        first_rows_kernel,
        out_shape=(shape((256, LANES), BF16), shape((FACE, LANES), F32)),
        in_specs=[VMEM],
        out_specs=(VMEM, VMEM),
        scratch_shapes=[pltpu.VMEM((4096, LANES), F32), pltpu.VMEM((FACE, LANES), F32)],
        cost_estimate=cost(1e6, 1.2e6),
        compiler_params=SMALL,
        name="first_rows",
    )(psi)


def first_y_kernel(rows_y, from_x, up_x, own, message, up, s20):
    message[0:256, :] = rows_y[...]
    message[256:272, :] = from_x[0:16, :]
    s20[0:4, :] = up_x[0:4, :]
    s20[4:12, :] = own[...]
    s20[12:20, :] = from_x[256:272, :].astype(F32)[0:8]
    s20[20:32, :] = jnp.zeros((12, LANES), F32)
    message[272:304, :] = s20[...].astype(BF16)
    for x in range(5):
        up[x * 2 : x * 2 + 2, :] = s20[x * 4 + 2 : x * 4 + 4, :]
    up[10:16, :] = jnp.zeros((6, LANES), F32)


def first_y(rows_y, from_x, up_x, own):
    return pl.pallas_call(
        first_y_kernel,
        out_shape=(shape((304, LANES), BF16), shape((16, LANES), F32), shape((32, LANES), F32)),
        in_specs=[VMEM] * 4,
        out_specs=(VMEM,) * 3,
        cost_estimate=cost(1e5, 2e5),
        compiler_params=SMALL,
        name="first_y",
    )(rows_y, from_x, up_x, own)


def first_z_kernel(rows, from_x, from_y, up_y, s20, after, message, up, s50, wide_x, wide_y, face):
    del after
    wide_x[...] = from_x[0:256, :].astype(F32)
    wide_y[...] = from_y[...].astype(F32)
    face[...] = rows[...]
    face[16 * SIDE : 16 * SIDE + 16, :] = wide_x[pl.ds(0, 16, stride=16), :]
    face[pl.ds(16, SIDE, stride=SIDE), :] = wide_y[pl.ds(0, SIDE, stride=16), :]
    message[0:FACE, :] = face[...].astype(BF16)
    for x in range(5):
        s50[x * 10 : x * 10 + 2, :] = up_y[x * 2 : x * 2 + 2, :]
        s50[x * 10 + 2 : x * 10 + 6, :] = s20[x * 4 : x * 4 + 4, :]
        s50[x * 10 + 6 : x * 10 + 10, :] = wide_y[272 + x * 4 : 272 + x * 4 + 4, :]
    s50[50:64, :] = jnp.zeros((14, LANES), F32)
    message[FACE : FACE + 64, :] = s50[...].astype(BF16)
    up[0:25, :] = s50[pl.ds(1, 25, stride=2), :]
    up[25:32, :] = jnp.zeros((7, LANES), F32)


def first_z(rows, from_x, from_y, up_y, s20, after):
    return pl.pallas_call(
        first_z_kernel,
        out_shape=(shape((FACE + 64, LANES), BF16), shape((32, LANES), F32), shape((64, LANES), F32)),
        in_specs=[VMEM] * 5 + [pl.BlockSpec(memory_space=pl.ANY)],
        out_specs=(VMEM,) * 3,
        scratch_shapes=[
            pltpu.VMEM((256, LANES), F32),
            pltpu.VMEM((304, LANES), F32),
            pltpu.VMEM((FACE, LANES), F32),
        ],
        cost_estimate=cost(1e5, 4e5),
        compiler_params=SMALL,
        name="first_z",
    )(rows, from_x, from_y, up_y, s20, after)


def begin_kernel(psi, from_x, from_y, from_z, field_out, field, wide):
    field[...] = jnp.zeros_like(field)

    def slab(x, carry):
        for y in range(16):
            start = pl.multiple_of(x * SLAB + y * ZPAD, 8)
            field[pl.ds(start, 16), :] = psi[x, y].astype(F32)
        return carry

    lax.fori_loop(0, 16, slab, 0)
    for y in range(16):
        at = 16 * SLAB + y * ZPAD
        field[at : at + 16, :] = from_x[y * 16 : y * 16 + 16, :].astype(F32)
    for x in range(SIDE):
        at = x * SLAB + 16 * ZPAD
        field[at : at + 16, :] = from_y[x * 16 : x * 16 + 16, :].astype(F32)
    wide[...] = from_z[0:FACE, :].astype(F32)
    field[pl.ds(16, PLANE, stride=ZPAD), :] = wide[0:PLANE, :]

    def chunk(n, carry):
        spot = pl.ds(pl.multiple_of(n * CHUNK, 16), CHUNK)
        field_out[spot, :] = field[spot, :].astype(BF16)
        return carry

    lax.fori_loop(0, ROWS // CHUNK, chunk, 0)


def begin(psi, from_x, from_y, from_z):
    return pl.pallas_call(
        begin_kernel,
        out_shape=shape((ROWS, LANES), BF16),
        in_specs=[VMEM] * 4,
        out_specs=VMEM,
        scratch_shapes=[pltpu.VMEM((ROWS, LANES), F32), pltpu.VMEM((FACE, LANES), F32)],
        cost_estimate=cost(1e7, 4e6),
        compiler_params=LARGE,
        name="begin",
    )(psi, from_x, from_y, from_z)


HAM_ROWS = 128


def by_cell_kernel(source, after, out, token, wide):
    del after
    token[...] = jnp.zeros_like(token)
    def piece(n, carry):
        for half in range(2):
            spot = pl.ds(pl.multiple_of(n * 32 + half * 16, 16), 16)
            for start in range(0, CELL, LANES):
                width = min(LANES, CELL - start)
                block = wide.at[half, start : start + LANES]
                block[:, 0:width] = source[spot, :, start : start + width].astype(F32).reshape(128, width)
        for half in range(2):
            spot = pl.ds(pl.multiple_of(n * 32 + half * 16, 16), 16)
            for start in range(0, CELL, LANES):
                width = min(LANES, CELL - start)
                block = wide.at[half, start : start + LANES]
                for c in range(8):
                    found = block[pl.ds(c, 16, stride=8), :]
                    out[c, spot, start : start + width] = found[:, 0:width].astype(BF16)
        return carry

    lax.fori_loop(0, HAM_ROWS // 32, piece, 0)


UPPER = 384


def by_cell(ham, first, count, after):
    return pl.pallas_call(
        by_cell_kernel,
        grid=(pl.cdiv(count, HAM_ROWS),),
        out_shape=(shape((8, count, CELL), BF16), shape((8, LANES), F32)),
        in_specs=[
            pl.BlockSpec((HAM_ROWS, 8, CELL), lambda n: (n + first // HAM_ROWS, 0, 0)),
            pl.BlockSpec(memory_space=pl.ANY),
        ],
        out_specs=(
            pl.BlockSpec((8, HAM_ROWS, CELL), lambda n: (0, n, 0)),
            pl.BlockSpec((8, LANES), lambda n: (0, 0)),
        ),
        scratch_shapes=[pltpu.VMEM((2, 768, LANES), F32)],
        cost_estimate=cost(1e7, 9e6),
        compiler_params=LARGE,
        name="by_cell",
    )(pltpu.with_memory_space_constraint(jnp.transpose(ham, (1, 0, 2)), pltpu.HBM), after)


MESSAGE_Y = FACE + 288
MESSAGE_Z = FACE + 480
MESSAGE_X = FACE + 800


def send(odd, low, high, first, second, rows):
    first[rows, :] = jnp.where(odd, low, high).astype(BF16)
    second[rows, :] = jnp.where(odd, high, low).astype(BF16)


def receive(odd, first, second, rows):
    one, two = first[rows, :].astype(F32), second[rows, :].astype(F32)
    return jnp.where(odd, one, two), jnp.where(odd, two, one)


def apply_kernel(full, odd, now, *refs):
    split = len(refs) - 12
    ham, refs = refs[:split], refs[split:]
    rows, mix, terms, send_one, send_two, zface, xface, weights, field, cell32, total, yface = refs
    def chunk(n, carry):
        spot = pl.ds(pl.multiple_of(n * CHUNK, 16), CHUNK)
        field[spot, :] = now[spot, :].astype(F32)
        return carry

    lax.fori_loop(0, ROWS // CHUNK, chunk, 0)
    for ref in (total, xface, yface, zface):
        ref[...] = jnp.zeros_like(ref)

    def pair(n, carry):
        staged = [cell32.at[0:736], cell32.at[736:1472]]
        loaded = []
        for h, stage in enumerate(staged):
            base = cell_base(n // 2, n % 2, h)
            for x in range(9):
                for y in range(9):
                    at = (x * 9 + y) * 9
                    stage[at : at + 9, :] = field[pl.ds(line_start(base, x, y), 9), :]
            loaded.append(stage[0:CELL, :].astype(BF16))
        for h, (stage, values) in enumerate(zip(staged, loaded)):
            position, a, b, c = n * 2 + h, n // 2, n % 2, h
            part = jnp.dot(rows[position], values, preferred_element_type=F32)
            for o in range(8):
                i, j, k = o // 4, (o // 2) % 2, o % 2
                vertex = (a + i) * 9 + (b + j) * 3 + c + k
                total[pl.ds(pl.multiple_of(vertex * 16, 16), 16), :] += part[o * 16 : (o + 1) * 16]
            if full:
                for block, spot in zip(ham, (slice(0, UPPER), slice(UPPER, CELL))):
                    result = jnp.dot(block[position], values, preferred_element_type=F32)
                    terms[position, spot, :] = result
                    stage[spot, :] = result
            else:
                terms[position] = values
                stage[0:PICKED, :] = jnp.dot(ham[0][position], values, preferred_element_type=F32)
        for h, stage in enumerate(staged):
            a, b, c = n // 2, n % 2, h
            sources = (stage, stage, stage)
            if full:
                sources = (
                    stage.at[pl.ds(pl.multiple_of(a * 648, 8), 88)],
                    stage.at[pl.ds(pl.multiple_of(b * 72, 8), 664)],
                    stage.at[c * 8 : c * 8 + 728],
                )
            places = (
                xface.at[pl.ds(pl.multiple_of(a * FACE + b * 136 + c * 8, 8), 152)],
                yface.at[pl.ds(pl.multiple_of(b * FACE + a * 136 + c * 8, 8), 152)],
                zface.at[pl.ds(pl.multiple_of(c * FACE + a * 136 + b * 8, 8), 152)],
            )
            for axis in range(3):
                for line in range(9):
                    if not full:
                        spot = slice(axis * 81 + line * 9, axis * 81 + line * 9 + 9)
                    elif axis == 0:
                        spot = slice(line * 9, line * 9 + 9)
                    elif axis == 1:
                        spot = slice(line * 81, line * 81 + 9)
                    else:
                        spot = pl.ds(line * 81, 9, stride=9)
                    places[axis][line * SIDE : line * SIDE + 9, :] += sources[axis][spot, :]
        return carry

    lax.fori_loop(0, 4, pair, 0)
    turn = odd[1] == 1
    for g in range(4):
        spot = slice(g * 128, g * 128 + 128)
        total[spot, :] = jnp.dot(mix[g], total[spot, :], precision=HIGHEST, preferred_element_type=F32)
    weights[...] = total[0:432, :]
    send(turn, yface[0:FACE, :], yface[FACE : 2 * FACE, :], send_one, send_two, slice(0, FACE))
    for p in range(2):
        for x in range(3):
            at = FACE + (p * 3 + x) * 48
            down = total[x * 144 + p * 48 : x * 144 + p * 48 + 48, :]
            up = total[x * 144 + (p + 1) * 48 : x * 144 + (p + 1) * 48 + 48, :]
            send(turn, down, up, send_one, send_two, slice(at, at + 48))


def apply_cells(full, odd, now, ham, rows, mix):
    faces = shape((2 * FACE, LANES), F32)
    message = shape((MESSAGE_Y, LANES), BF16)
    return pl.pallas_call(
        functools.partial(apply_kernel, full),
        out_shape=(shape((8, CELL, LANES), F32 if full else BF16), message, message, faces, faces, shape((432, LANES), F32)),
        in_specs=[SMEM] + [VMEM] * (3 + len(ham)),
        out_specs=(VMEM,) * 6,
        scratch_shapes=[
            pltpu.VMEM((ROWS, LANES), F32),
            pltpu.VMEM((1472, LANES), F32),
            pltpu.VMEM((512, LANES), F32),
            pltpu.VMEM((2 * FACE, LANES), F32),
        ],
        cost_estimate=cost(1.3e9 if full else 6e8, 1.6e7),
        compiler_params=LARGE,
        name="apply_cells",
    )(odd, now, *ham, rows, mix)


PICKED = 256


def pick_kernel(upper, lower, after, out):
    del after
    row = lax.broadcasted_iota(jnp.int32, (PICKED, 1), 0)
    column = lax.broadcasted_iota(jnp.int32, (PICKED, CELL), 1)

    def cell(position, carry):
        a, b, c = position // 4, (position // 2) % 2, position % 2
        on_y, on_z = row - 81, row - 162
        nine_y, nine_z = lax.shift_right_arithmetic(on_y * 57, 9), lax.shift_right_arithmetic(on_z * 57, 9)
        node = nine_z * 81 + (on_z - nine_z * 9) * 9 + c * 8
        node = jnp.where(row < 162, nine_y * 81 + b * 72 + (on_y - nine_y * 9), node)
        node = jnp.where(row < 81, a * 648 + row, node)
        node = jnp.where(row < 243, node, -1)
        chosen = jnp.where(column == node, 1.0, 0.0).astype(BF16)
        found = jnp.dot(chosen[:, 0:UPPER], upper[position], preferred_element_type=F32)
        found += jnp.dot(chosen[:, UPPER:CELL], lower[position], preferred_element_type=F32)
        out[position] = found.astype(BF16)
        return carry

    lax.fori_loop(0, 8, cell, 0)


def pick(ham, after):
    return pl.pallas_call(
        pick_kernel,
        out_shape=shape((8, PICKED, CELL), BF16),
        in_specs=[VMEM, VMEM, pl.BlockSpec(memory_space=pl.ANY)],
        out_specs=VMEM,
        cost_estimate=cost(2e9, 1.2e7),
        compiler_params=LARGE,
        name="pick",
    )(*ham, after)


def local_kernel(upper, lower, values, terms, token):
    token[...] = jnp.zeros_like(token)

    def cell(position, carry):
        for part, spot in ((upper, slice(0, UPPER)), (lower, slice(UPPER, CELL))):
            terms[position, spot, :] = jnp.dot(part[position], values[position], preferred_element_type=F32)
        return carry

    lax.fori_loop(0, 8, cell, 0)


def local_part(ham, values):
    return pl.pallas_call(
        local_kernel,
        out_shape=(shape((8, CELL, LANES), F32), shape((8, LANES), F32)),
        in_specs=[VMEM] * 3,
        out_specs=(VMEM, VMEM),
        cost_estimate=cost(1.1e9, 1.4e7),
        compiler_params=LARGE,
        name="local_part",
    )(*ham, values)


def assemble_kernel(first, terms, now, *refs):
    before = None if first else refs[0]
    field = refs[-1]
    scale = 1.0 if first else 2.0

    def chunk(n, carry):
        spot = pl.ds(pl.multiple_of(n * CHUNK, 16), CHUNK)
        value = -scale * now[spot, :].astype(F32)
        if before is not None:
            value = value - before[spot, :].astype(F32)
        field[spot, :] = value
        return carry

    lax.fori_loop(0, ROWS // CHUNK, chunk, 0)

    def cell(position, carry):
        a, b, c = position // 4, (position // 2) % 2, position % 2
        base = cell_base(a, b, c)
        for x in range(9):
            for y in range(9):
                at = (x * 9 + y) * 9
                field[pl.ds(line_start(base, x, y), 9), :] += scale * terms[position, at : at + 9, :]
        return carry

    lax.fori_loop(0, 8, cell, 0)


def assemble(terms, now, before):
    args = [terms, now] + ([] if before is None else [before])
    return pl.pallas_call(
        functools.partial(assemble_kernel, before is None),
        out_shape=shape((ROWS, LANES), F32),
        in_specs=[VMEM] * len(args),
        out_specs=VMEM,
        cost_estimate=cost(1e7, 1.2e7),
        compiler_params=SMALL,
        name="assemble",
    )(*args)


def after_y_kernel(odd, one, two, zface, xface, weights, after, send_one, send_two, xface_out, weights_out, low, high, face_low, face_high):
    del after
    low[...], high[...] = receive(odd[1] == 1, one, two, slice(0, FACE))
    turn = odd[2] == 1
    last = 16 * SIDE
    for face, start, column in ((face_low, 0, 0), (face_high, FACE, 16)):
        face[...] = zface[start : start + FACE, :]
        face[pl.ds(0, SIDE, stride=SIDE), :] += low[pl.ds(column, SIDE, stride=SIDE), :]
        face[pl.ds(16, SIDE, stride=SIDE), :] += high[pl.ds(column, SIDE, stride=SIDE), :]
    send(turn, face_low[...], face_high[...], send_one, send_two, slice(0, FACE))
    xface_out[...] = xface[...]
    for start, row in ((0, 0), (FACE, last)):
        xface_out[start : start + SIDE, :] += low[row : row + SIDE, :]
        xface_out[start + last : start + last + SIDE, :] += high[row : row + SIDE, :]
    for x in range(3):
        weights_out[x * 240 + 48 : x * 240 + 192, :] = weights[x * 144 : x * 144 + 144, :]
        for p in range(2):
            at = FACE + (p * 3 + x) * 48
            below, above = receive(odd[1] == 1, one, two, slice(at, at + 48))
            if p == 0:
                weights_out[x * 240 : x * 240 + 48, :] = below
                weights_out[x * 240 + 144 : x * 240 + 192, :] += above
            else:
                weights_out[x * 240 + 48 : x * 240 + 96, :] += below
                weights_out[x * 240 + 192 : x * 240 + 240, :] = above
    for p in range(2):
        for n in range(15):
            at = FACE + (p * 15 + n) * 16
            down = weights_out[n * 48 + p * 16 : n * 48 + p * 16 + 16, :]
            up = weights_out[n * 48 + p * 16 + 16 : n * 48 + p * 16 + 32, :]
            send(turn, down, up, send_one, send_two, slice(at, at + 16))


def after_y(odd, one, two, zface, xface, weights, after):
    message = shape((MESSAGE_Z, LANES), BF16)
    return pl.pallas_call(
        after_y_kernel,
        out_shape=(message, message, shape((2 * FACE, LANES), F32), shape((720, LANES), F32)),
        in_specs=[SMEM] + [VMEM] * 5 + [pl.BlockSpec(memory_space=pl.ANY)],
        out_specs=(VMEM,) * 4,
        scratch_shapes=[pltpu.VMEM((FACE, LANES), F32)] * 4,
        cost_estimate=cost(1e5, 2e6),
        compiler_params=SMALL,
        name="after_y",
    )(odd, one, two, zface, xface, weights, after)


def after_z_kernel(odd, one, two, xface, weights, send_one, send_two, weights_out, low, high, face_low, face_high):
    low[...], high[...] = receive(odd[2] == 1, one, two, slice(0, FACE))
    turn = odd[0] == 1
    for face, start, row in ((face_low, 0, 0), (face_high, FACE, 16 * SIDE)):
        face[...] = xface[start : start + FACE, :]
        face[pl.ds(0, SIDE, stride=SIDE), :] += low[row : row + SIDE, :]
        face[pl.ds(16, SIDE, stride=SIDE), :] += high[row : row + SIDE, :]
    send(turn, face_low[...], face_high[...], send_one, send_two, slice(0, FACE))
    for n in range(15):
        weights_out[n * 80 + 16 : n * 80 + 64, :] = weights[n * 48 : n * 48 + 48, :]
        for p in range(2):
            at = FACE + (p * 15 + n) * 16
            below, above = receive(odd[2] == 1, one, two, slice(at, at + 16))
            if p == 0:
                weights_out[n * 80 : n * 80 + 16, :] = below
                weights_out[n * 80 + 48 : n * 80 + 64, :] += above
            else:
                weights_out[n * 80 + 16 : n * 80 + 32, :] += below
                weights_out[n * 80 + 64 : n * 80 + 80, :] = above
    for p in range(2):
        at = FACE + p * 400
        down, up = weights_out[p * 400 : p * 400 + 400, :], weights_out[p * 400 + 400 : p * 400 + 800, :]
        send(turn, down, up, send_one, send_two, slice(at, at + 400))


def after_z(odd, one, two, xface, weights):
    message = shape((MESSAGE_X, LANES), BF16)
    return pl.pallas_call(
        after_z_kernel,
        out_shape=(message, message, shape((1200, LANES), F32)),
        in_specs=[SMEM] + [VMEM] * 4,
        out_specs=(VMEM,) * 3,
        scratch_shapes=[pltpu.VMEM((FACE, LANES), F32)] * 4,
        cost_estimate=cost(1e5, 2e6),
        compiler_params=SMALL,
        name="after_z",
    )(odd, one, two, xface, weights)


def corner_weights(weights, a, b, c):
    pieces = []
    for o in range(8):
        i, j, k = o // 4, (o // 2) % 2, o % 2
        vertex = ((a + i) * 5 + b + j) * 5 + c + k
        pieces.append(weights[pl.ds(pl.multiple_of(vertex * 16, 16), 16), :])
    return jnp.concatenate(pieces, axis=0)


def advance_kernel(first, last, odd, start_field, y1, y2, z1, z2, x1, x2, w75, columns, faces, edges, points, out, *refs):
    del start_field
    parts = refs[: len(refs) - 6]
    field, cell32, weights, xs, ys, zs = refs[len(refs) - 6 :]
    scale = 1.0 if first else 2.0
    for ref, one, two, axis in ((xs, x1, x2, 0), (ys, y1, y2, 1), (zs, z1, z2, 2)):
        low, high = receive(odd[axis] == 1, one, two, slice(0, FACE))
        ref[0:FACE, :] = low
        ref[FACE : 2 * FACE, :] = high
    for p in range(2):
        at = FACE + p * 400
        below, above = receive(odd[0] == 1, x1, x2, slice(at, at + 400))
        if p == 0:
            weights[0:400, :] = below.astype(BF16)
            weights[1200:1600, :] = (w75[800:1200, :] + above).astype(BF16)
        else:
            weights[400:800, :] = (w75[0:400, :] + below).astype(BF16)
            weights[1600:2000, :] = above.astype(BF16)
    weights[800:1200, :] = w75[400:800, :].astype(BF16)

    def pair(n, carry):
        for h in range(2):
            corner = corner_weights(weights, n // 2 + 1, n % 2 + 1, h + 1)
            term = jnp.dot(columns[n * 2 + h], corner, preferred_element_type=F32)
            cell32[h * 736 : h * 736 + CELL, :] = scale * term
        for h in range(2):
            base = cell_base(n // 2, n % 2, h)
            for x in range(9):
                for y in range(9):
                    at = h * 736 + (x * 9 + y) * 9
                    field[pl.ds(line_start(base, x, y), 9), :] += cell32[at : at + 9, :]
        return carry

    lax.fori_loop(0, 4, pair, 0)

    for axis, ref in enumerate((xs, ys, zs)):

        def face(s, carry, axis=axis, ref=ref):
            for n in range(4):
                spot = [n // 2 + 1, n % 2 + 1]
                spot.insert(axis, 3 * s)
                cell32[n * 88 : n * 88 + 81, :] = jnp.dot(
                    faces[axis * 8 + s * 4 + n], corner_weights(weights, *spot), preferred_element_type=F32
                )
            for n in range(4):
                view = ref.at[pl.ds(pl.multiple_of(s * FACE + (n // 2) * 136 + (n % 2) * 8, 8), 152)]
                for row in range(9):
                    at = n * 88 + row * 9
                    view[row * SIDE : row * SIDE + 9, :] += cell32[at : at + 9, :]
            return carry

        lax.fori_loop(0, 2, face, 0, unroll=True)

    for axis in range(3):

        def edge(s, carry, axis=axis):
            terms = []
            for n in range(4):
                spot = [3 * s, 3 * (n // 2)]
                spot.insert(axis, n % 2 + 1)
                terms.append(
                    jnp.dot(edges[axis * 8 + s * 4 + n], corner_weights(weights, *spot), preferred_element_type=F32)
                )
            for n, term in enumerate(terms):
                t, u = n // 2, n % 2
                if axis == 2:
                    view = xs.at[pl.ds(pl.multiple_of(s * FACE + t * 272 + u * 8, 8), 16)]
                    view[0:9, :] += term
                else:
                    ref = xs if axis == 1 else ys
                    view = ref.at[pl.ds(pl.multiple_of(s * FACE + u * 136 + t * 16, 8), 152)]
                    view[pl.ds(0, 9, stride=SIDE), :] += term
            return carry

        lax.fori_loop(0, 2, edge, 0, unroll=True)

    def point(s, carry):
        terms = []
        for n in range(4):
            corner = corner_weights(weights, 3 * s, 3 * (n // 2), 3 * (n % 2))
            terms.append(jnp.dot(points[s * 4 + n], corner, preferred_element_type=F32))
        for n, term in enumerate(terms):
            view = xs.at[pl.ds(pl.multiple_of(s * FACE + (n // 2) * 272 + (n % 2) * 16, 8), 8)]
            view[0:1, :] += term
        return carry

    lax.fori_loop(0, 2, point, 0, unroll=True)

    for s in range(2):
        for y in range(SIDE):
            at = s * 16 * SLAB + y * ZPAD
            field[at : at + SIDE, :] += scale * xs[s * FACE + y * SIDE : s * FACE + (y + 1) * SIDE, :]
        for x in range(SIDE):
            at = s * 16 * ZPAD + x * SLAB
            field[at : at + SIDE, :] += scale * ys[s * FACE + x * SIDE : s * FACE + (x + 1) * SIDE, :]
        field[pl.ds(s * 16, PLANE, stride=ZPAD), :] += scale * zs[s * FACE : s * FACE + PLANE, :]

    if last:

        def slab(x, carry):
            for y in range(16):
                start = pl.multiple_of(x * SLAB + y * ZPAD, 8)
                out[x, y] = field[pl.ds(start, 16), :].astype(BF16)
            return carry

        lax.fori_loop(0, 16, slab, 0)
        for offset, part in enumerate(parts):
            quarter = (odd[3] + offset) % 4
            part[...] = out[pl.ds(quarter * 4, 4)].reshape(1024, LANES)
    else:

        def chunk(n, carry):
            spot = pl.ds(pl.multiple_of(n * CHUNK, 16), CHUNK)
            out[spot, :] = field[spot, :].astype(BF16)
            return carry

        lax.fori_loop(0, ROWS // CHUNK, chunk, 0)


def advance(odd, field, messages, w75, tables, first, last):
    args = [odd, field, *messages, w75, *tables]
    if last:
        outs = [shape((16, 16, 16, LANES), BF16)] + [shape((1024, LANES), BF16)] * 4
    else:
        outs = [shape((ROWS, LANES), BF16)]
    outs.append(shape((ROWS, LANES), F32))
    return pl.pallas_call(
        functools.partial(advance_kernel, first, last),
        out_shape=tuple(outs),
        in_specs=[SMEM] + [VMEM] * (len(args) - 1),
        out_specs=(VMEM,) * len(outs),
        input_output_aliases={1: len(outs) - 1},
        scratch_shapes=[pltpu.VMEM((1472, LANES), F32), pltpu.VMEM((2000, LANES), BF16)]
        + [pltpu.VMEM((2 * FACE, LANES), F32)] * 3,
        cost_estimate=cost(3e8, 1.2e7),
        compiler_params=LARGE,
        name="advance",
    )(*args)[:-1]


def gram_kernel(x0, x1, x2, x3, own, m1, m2, m3):
    blocks = [x0[...], x1[...], x2[...], x3[...]]
    for row, left in enumerate(blocks):
        turned = left.T
        for column, out in ((0, own), (3, m1), (2, m2), (1, m3)):
            part = jnp.dot(turned, blocks[column], preferred_element_type=F32)
            out[row * 128 : row * 128 + 128, :] = part.astype(out.dtype)


def gram(blocks):
    return pl.pallas_call(
        gram_kernel,
        out_shape=(shape((512, LANES), F32),) + (shape((512, LANES), BF16),) * 3,
        in_specs=[VMEM] * 4,
        out_specs=(VMEM,) * 4,
        cost_estimate=cost(6e8, 2e6),
        compiler_params=LARGE,
        name="gram",
    )(*blocks)


def collect_kernel(band, own, m1, m2, m3, out):
    for row in range(4):
        total = own[row * 128 : row * 128 + 128, :]
        for offset, ref in ((1, m1), (2, m2), (3, m3)):
            source = (row - offset) % 4
            total = total + ref[source * 128 : source * 128 + 128, :].astype(F32)
        place = (band[0] + 4 - row) % 4
        out[pl.ds(place * 16, 16)] = total.reshape(16, 8, LANES).astype(BF16)


def collect(band, own, received):
    return pl.pallas_call(
        collect_kernel,
        out_shape=shape((64, 8, LANES), BF16),
        in_specs=[SMEM] + [VMEM] * 4,
        out_specs=VMEM,
        cost_estimate=cost(1e6, 1e6),
        compiler_params=SMALL,
        name="collect",
    )(band, own, *received)


def total_kernel(scale, terms, out):
    out[...] = jnp.sum(terms[...].astype(F32), axis=0) * scale


def total(terms, scale):
    return pl.pallas_call(
        functools.partial(total_kernel, scale),
        out_shape=shape(terms.shape[1:], F32),
        in_specs=[VMEM],
        out_specs=VMEM,
        cost_estimate=cost(1e5, 2e5),
        compiler_params=SMALL,
        name="total",
    )(terms)


def local(psi, cell_ham, proj_table, coupling, atom_kind):
    devices = lax.axis_size("cells")
    side = cube_root(devices)
    offsets = (1, side, side * side)
    block = lax.axis_index("cells")
    band = lax.axis_index("bands")
    odd = jnp.stack([(block // offset) % 2 for offset in offsets] + [band]).astype(jnp.int32)

    def upward(x, axis):
        return shifted(x, "cells", offsets[axis])

    def downward(x, axis):
        return shifted(x, "cells", -offsets[axis])

    def swap(messages, axis):
        offset = offsets[axis]
        arrived = []
        for start, message in enumerate(messages):
            pairs = []
            for i in range(devices):
                forward = (i // offset) % 2 == start
                pairs.append((i, (i + offset) % devices if forward else (i - offset) % devices))
            arrived.append(lax.ppermute(message, "cells", pairs))
        return arrived

    message, up, own = first_x(psi, atom_kind)
    from_x, up_x = downward(message, 0), upward(up, 0)
    rows_y, rows_z = first_rows(psi)
    message, up, s20 = first_y(rows_y, from_x, up_x, own)
    from_y, up_y = downward(message, 1), upward(up, 1)
    upper, token = by_cell(cell_ham, 0, UPPER, s20)
    message, up, s50 = first_z(rows_z, from_x, from_y, up_y, s20, token)
    from_z, up_z = downward(message, 2), upward(up, 2)
    lower, _ = by_cell(cell_ham, UPPER, CELL - UPPER, s50)
    ham = (upper, lower)
    table = proj_table.reshape(4, 128, CELL)
    kinds, rows, mix = first_tables(from_z, up_z, s50, table, coupling)

    def step(now, before, last, tables):
        first = tables is None
        terms, one, two, zface, xface, weights = apply_cells(
            first, odd, now, ham if first else (tables[-1],), rows, mix
        )
        ys = swap((one, two), 1)
        if first:
            picked = pick(ham, weights)
            token = picked
            tables = (*make_tables(kinds, turn(table, weights), weights), picked)
        else:
            terms, token = local_part(ham, terms)
        field = assemble(terms, now, before)
        one, two, xface, weights = after_y(odd, *ys, zface, xface, weights, token)
        zs = swap((one, two), 2)
        one, two, weights = after_z(odd, *zs, xface, weights)
        xs = swap((one, two), 0)
        return tables, advance(odd, field, (*ys, *zs, *xs), weights, tables[:4], before is None, last)

    y0 = begin(psi, from_x, from_y, from_z)
    tables, (y1,) = step(y0, None, False, None)
    tables, (y2,) = step(y1, y0, False, tables)
    tables, (filtered, *blocks) = step(y2, y1, True, tables)

    two = shifted(blocks[2], "bands", 2)
    blocks = [blocks[0], shifted(blocks[1], "bands", 1), two, shifted(blocks[3], "bands", 3)]
    own, *messages = gram(blocks)
    messages = [shifted(message, "bands", n + 1) for n, message in enumerate(messages)]
    terms = collect(band.astype(jnp.int32).reshape(1), own, messages)
    terms = lax.all_to_all(terms, "cells", 0, 0)
    inverse_count = 1.0 / (4096 * devices)
    correlation = total(terms, inverse_count)
    return filtered, correlation


def solution(mesh):
    in_specs = (
        P("cells", None, None, "bands"),
        P("cells", None, None),
        P(),
        P(),
        P("cells", None, None),
    )
    out_specs = (P("cells", None, None, "bands"), P("cells", "bands"))
    return jax.shard_map(local, mesh=mesh, in_specs=in_specs, out_specs=out_specs, check_vma=False)
```
